512 devices in a mesh: sx: 32 (over z_hi, y, core), sy: 16 (over x, z_lo).
Axes of the slice: x: 4, y: 4, z: 16 (z_hi: 4, z_lo: 4; z = z_hi * 4 + z_lo), core: 2. Of those that a mesh axis runs over, the one named last changes fastest.
Arguments:
- forward_prop: bfloat16 [2, 2, 12, 12, 64, 4096], P(None, None, None, None, 'sx', 'sy'), may hold values from -0.08984375 to 0.08984375
- backward_prop: bfloat16 [2, 2, 12, 12, 64, 4096], P(None, None, None, None, 'sx', 'sy'), may hold values from -0.08984375 to 0.08984375
- gamma_table: int32 [16, 4, 2], replicated, may hold values from 0 to 3, as said below
- source_site: int32 [3], replicated, may hold values from 0 to 63
- momenta: int32 [32, 3], replicated, may hold values from -8 to 7
Outputs:
- corr: float32 [16, 2, 2, 64, 4096], P(None, None, None, 'sx', 'sy')
- listed: float32 [2, 16, 2, 32], replicated
The draws below stay inside these ranges and needn't reach their ends.
Inputs may be any that keep to these rules, and one draw needn't show every extreme that they name: For every insertion g, gamma_table[g, 0..3, 0] is a permutation of 0..3; gamma_table[g, s, 1] is the power of i of that entry.
All inputs are finite; a program needn't handle non-finite values.
Results may differ from the reference program's by a relative error of at most 0.0003.
Values sent between devices are 32-bit elements; how exact they have to be, the bound alone decides.
A program may use at most 64 MiB of HBM per device.

```python
import math
import jax
import jax.numpy as jnp
from jax import lax

L = 64
LZ = 64
G = 16
TW = 2
NMOM = 32


def draw_gamma_table(key, part):
    perm_key, phase_key = jax.random.split(jax.random.fold_in(key, 7))
    row_keys = jax.random.split(perm_key, G)
    columns = jax.vmap(lambda single: jax.random.permutation(single, 4))(row_keys)
    powers = jax.random.randint(phase_key, (G, 4), 0, 4)
    return jnp.stack([columns.astype(jnp.int32), powers.astype(jnp.int32)], -1)


def touch_ends(entries, key, smallest, largest):
    longest = entries.shape.index(max(entries.shape))
    spots = []
    for shift in (0, 1):
        where = [jax.random.randint(jax.random.fold_in(key, axis), (), 0, length) for axis, length in enumerate(entries.shape)]
        where[longest] = (where[longest] + shift) % entries.shape[longest]
        spots.append(tuple(where))
    return entries.at[spots[0]].set(smallest).at[spots[1]].set(largest)


def block_scale(rng, dims, shards, least, high):
    def one(position, parts):
        heights = jax.random.uniform(jax.random.fold_in(jax.random.fold_in(rng, 6), position), (parts,), jnp.float32, least / len(shards), high / len(shards))
        return jnp.repeat(jnp.exp(heights), dims[position] // parts).reshape((-1,) + (1,) * (len(dims) - position - 1))

    loudness = one(*shards[0])
    for cut in shards[1:]:
        loudness = loudness * one(*cut)
    return loudness


def scatter_about(rng, shape, width, limit, pieces=(), kind=jnp.bfloat16):
    drawn = width * jax.random.normal(rng, shape, jnp.float32)
    if pieces:
        drawn = drawn * block_scale(rng, shape, pieces, -0.22, 0.18)
    return jnp.clip(drawn, -limit, limit).astype(kind)


def setup_inputs(seed: int = 0) -> dict:
    arg_keys = jax.random.split(jax.random.key(seed), 6)
    forward_prop = scatter_about(arg_keys[0], (TW, 2, 12, 12, L, L * LZ), 0.015, 0.08984375, ((4, 32), (5, 16)))
    backward_prop = scatter_about(arg_keys[1], (TW, 2, 12, 12, L, L * LZ), 0.015, 0.08984375, ((4, 32), (5, 16)))
    gamma_table = draw_gamma_table(jax.random.fold_in(arg_keys[5], 71), 0)
    source_site = jax.random.randint(arg_keys[3], (3,), 0, LZ).astype(jnp.int32)
    momenta = touch_ends(jax.random.randint(arg_keys[4], (NMOM, 3), -8, 8), jax.random.fold_in(arg_keys[4], 1), -8, 7).astype(jnp.int32)
    return dict(forward_prop=forward_prop, backward_prop=backward_prop, gamma_table=gamma_table, source_site=source_site, momenta=momenta)


HIGHEST = lax.Precision.HIGHEST


def gamma_matrices(gamma_table):
    inserts = gamma_table.shape[0]
    columns = gamma_table[:, :, 0]
    powers = gamma_table[:, :, 1]
    spin_ids = jnp.arange(4, dtype=jnp.int32)
    matches = (columns[:, :, None] == spin_ids[None, None, :]).astype(jnp.float32)
    unit_re = (powers == 0).astype(jnp.float32) - (powers == 2).astype(jnp.float32)
    unit_im = (powers == 1).astype(jnp.float32) - (powers == 3).astype(jnp.float32)
    return (matches * unit_re[:, :, None]).reshape(inserts, 16), (matches * unit_im[:, :, None]).reshape(inserts, 16)


def reference(forward_prop, backward_prop, gamma_table, source_site, momenta):
    mat_re, mat_im = gamma_matrices(gamma_table)
    volume = L * L * LZ
    wave_xy = jnp.arange(L, dtype=jnp.int32)
    wave_z = jnp.arange(LZ, dtype=jnp.int32)
    index_xy = jnp.mod(wave_xy[:, None] * source_site[0] + wave_xy[None, :] * source_site[1], L)
    index_z = jnp.mod(wave_z * source_site[2], LZ)
    angles = (2.0 * math.pi / L) * index_xy.astype(jnp.float32)[:, :, None] + (2.0 * math.pi / LZ) * index_z.astype(jnp.float32)[None, None, :]
    rotate = jnp.cos(angles) + 1j * jnp.sin(angles)
    pattern = "scjn,ucjn->sun"

    def one_slice(which):
        forward = lax.dynamic_index_in_dim(forward_prop, which, 0, keepdims=False).astype(jnp.float32)
        backward = lax.dynamic_index_in_dim(backward_prop, which, 0, keepdims=False).astype(jnp.float32)
        forward = forward.reshape(2, 4, 3, 12, volume)
        backward = backward.reshape(2, 4, 3, 12, volume)
        pair_re = jnp.einsum(pattern, backward[0], forward[0], precision=HIGHEST) + jnp.einsum(pattern, backward[1], forward[1], precision=HIGHEST)
        pair_im = jnp.einsum(pattern, backward[0], forward[1], precision=HIGHEST) - jnp.einsum(pattern, backward[1], forward[0], precision=HIGHEST)
        pair_re = pair_re.reshape(16, volume)
        pair_im = pair_im.reshape(16, volume)
        field_re = jnp.dot(mat_re, pair_re, precision=HIGHEST) - jnp.dot(mat_im, pair_im, precision=HIGHEST)
        field_im = jnp.dot(mat_re, pair_im, precision=HIGHEST) + jnp.dot(mat_im, pair_re, precision=HIGHEST)
        field = (field_re + 1j * field_im).reshape(G, L, L, LZ)
        spectrum = jnp.fft.fftn(field, axes=(1, 2, 3)) * rotate[None]
        return spectrum.real.astype(jnp.float32), spectrum.imag.astype(jnp.float32)

    spec_re, spec_im = lax.map(one_slice, jnp.arange(TW, dtype=jnp.int32))
    corr = jnp.stack([spec_re, spec_im], 2).transpose(1, 0, 2, 4, 5, 3).reshape(G, TW, 2, L, LZ * L)
    mom_x = jnp.mod(momenta[:, 0], L)
    mom_y = jnp.mod(momenta[:, 1], L)
    mom_z = jnp.mod(momenta[:, 2], LZ)
    pick_re = spec_re[:, :, mom_x, mom_y, mom_z].transpose(1, 0, 2)
    pick_im = spec_im[:, :, mom_x, mom_y, mom_z].transpose(1, 0, 2)
    listed = jnp.stack([pick_re, pick_im], 0)
    return corr, listed
```

```python
import math

import jax
import jax.numpy as jnp
from jax import lax
from jax.sharding import PartitionSpec as P

L = 64
LZ = 64


HIGHEST = lax.Precision.HIGHEST


def gamma_matrices(gamma_table):
    inserts = gamma_table.shape[0]
    columns = gamma_table[:, :, 0]
    powers = gamma_table[:, :, 1]
    spin_ids = jnp.arange(4, dtype=jnp.int32)
    matches = (columns[:, :, None] == spin_ids[None, None, :]).astype(jnp.float32)
    unit_re = (powers == 0).astype(jnp.float32) - (powers == 2).astype(jnp.float32)
    unit_im = (powers == 1).astype(jnp.float32) - (powers == 3).astype(jnp.float32)
    return (
        (matches * unit_re[:, :, None]).reshape(inserts, 16),
        (matches * unit_im[:, :, None]).reshape(inserts, 16),
    )


def dft_table(length, anchor):
    wavenum = jnp.arange(length, dtype=jnp.int32)
    offsets = jnp.mod(wavenum - anchor, length)
    phase_index = jnp.mod(offsets[:, None] * wavenum[None, :], length)
    angles = 2.0 * math.pi / length * phase_index.astype(jnp.float32)
    return (jnp.cos(angles), -jnp.sin(angles))


def dft_matrix(length, anchor):
    table_re, table_im = dft_table(length, anchor)
    rows_re = jnp.stack([table_re, table_im], 1)
    rows_im = jnp.stack([-table_im, table_re], 1)
    return jnp.stack([rows_re, rows_im], 0)


def exchange(blocks, shared, axis):
    parts = blocks.shape[0]
    width = blocks.shape[1]
    extra = jnp.broadcast_to(shared.reshape(1, -1), (parts, shared.size))
    got = lax.all_to_all(jnp.concatenate([blocks, extra], 1), axis, 0, 0, tiled=True)
    return got[:, :width], got[:, width:].sum(0).reshape(shared.shape)


def apply_gammas(mat_re, mat_im, real_part, imag_part):
    extent = real_part.shape
    flat_re = real_part.reshape(extent[0], -1)
    flat_im = imag_part.reshape(extent[0], -1)
    out_re = jnp.dot(mat_re, flat_re, precision=HIGHEST) - jnp.dot(
        mat_im, flat_im, precision=HIGHEST
    )
    out_im = jnp.dot(mat_re, flat_im, precision=HIGHEST) + jnp.dot(
        mat_im, flat_re, precision=HIGHEST
    )
    return (out_re.reshape(extent), out_im.reshape(extent))


def project_sites(fields, source_site, momenta, rows_x, rows_y, length, depth):
    coord_x = lax.axis_index("sx") * rows_x + jnp.arange(rows_x, dtype=jnp.int32) - source_site[0]
    coord_y = lax.axis_index("sy") * rows_y + jnp.arange(rows_y, dtype=jnp.int32) - source_site[1]
    coord_z = jnp.arange(depth, dtype=jnp.int32) - source_site[2]
    part_x = jnp.mod(momenta[:, 0:1] * coord_x[None, :], length)
    part_y = jnp.mod(momenta[:, 1:2] * coord_y[None, :], length)
    part_z = jnp.mod(momenta[:, 2:3] * coord_z[None, :], depth)
    plane = jnp.mod(part_x[:, :, None] + part_y[:, None, :], length).astype(jnp.float32)
    angles = (
        2.0 * math.pi / length * plane[:, :, :, None]
        + 2.0 * math.pi / depth * part_z.astype(jnp.float32)[:, None, None, :]
    )
    angles = angles.reshape(momenta.shape[0], -1)
    cosine = jnp.cos(angles)
    sine = jnp.sin(angles)
    field_re = fields[:, 0].reshape(fields.shape[0], -1)
    field_im = fields[:, 1].reshape(fields.shape[0], -1)
    local_re = jnp.dot(field_re, cosine.T, precision=HIGHEST) + jnp.dot(
        field_im, sine.T, precision=HIGHEST
    )
    local_im = jnp.dot(field_im, cosine.T, precision=HIGHEST) - jnp.dot(
        field_re, sine.T, precision=HIGHEST
    )
    return (local_re, local_im)


def body(forward_prop, backward_prop, gamma_table, source_site, momenta):
    slices = forward_prop.shape[0]
    rows_x = forward_prop.shape[4]
    rows_y = backward_prop.shape[5] // LZ
    inserts = gamma_table.shape[0]
    forward = forward_prop.reshape(slices, 2, 4, 3, 12, -1)
    backward = backward_prop.reshape(slices, 2, 4, 3, 12, -1)
    pattern = "tscjn,tucjn->sutn"
    pair_re = jnp.einsum(
        pattern, backward[:, 0], forward[:, 0], preferred_element_type=jnp.float32
    ) + jnp.einsum(pattern, backward[:, 1], forward[:, 1], preferred_element_type=jnp.float32)
    pair_im = jnp.einsum(
        pattern, backward[:, 0], forward[:, 1], preferred_element_type=jnp.float32
    ) - jnp.einsum(pattern, backward[:, 1], forward[:, 0], preferred_element_type=jnp.float32)
    pair_re = pair_re.reshape(16, slices, -1)
    pair_im = pair_im.reshape(16, slices, -1)
    mat_re, mat_im = gamma_matrices(gamma_table)
    field_re, field_im = apply_gammas(mat_re, mat_im, pair_re, pair_im)
    fields = jnp.stack([field_re, field_im], 2).reshape(inserts * slices, 2, rows_x, rows_y, LZ)
    count = fields.shape[0]
    local_re, local_im = project_sites(fields, source_site, momenta, rows_x, rows_y, L, LZ)
    partial = jnp.stack([local_re, local_im], 0)
    groups_y = lax.axis_size("sy")
    groups_x = lax.axis_size("sx")
    along_z = jnp.einsum(
        "nrxyz,rzsk->nsxyk", fields, dft_matrix(LZ, source_site[2]), precision=HIGHEST
    )
    share_z = LZ // groups_y
    blocks = along_z.reshape(count, 2, rows_x, rows_y, groups_y, share_z)
    blocks = blocks.transpose(4, 0, 1, 2, 3, 5).reshape(groups_y, -1)
    blocks, partial = exchange(blocks, partial, "sy")
    blocks = blocks.reshape(groups_y, count, 2, rows_x, rows_y, share_z)
    table_y = dft_matrix(rows_y * groups_y, source_site[1]).reshape(2, groups_y, rows_y, 2, -1)
    along_y = jnp.einsum("jnrxyc,rjysk->nsxkc", blocks, table_y, precision=HIGHEST)
    share_y = along_y.shape[3] // groups_x
    blocks = along_y.reshape(count, 2, rows_x, groups_x, share_y, share_z)
    blocks = blocks.transpose(3, 0, 1, 2, 4, 5).reshape(groups_x, -1)
    blocks, partial = exchange(blocks, partial, "sx")
    blocks = blocks.reshape(groups_x, count, 2, rows_x, share_y, share_z)
    table_x = dft_matrix(rows_x * groups_x, source_site[0]).reshape(2, groups_x, rows_x, 2, -1)
    spectrum = jnp.einsum("inrxbc,rixsk->nsbck", blocks, table_x, precision=HIGHEST)
    corr = spectrum.reshape(inserts, slices, 2, share_y, -1)
    listed = partial.reshape(2, inserts, slices, -1)
    return (corr, listed)


def solution(mesh):
    placed = (
        P(None, None, None, None, "sx", "sy"),
        P(None, None, None, None, "sx", "sy"),
        P(),
        P(),
        P(),
    )
    return jax.shard_map(
        body,
        mesh=mesh,
        in_specs=placed,
        out_specs=(P(None, None, None, "sx", "sy"), P()),
        check_vma=False,
    )
```

```python
import math

import jax
import jax.numpy as jnp
from jax import lax
from jax.experimental import pallas as pl
from jax.experimental.pallas import tpu as pltpu
from jax.sharding import PartitionSpec as P

L = 64
LZ = 64


HIGHEST = lax.Precision.HIGHEST


def gamma_matrices(gamma_table):
    inserts = gamma_table.shape[0]
    columns = gamma_table[:, :, 0]
    powers = gamma_table[:, :, 1]
    spin_ids = jnp.arange(4, dtype=jnp.int32)
    matches = (columns[:, :, None] == spin_ids[None, None, :]).astype(jnp.float32)
    unit_re = (powers == 0).astype(jnp.float32) - (powers == 2).astype(jnp.float32)
    unit_im = (powers == 1).astype(jnp.float32) - (powers == 3).astype(jnp.float32)
    return (
        (matches * unit_re[:, :, None]).reshape(inserts, 16),
        (matches * unit_im[:, :, None]).reshape(inserts, 16),
    )


def dft_table(length, anchor):
    wavenum = jnp.arange(length, dtype=jnp.int32)
    offsets = jnp.mod(wavenum - anchor, length)
    phase_index = jnp.mod(offsets[:, None] * wavenum[None, :], length)
    angles = 2.0 * math.pi / length * phase_index.astype(jnp.float32)
    return (jnp.cos(angles), -jnp.sin(angles))


def dft_matrix(length, anchor):
    table_re, table_im = dft_table(length, anchor)
    rows_re = jnp.stack([table_re, table_im], 1)
    rows_im = jnp.stack([-table_im, table_re], 1)
    return jnp.stack([rows_re, rows_im], 0)


def exchange(blocks, shared, axis):
    parts = blocks.shape[0]
    width = blocks.shape[1]
    extra = jnp.broadcast_to(shared.reshape(1, -1), (parts, shared.size))
    got = lax.all_to_all(jnp.concatenate([blocks, extra], 1), axis, 0, 0, tiled=True)
    return got[:, :width], got[:, width:].sum(0).reshape(shared.shape)


def apply_gammas(mat_re, mat_im, real_part, imag_part):
    extent = real_part.shape
    flat_re = real_part.reshape(extent[0], -1)
    flat_im = imag_part.reshape(extent[0], -1)
    out_re = jnp.dot(mat_re, flat_re, precision=HIGHEST) - jnp.dot(
        mat_im, flat_im, precision=HIGHEST
    )
    out_im = jnp.dot(mat_re, flat_im, precision=HIGHEST) + jnp.dot(
        mat_im, flat_re, precision=HIGHEST
    )
    return (out_re.reshape(extent), out_im.reshape(extent))


def project_sites(fields, source_site, momenta, rows_x, rows_y, length, depth):
    coord_x = lax.axis_index("sx") * rows_x + jnp.arange(rows_x, dtype=jnp.int32) - source_site[0]
    coord_y = lax.axis_index("sy") * rows_y + jnp.arange(rows_y, dtype=jnp.int32) - source_site[1]
    coord_z = jnp.arange(depth, dtype=jnp.int32) - source_site[2]
    part_x = jnp.mod(momenta[:, 0:1] * coord_x[None, :], length)
    part_y = jnp.mod(momenta[:, 1:2] * coord_y[None, :], length)
    part_z = jnp.mod(momenta[:, 2:3] * coord_z[None, :], depth)
    plane = jnp.mod(part_x[:, :, None] + part_y[:, None, :], length).astype(jnp.float32)
    angles = (
        2.0 * math.pi / length * plane[:, :, :, None]
        + 2.0 * math.pi / depth * part_z.astype(jnp.float32)[:, None, None, :]
    )
    angles = angles.reshape(momenta.shape[0], -1)
    cosine = jnp.cos(angles)
    sine = jnp.sin(angles)
    field_re = fields[:, 0].reshape(fields.shape[0], -1)
    field_im = fields[:, 1].reshape(fields.shape[0], -1)
    local_re = jnp.dot(field_re, cosine.T, precision=HIGHEST) + jnp.dot(
        field_im, sine.T, precision=HIGHEST
    )
    local_im = jnp.dot(field_im, cosine.T, precision=HIGHEST) - jnp.dot(
        field_re, sine.T, precision=HIGHEST
    )
    return (local_re, local_im)


def contract_kernel(mix_ref, forward_ref, backward_ref, out_ref, pair_ref):
    slices = forward_ref.shape[0]
    rows = forward_ref.shape[3]
    for t in range(slices):
        for u in range(4):
            f_re = [forward_ref[t, 0, 3 * u + c].astype(jnp.float32) for c in range(3)]
            f_im = [forward_ref[t, 1, 3 * u + c].astype(jnp.float32) for c in range(3)]
            for s in range(4):
                acc_re = None
                acc_im = None
                for c in range(3):
                    b_re = backward_ref[t, 0, 3 * s + c].astype(jnp.float32)
                    b_im = backward_ref[t, 1, 3 * s + c].astype(jnp.float32)
                    term_re = b_re * f_re[c] + b_im * f_im[c]
                    term_im = b_re * f_im[c] - b_im * f_re[c]
                    acc_re = term_re if acc_re is None else acc_re + term_re
                    acc_im = term_im if acc_im is None else acc_im + term_im
                base = (s * 4 + u) * 2 * rows
                pair_ref[base : base + rows, :] = acc_re
                pair_ref[base + rows : base + 2 * rows, :] = acc_im
        out_ref[t] = jnp.dot(
            mix_ref[...], pair_ref[...], precision=HIGHEST, preferred_element_type=jnp.float32
        )


def contract(forward_prop, backward_prop, gamma_table):
    slices = forward_prop.shape[0]
    rows_x = forward_prop.shape[4]
    sites = forward_prop.shape[5]
    inserts = gamma_table.shape[0]
    forward = forward_prop.reshape(slices, 2, 12, 12 * rows_x, sites)
    backward = backward_prop.reshape(slices, 2, 12, 12 * rows_x, sites)
    mat_re, mat_im = gamma_matrices(gamma_table)
    mix = jnp.stack([jnp.stack([mat_re, -mat_im], 2), jnp.stack([mat_im, mat_re], 2)], 1)
    keep = jnp.eye(rows_x, dtype=jnp.float32)
    mix = jnp.einsum("gasr,xy->gaxsry", mix, keep)[:, :, :, :, :, None, :]
    mix = jnp.broadcast_to(
        mix, (inserts, 2, rows_x, 16, 2, 12, rows_x)
    ).reshape(inserts * 2 * rows_x, 16 * 2 * 12 * rows_x)
    out = pl.pallas_call(
        contract_kernel,
        out_shape=jax.ShapeDtypeStruct((slices, inserts * 2 * rows_x, sites), jnp.float32),
        in_specs=[pl.BlockSpec(memory_space=pltpu.VMEM)] * 3,
        out_specs=pl.BlockSpec(memory_space=pltpu.VMEM),
        scratch_shapes=[pltpu.VMEM((16 * 2 * 12 * rows_x, sites), jnp.float32)],
    )(mix, forward, backward)
    return out.reshape(slices, inserts, 2, rows_x, sites).transpose(1, 0, 2, 3, 4)


def body(forward_prop, backward_prop, gamma_table, source_site, momenta):
    slices = forward_prop.shape[0]
    rows_x = forward_prop.shape[4]
    rows_y = backward_prop.shape[5] // LZ
    inserts = gamma_table.shape[0]
    fields = contract(forward_prop, backward_prop, gamma_table)
    fields = fields.reshape(inserts * slices, 2, rows_x, rows_y, LZ)
    count = fields.shape[0]
    local_re, local_im = project_sites(fields, source_site, momenta, rows_x, rows_y, L, LZ)
    partial = jnp.stack([local_re, local_im], 0)
    groups_y = lax.axis_size("sy")
    groups_x = lax.axis_size("sx")
    along_z = jnp.einsum(
        "nrxyz,rzsk->nsxyk", fields, dft_matrix(LZ, source_site[2]), precision=HIGHEST
    )
    share_z = LZ // groups_y
    blocks = along_z.reshape(count, 2, rows_x, rows_y, groups_y, share_z)
    blocks = blocks.transpose(4, 0, 1, 2, 3, 5).reshape(groups_y, -1)
    blocks, partial = exchange(blocks, partial, "sy")
    blocks = blocks.reshape(groups_y, count, 2, rows_x, rows_y, share_z)
    table_y = dft_matrix(rows_y * groups_y, source_site[1]).reshape(2, groups_y, rows_y, 2, -1)
    along_y = jnp.einsum("jnrxyc,rjysk->nsxkc", blocks, table_y, precision=HIGHEST)
    share_y = along_y.shape[3] // groups_x
    blocks = along_y.reshape(count, 2, rows_x, groups_x, share_y, share_z)
    blocks = blocks.transpose(3, 0, 1, 2, 4, 5).reshape(groups_x, -1)
    blocks, partial = exchange(blocks, partial, "sx")
    blocks = blocks.reshape(groups_x, count, 2, rows_x, share_y, share_z)
    table_x = dft_matrix(rows_x * groups_x, source_site[0]).reshape(2, groups_x, rows_x, 2, -1)
    spectrum = jnp.einsum("inrxbc,rixsk->nsbck", blocks, table_x, precision=HIGHEST)
    corr = spectrum.reshape(inserts, slices, 2, share_y, -1)
    listed = partial.reshape(2, inserts, slices, -1)
    return (corr, listed)


def solution(mesh):
    placed = (
        P(None, None, None, None, "sx", "sy"),
        P(None, None, None, None, "sx", "sy"),
        P(),
        P(),
        P(),
    )
    return jax.shard_map(
        body,
        mesh=mesh,
        in_specs=placed,
        out_specs=(P(None, None, None, "sx", "sy"), P()),
        check_vma=False,
    )
```

```python
import math

import jax
import jax.numpy as jnp
from jax import lax
from jax.experimental import pallas as pl
from jax.experimental.pallas import tpu as pltpu
from jax.sharding import PartitionSpec as P

L = 64
LZ = 64


HIGHEST = lax.Precision.HIGHEST


def gamma_matrices(gamma_table):
    inserts = gamma_table.shape[0]
    columns = gamma_table[:, :, 0]
    powers = gamma_table[:, :, 1]
    spin_ids = jnp.arange(4, dtype=jnp.int32)
    matches = (columns[:, :, None] == spin_ids[None, None, :]).astype(jnp.float32)
    unit_re = (powers == 0).astype(jnp.float32) - (powers == 2).astype(jnp.float32)
    unit_im = (powers == 1).astype(jnp.float32) - (powers == 3).astype(jnp.float32)
    return (
        (matches * unit_re[:, :, None]).reshape(inserts, 16),
        (matches * unit_im[:, :, None]).reshape(inserts, 16),
    )


def dft_table(length, anchor):
    wavenum = jnp.arange(length, dtype=jnp.int32)
    offsets = jnp.mod(wavenum - anchor, length)
    phase_index = jnp.mod(offsets[:, None] * wavenum[None, :], length)
    angles = 2.0 * math.pi / length * phase_index.astype(jnp.float32)
    return (jnp.cos(angles), -jnp.sin(angles))


def dft_matrix(length, anchor):
    table_re, table_im = dft_table(length, anchor)
    rows_re = jnp.stack([table_re, table_im], 1)
    rows_im = jnp.stack([-table_im, table_re], 1)
    return jnp.stack([rows_re, rows_im], 0)


def exchange(blocks, shared, axis):
    parts = blocks.shape[0]
    width = blocks.shape[1]
    extra = jnp.broadcast_to(shared.reshape(1, -1), (parts, shared.size))
    got = lax.all_to_all(jnp.concatenate([blocks, extra], 1), axis, 0, 0, tiled=True)
    return got[:, :width], got[:, width:].sum(0).reshape(shared.shape)


def apply_gammas(mat_re, mat_im, real_part, imag_part):
    extent = real_part.shape
    flat_re = real_part.reshape(extent[0], -1)
    flat_im = imag_part.reshape(extent[0], -1)
    out_re = jnp.dot(mat_re, flat_re, precision=HIGHEST) - jnp.dot(
        mat_im, flat_im, precision=HIGHEST
    )
    out_im = jnp.dot(mat_re, flat_im, precision=HIGHEST) + jnp.dot(
        mat_im, flat_re, precision=HIGHEST
    )
    return (out_re.reshape(extent), out_im.reshape(extent))


def project_sites(fields, source_site, momenta, rows_x, rows_y, length, depth):
    coord_x = lax.axis_index("sx") * rows_x + jnp.arange(rows_x, dtype=jnp.int32) - source_site[0]
    coord_y = lax.axis_index("sy") * rows_y + jnp.arange(rows_y, dtype=jnp.int32) - source_site[1]
    coord_z = jnp.arange(depth, dtype=jnp.int32) - source_site[2]
    part_x = jnp.mod(momenta[:, 0:1] * coord_x[None, :], length)
    part_y = jnp.mod(momenta[:, 1:2] * coord_y[None, :], length)
    part_z = jnp.mod(momenta[:, 2:3] * coord_z[None, :], depth)
    plane = jnp.mod(part_x[:, :, None] + part_y[:, None, :], length).astype(jnp.float32)
    angles = (
        2.0 * math.pi / length * plane[:, :, :, None]
        + 2.0 * math.pi / depth * part_z.astype(jnp.float32)[:, None, None, :]
    )
    angles = angles.reshape(momenta.shape[0], -1)
    cosine = jnp.cos(angles)
    sine = jnp.sin(angles)
    field_re = fields[:, 0].reshape(fields.shape[0], -1)
    field_im = fields[:, 1].reshape(fields.shape[0], -1)
    local_re = jnp.dot(field_re, cosine.T, precision=HIGHEST) + jnp.dot(
        field_im, sine.T, precision=HIGHEST
    )
    local_im = jnp.dot(field_im, cosine.T, precision=HIGHEST) - jnp.dot(
        field_re, sine.T, precision=HIGHEST
    )
    return (local_re, local_im)


def contract_kernel(mix_ref, forward_ref, backward_ref, out_ref, pair_ref):
    slices = forward_ref.shape[0]
    rows = forward_ref.shape[3]
    for t in range(slices):
        for u in range(4):
            f_re = [forward_ref[t, 0, 3 * u + c].astype(jnp.float32) for c in range(3)]
            f_im = [forward_ref[t, 1, 3 * u + c].astype(jnp.float32) for c in range(3)]
            for s in range(4):
                acc_re = None
                acc_im = None
                for c in range(3):
                    b_re = backward_ref[t, 0, 3 * s + c].astype(jnp.float32)
                    b_im = backward_ref[t, 1, 3 * s + c].astype(jnp.float32)
                    term_re = b_re * f_re[c] + b_im * f_im[c]
                    term_im = b_re * f_im[c] - b_im * f_re[c]
                    acc_re = term_re if acc_re is None else acc_re + term_re
                    acc_im = term_im if acc_im is None else acc_im + term_im
                base = (s * 4 + u) * 2 * rows
                pair_ref[base : base + rows, :] = acc_re
                pair_ref[base + rows : base + 2 * rows, :] = acc_im
        width = pair_ref.shape[0]
        kinds = mix_ref.shape[1]
        lines = out_ref.shape[1] * kinds
        row = lax.broadcasted_iota(jnp.int32, (lines, width), 0)
        col = lax.broadcasted_iota(jnp.int32, (lines, width), 1)
        pick = jnp.logical_and(row % kinds == col // rows, row // kinds == col % out_ref.shape[1])
        summed = jnp.dot(
            pick.astype(jnp.float32), pair_ref[...], precision=HIGHEST,
            preferred_element_type=jnp.float32,
        )
        for x in range(out_ref.shape[1]):
            out_ref[t, x] = jnp.dot(
                mix_ref[...], summed[x * kinds : (x + 1) * kinds], precision=HIGHEST,
                preferred_element_type=jnp.float32,
            )


def contract(forward_prop, backward_prop, gamma_table):
    slices = forward_prop.shape[0]
    rows_x = forward_prop.shape[4]
    sites = forward_prop.shape[5]
    inserts = gamma_table.shape[0]
    forward = forward_prop.reshape(slices, 2, 12, 12 * rows_x, sites)
    backward = backward_prop.reshape(slices, 2, 12, 12 * rows_x, sites)
    mat_re, mat_im = gamma_matrices(gamma_table)
    mix = jnp.stack([jnp.stack([mat_re, -mat_im], 2), jnp.stack([mat_im, mat_re], 2)], 1)
    mix = mix.reshape(inserts * 2, 16 * 2)
    out = pl.pallas_call(
        contract_kernel,
        out_shape=jax.ShapeDtypeStruct((slices, rows_x, inserts * 2, sites), jnp.float32),
        in_specs=[pl.BlockSpec(memory_space=pltpu.VMEM)] * 3,
        out_specs=pl.BlockSpec(memory_space=pltpu.VMEM),
        scratch_shapes=[pltpu.VMEM((16 * 2 * 12 * rows_x, sites), jnp.float32)],
    )(mix, forward, backward)
    return out.reshape(slices, rows_x, inserts, 2, sites).transpose(2, 0, 3, 1, 4)


def body(forward_prop, backward_prop, gamma_table, source_site, momenta):
    slices = forward_prop.shape[0]
    rows_x = forward_prop.shape[4]
    rows_y = backward_prop.shape[5] // LZ
    inserts = gamma_table.shape[0]
    fields = contract(forward_prop, backward_prop, gamma_table)
    fields = fields.reshape(inserts * slices, 2, rows_x, rows_y, LZ)
    count = fields.shape[0]
    local_re, local_im = project_sites(fields, source_site, momenta, rows_x, rows_y, L, LZ)
    partial = jnp.stack([local_re, local_im], 0)
    groups_y = lax.axis_size("sy")
    groups_x = lax.axis_size("sx")
    along_z = jnp.einsum(
        "nrxyz,rzsk->nsxyk", fields, dft_matrix(LZ, source_site[2]), precision=HIGHEST
    )
    share_z = LZ // groups_y
    blocks = along_z.reshape(count, 2, rows_x, rows_y, groups_y, share_z)
    blocks = blocks.transpose(4, 0, 1, 2, 3, 5).reshape(groups_y, -1)
    blocks, partial = exchange(blocks, partial, "sy")
    blocks = blocks.reshape(groups_y, count, 2, rows_x, rows_y, share_z)
    table_y = dft_matrix(rows_y * groups_y, source_site[1]).reshape(2, groups_y, rows_y, 2, -1)
    along_y = jnp.einsum("jnrxyc,rjysk->nsxkc", blocks, table_y, precision=HIGHEST)
    share_y = along_y.shape[3] // groups_x
    blocks = along_y.reshape(count, 2, rows_x, groups_x, share_y, share_z)
    blocks = blocks.transpose(3, 0, 1, 2, 4, 5).reshape(groups_x, -1)
    blocks, partial = exchange(blocks, partial, "sx")
    blocks = blocks.reshape(groups_x, count, 2, rows_x, share_y, share_z)
    table_x = dft_matrix(rows_x * groups_x, source_site[0]).reshape(2, groups_x, rows_x, 2, -1)
    spectrum = jnp.einsum("inrxbc,rixsk->nsbck", blocks, table_x, precision=HIGHEST)
    corr = spectrum.reshape(inserts, slices, 2, share_y, -1)
    listed = partial.reshape(2, inserts, slices, -1)
    return (corr, listed)


def solution(mesh):
    placed = (
        P(None, None, None, None, "sx", "sy"),
        P(None, None, None, None, "sx", "sy"),
        P(),
        P(),
        P(),
    )
    return jax.shard_map(
        body,
        mesh=mesh,
        in_specs=placed,
        out_specs=(P(None, None, None, "sx", "sy"), P()),
        check_vma=False,
    )
```

```python
import functools
import math

import jax
import jax.numpy as jnp
from jax import lax
from jax.experimental import pallas as pl
from jax.experimental.pallas import tpu as pltpu
from jax.sharding import PartitionSpec as P

L = 64
LZ = 64


HIGHEST = lax.Precision.HIGHEST


def gamma_matrices(gamma_table):
    inserts = gamma_table.shape[0]
    columns = gamma_table[:, :, 0]
    powers = gamma_table[:, :, 1]
    spin_ids = jnp.arange(4, dtype=jnp.int32)
    matches = (columns[:, :, None] == spin_ids[None, None, :]).astype(jnp.float32)
    unit_re = (powers == 0).astype(jnp.float32) - (powers == 2).astype(jnp.float32)
    unit_im = (powers == 1).astype(jnp.float32) - (powers == 3).astype(jnp.float32)
    return (
        (matches * unit_re[:, :, None]).reshape(inserts, 16),
        (matches * unit_im[:, :, None]).reshape(inserts, 16),
    )


def dft_table(length, anchor):
    wavenum = jnp.arange(length, dtype=jnp.int32)
    offsets = jnp.mod(wavenum - anchor, length)
    phase_index = jnp.mod(offsets[:, None] * wavenum[None, :], length)
    angles = 2.0 * math.pi / length * phase_index.astype(jnp.float32)
    return (jnp.cos(angles), -jnp.sin(angles))


def dft_matrix(length, anchor):
    table_re, table_im = dft_table(length, anchor)
    rows_re = jnp.stack([table_re, table_im], 1)
    rows_im = jnp.stack([-table_im, table_re], 1)
    return jnp.stack([rows_re, rows_im], 0)


def swap_kernel(axis, blocks_ref, out_ref, send_sem, recv_sem):
    parts = blocks_ref.shape[0]
    me = lax.axis_index(axis)
    mesh_ids = pl.DeviceIdType.MESH
    barrier = pltpu.get_barrier_semaphore()
    for step in range(1, parts):
        pl.semaphore_signal(
            barrier, 1, device_id={axis: lax.rem(me + step, parts)}, device_id_type=mesh_ids
        )
    pl.semaphore_wait(barrier, parts - 1)

    def copy_to(step):
        peer = lax.rem(me + step, parts)
        return pltpu.make_async_remote_copy(
            src_ref=blocks_ref.at[peer],
            dst_ref=out_ref.at[me],
            send_sem=send_sem.at[step],
            recv_sem=recv_sem.at[step],
            device_id={axis: peer},
            device_id_type=mesh_ids,
        )

    def copy_from(step):
        source = lax.rem(me + parts - step, parts)
        return pltpu.make_async_remote_copy(
            src_ref=blocks_ref.at[source],
            dst_ref=out_ref.at[source],
            send_sem=send_sem.at[step],
            recv_sem=recv_sem.at[step],
            device_id={axis: source},
            device_id_type=mesh_ids,
        )

    @pl.loop(1, parts)
    def _(step):
        copy_to(step).start()

    out_ref[me] = blocks_ref[me]

    @pl.loop(1, parts)
    def _(step):
        copy_to(step).wait_send()

    @pl.loop(1, parts)
    def _(step):
        copy_from(step).wait_recv()


def swap(blocks, axis, ident):
    parts = blocks.shape[0]
    lanes = 128
    shaped = blocks.reshape(parts, -1, lanes)
    out = pl.pallas_call(
        functools.partial(swap_kernel, axis),
        out_shape=jax.ShapeDtypeStruct(shaped.shape, shaped.dtype),
        in_specs=[pl.BlockSpec(memory_space=pltpu.VMEM)],
        out_specs=pl.BlockSpec(memory_space=pltpu.VMEM),
        scratch_shapes=[pltpu.SemaphoreType.DMA((parts,)), pltpu.SemaphoreType.DMA((parts,))],
        compiler_params=pltpu.CompilerParams(collective_id=ident, has_side_effects=True),
    )(shaped)
    return out.reshape(blocks.shape)


def exchange(blocks, shared, axis, ident):
    parts = blocks.shape[0]
    width = blocks.shape[1]
    extra = jnp.broadcast_to(shared.reshape(1, -1), (parts, shared.size))
    got = swap(jnp.concatenate([blocks, extra], 1), axis, ident)
    return got[:, :width], got[:, width:].sum(0).reshape(shared.shape)


def apply_gammas(mat_re, mat_im, real_part, imag_part):
    extent = real_part.shape
    flat_re = real_part.reshape(extent[0], -1)
    flat_im = imag_part.reshape(extent[0], -1)
    out_re = jnp.dot(mat_re, flat_re, precision=HIGHEST) - jnp.dot(
        mat_im, flat_im, precision=HIGHEST
    )
    out_im = jnp.dot(mat_re, flat_im, precision=HIGHEST) + jnp.dot(
        mat_im, flat_re, precision=HIGHEST
    )
    return (out_re.reshape(extent), out_im.reshape(extent))


def project_sites(fields, source_site, momenta, rows_x, rows_y, length, depth):
    coord_x = lax.axis_index("sx") * rows_x + jnp.arange(rows_x, dtype=jnp.int32) - source_site[0]
    coord_y = lax.axis_index("sy") * rows_y + jnp.arange(rows_y, dtype=jnp.int32) - source_site[1]
    coord_z = jnp.arange(depth, dtype=jnp.int32) - source_site[2]
    part_x = jnp.mod(momenta[:, 0:1] * coord_x[None, :], length)
    part_y = jnp.mod(momenta[:, 1:2] * coord_y[None, :], length)
    part_z = jnp.mod(momenta[:, 2:3] * coord_z[None, :], depth)
    plane = jnp.mod(part_x[:, :, None] + part_y[:, None, :], length).astype(jnp.float32)
    angles = (
        2.0 * math.pi / length * plane[:, :, :, None]
        + 2.0 * math.pi / depth * part_z.astype(jnp.float32)[:, None, None, :]
    )
    angles = angles.reshape(momenta.shape[0], -1)
    cosine = jnp.cos(angles)
    sine = jnp.sin(angles)
    field_re = fields[:, 0].reshape(fields.shape[0], -1)
    field_im = fields[:, 1].reshape(fields.shape[0], -1)
    local_re = jnp.dot(field_re, cosine.T, precision=HIGHEST) + jnp.dot(
        field_im, sine.T, precision=HIGHEST
    )
    local_im = jnp.dot(field_im, cosine.T, precision=HIGHEST) - jnp.dot(
        field_re, sine.T, precision=HIGHEST
    )
    return (local_re, local_im)


def contract_kernel(mix_ref, forward_ref, backward_ref, out_ref, pair_ref):
    slices = forward_ref.shape[0]
    rows = forward_ref.shape[3]
    for t in range(slices):
        for u in range(4):
            f_re = [forward_ref[t, 0, 3 * u + c].astype(jnp.float32) for c in range(3)]
            f_im = [forward_ref[t, 1, 3 * u + c].astype(jnp.float32) for c in range(3)]
            for s in range(4):
                acc_re = None
                acc_im = None
                for c in range(3):
                    b_re = backward_ref[t, 0, 3 * s + c].astype(jnp.float32)
                    b_im = backward_ref[t, 1, 3 * s + c].astype(jnp.float32)
                    term_re = b_re * f_re[c] + b_im * f_im[c]
                    term_im = b_re * f_im[c] - b_im * f_re[c]
                    acc_re = term_re if acc_re is None else acc_re + term_re
                    acc_im = term_im if acc_im is None else acc_im + term_im
                base = (s * 4 + u) * 2 * rows
                pair_ref[base : base + rows, :] = acc_re
                pair_ref[base + rows : base + 2 * rows, :] = acc_im
        width = pair_ref.shape[0]
        kinds = mix_ref.shape[1]
        lines = out_ref.shape[1] * kinds
        row = lax.broadcasted_iota(jnp.int32, (lines, width), 0)
        col = lax.broadcasted_iota(jnp.int32, (lines, width), 1)
        pick = jnp.logical_and(row % kinds == col // rows, row // kinds == col % out_ref.shape[1])
        summed = jnp.dot(
            pick.astype(jnp.float32), pair_ref[...], precision=HIGHEST,
            preferred_element_type=jnp.float32,
        )
        for x in range(out_ref.shape[1]):
            out_ref[t, x] = jnp.dot(
                mix_ref[...], summed[x * kinds : (x + 1) * kinds], precision=HIGHEST,
                preferred_element_type=jnp.float32,
            )


def contract(forward_prop, backward_prop, gamma_table):
    slices = forward_prop.shape[0]
    rows_x = forward_prop.shape[4]
    sites = forward_prop.shape[5]
    inserts = gamma_table.shape[0]
    forward = forward_prop.reshape(slices, 2, 12, 12 * rows_x, sites)
    backward = backward_prop.reshape(slices, 2, 12, 12 * rows_x, sites)
    mat_re, mat_im = gamma_matrices(gamma_table)
    mix = jnp.stack([jnp.stack([mat_re, -mat_im], 2), jnp.stack([mat_im, mat_re], 2)], 1)
    mix = mix.reshape(inserts * 2, 16 * 2)
    out = pl.pallas_call(
        contract_kernel,
        out_shape=jax.ShapeDtypeStruct((slices, rows_x, inserts * 2, sites), jnp.float32),
        in_specs=[pl.BlockSpec(memory_space=pltpu.VMEM)] * 3,
        out_specs=pl.BlockSpec(memory_space=pltpu.VMEM),
        scratch_shapes=[pltpu.VMEM((16 * 2 * 12 * rows_x, sites), jnp.float32)],
    )(mix, forward, backward)
    return out.reshape(slices, rows_x, inserts, 2, sites).transpose(2, 0, 3, 1, 4)


def body(forward_prop, backward_prop, gamma_table, source_site, momenta):
    slices = forward_prop.shape[0]
    rows_x = forward_prop.shape[4]
    rows_y = backward_prop.shape[5] // LZ
    inserts = gamma_table.shape[0]
    fields = contract(forward_prop, backward_prop, gamma_table)
    fields = fields.reshape(inserts * slices, 2, rows_x, rows_y, LZ)
    count = fields.shape[0]
    local_re, local_im = project_sites(fields, source_site, momenta, rows_x, rows_y, L, LZ)
    partial = jnp.stack([local_re, local_im], 0)
    groups_y = lax.axis_size("sy")
    groups_x = lax.axis_size("sx")
    along_z = jnp.einsum(
        "nrxyz,rzsk->nsxyk", fields, dft_matrix(LZ, source_site[2]), precision=HIGHEST
    )
    share_z = LZ // groups_y
    blocks = along_z.reshape(count, 2, rows_x, rows_y, groups_y, share_z)
    blocks = blocks.transpose(4, 0, 1, 2, 3, 5).reshape(groups_y, -1)
    blocks, partial = exchange(blocks, partial, "sy", 0)
    blocks = blocks.reshape(groups_y, count, 2, rows_x, rows_y, share_z)
    table_y = dft_matrix(rows_y * groups_y, source_site[1]).reshape(2, groups_y, rows_y, 2, -1)
    along_y = jnp.einsum("jnrxyc,rjysk->nsxkc", blocks, table_y, precision=HIGHEST)
    share_y = along_y.shape[3] // groups_x
    blocks = along_y.reshape(count, 2, rows_x, groups_x, share_y, share_z)
    blocks = blocks.transpose(3, 0, 1, 2, 4, 5).reshape(groups_x, -1)
    blocks, partial = exchange(blocks, partial, "sx", 1)
    blocks = blocks.reshape(groups_x, count, 2, rows_x, share_y, share_z)
    table_x = dft_matrix(rows_x * groups_x, source_site[0]).reshape(2, groups_x, rows_x, 2, -1)
    spectrum = jnp.einsum("inrxbc,rixsk->nsbck", blocks, table_x, precision=HIGHEST)
    corr = spectrum.reshape(inserts, slices, 2, share_y, -1)
    listed = partial.reshape(2, inserts, slices, -1)
    return (corr, listed)


def solution(mesh):
    placed = (
        P(None, None, None, None, "sx", "sy"),
        P(None, None, None, None, "sx", "sy"),
        P(),
        P(),
        P(),
    )
    return jax.shard_map(
        body,
        mesh=mesh,
        in_specs=placed,
        out_specs=(P(None, None, None, "sx", "sy"), P()),
        check_vma=False,
    )
```

```python
import functools
import math

import jax
import jax.numpy as jnp
from jax import lax
from jax.experimental import pallas as pl
from jax.experimental.pallas import tpu as pltpu
from jax.sharding import PartitionSpec as P

L = 64
LZ = 64


HIGHEST = lax.Precision.HIGHEST


def gamma_matrices(gamma_table):
    inserts = gamma_table.shape[0]
    columns = gamma_table[:, :, 0]
    powers = gamma_table[:, :, 1]
    spin_ids = jnp.arange(4, dtype=jnp.int32)
    matches = (columns[:, :, None] == spin_ids[None, None, :]).astype(jnp.float32)
    unit_re = (powers == 0).astype(jnp.float32) - (powers == 2).astype(jnp.float32)
    unit_im = (powers == 1).astype(jnp.float32) - (powers == 3).astype(jnp.float32)
    return (
        (matches * unit_re[:, :, None]).reshape(inserts, 16),
        (matches * unit_im[:, :, None]).reshape(inserts, 16),
    )


def dft_table(length, anchor):
    wavenum = jnp.arange(length, dtype=jnp.int32)
    offsets = jnp.mod(wavenum - anchor, length)
    phase_index = jnp.mod(offsets[:, None] * wavenum[None, :], length)
    angles = 2.0 * math.pi / length * phase_index.astype(jnp.float32)
    return (jnp.cos(angles), -jnp.sin(angles))


def dft_matrix(length, anchor):
    table_re, table_im = dft_table(length, anchor)
    rows_re = jnp.stack([table_re, table_im], 1)
    rows_im = jnp.stack([-table_im, table_re], 1)
    return jnp.stack([rows_re, rows_im], 0)


def swap_kernel(axis, blocks_ref, out_ref, send_sem, recv_sem):
    parts = blocks_ref.shape[0]
    me = lax.axis_index(axis)
    mesh_ids = pl.DeviceIdType.MESH
    barrier = pltpu.get_barrier_semaphore()
    for step in range(1, parts):
        pl.semaphore_signal(
            barrier, 1, device_id={axis: lax.rem(me + step, parts)}, device_id_type=mesh_ids
        )
    pl.semaphore_wait(barrier, parts - 1)

    def copy_to(step):
        peer = lax.rem(me + step, parts)
        return pltpu.make_async_remote_copy(
            src_ref=blocks_ref.at[peer],
            dst_ref=out_ref.at[me],
            send_sem=send_sem.at[step],
            recv_sem=recv_sem.at[step],
            device_id={axis: peer},
            device_id_type=mesh_ids,
        )

    def copy_from(step):
        source = lax.rem(me + parts - step, parts)
        return pltpu.make_async_remote_copy(
            src_ref=blocks_ref.at[source],
            dst_ref=out_ref.at[source],
            send_sem=send_sem.at[step],
            recv_sem=recv_sem.at[step],
            device_id={axis: source},
            device_id_type=mesh_ids,
        )

    @pl.loop(1, parts)
    def _(step):
        copy_to(step).start()

    out_ref[me] = blocks_ref[me]

    @pl.loop(1, parts)
    def _(step):
        copy_to(step).wait_send()

    @pl.loop(1, parts)
    def _(step):
        copy_from(step).wait_recv()


def swap(blocks, axis, ident):
    parts = blocks.shape[0]
    lanes = 128
    shaped = blocks.reshape(parts, -1, lanes)
    out = pl.pallas_call(
        functools.partial(swap_kernel, axis),
        out_shape=jax.ShapeDtypeStruct(shaped.shape, shaped.dtype),
        in_specs=[pl.BlockSpec(memory_space=pltpu.VMEM)],
        out_specs=pl.BlockSpec(memory_space=pltpu.VMEM),
        scratch_shapes=[pltpu.SemaphoreType.DMA((parts,)), pltpu.SemaphoreType.DMA((parts,))],
        compiler_params=pltpu.CompilerParams(collective_id=ident, has_side_effects=True),
    )(shaped)
    return out.reshape(blocks.shape)


def exchange(blocks, extra, axis, ident):
    width = blocks.shape[1]
    got = swap(jnp.concatenate([blocks, extra], 1), axis, ident)
    return got[:, :width], got[:, width:].sum(0)


def apply_gammas(mat_re, mat_im, real_part, imag_part):
    extent = real_part.shape
    flat_re = real_part.reshape(extent[0], -1)
    flat_im = imag_part.reshape(extent[0], -1)
    out_re = jnp.dot(mat_re, flat_re, precision=HIGHEST) - jnp.dot(
        mat_im, flat_im, precision=HIGHEST
    )
    out_im = jnp.dot(mat_re, flat_im, precision=HIGHEST) + jnp.dot(
        mat_im, flat_re, precision=HIGHEST
    )
    return (out_re.reshape(extent), out_im.reshape(extent))


def project_sites(fields, source_site, momenta, rows_x, rows_y, length, depth):
    coord_x = lax.axis_index("sx") * rows_x + jnp.arange(rows_x, dtype=jnp.int32) - source_site[0]
    coord_y = lax.axis_index("sy") * rows_y + jnp.arange(rows_y, dtype=jnp.int32) - source_site[1]
    coord_z = jnp.arange(depth, dtype=jnp.int32) - source_site[2]
    part_x = jnp.mod(momenta[:, 0:1] * coord_x[None, :], length)
    part_y = jnp.mod(momenta[:, 1:2] * coord_y[None, :], length)
    part_z = jnp.mod(momenta[:, 2:3] * coord_z[None, :], depth)
    plane = jnp.mod(part_x[:, :, None] + part_y[:, None, :], length).astype(jnp.float32)
    angles = (
        2.0 * math.pi / length * plane[:, :, :, None]
        + 2.0 * math.pi / depth * part_z.astype(jnp.float32)[:, None, None, :]
    )
    angles = angles.reshape(momenta.shape[0], -1)
    cosine = jnp.cos(angles)
    sine = jnp.sin(angles)
    field_re = fields[:, 0].reshape(fields.shape[0], -1)
    field_im = fields[:, 1].reshape(fields.shape[0], -1)
    local_re = jnp.dot(field_re, cosine.T, precision=HIGHEST) + jnp.dot(
        field_im, sine.T, precision=HIGHEST
    )
    local_im = jnp.dot(field_im, cosine.T, precision=HIGHEST) - jnp.dot(
        field_re, sine.T, precision=HIGHEST
    )
    return (local_re, local_im)


def contract_kernel(mix_ref, forward_ref, backward_ref, out_ref, pair_ref):
    slices = forward_ref.shape[0]
    rows = forward_ref.shape[3]
    for t in range(slices):
        for u in range(4):
            f_re = [forward_ref[t, 0, 3 * u + c].astype(jnp.float32) for c in range(3)]
            f_im = [forward_ref[t, 1, 3 * u + c].astype(jnp.float32) for c in range(3)]
            for s in range(4):
                acc_re = None
                acc_im = None
                for c in range(3):
                    b_re = backward_ref[t, 0, 3 * s + c].astype(jnp.float32)
                    b_im = backward_ref[t, 1, 3 * s + c].astype(jnp.float32)
                    term_re = b_re * f_re[c] + b_im * f_im[c]
                    term_im = b_re * f_im[c] - b_im * f_re[c]
                    acc_re = term_re if acc_re is None else acc_re + term_re
                    acc_im = term_im if acc_im is None else acc_im + term_im
                base = (s * 4 + u) * 2 * rows
                pair_ref[base : base + rows, :] = acc_re
                pair_ref[base + rows : base + 2 * rows, :] = acc_im
        width = pair_ref.shape[0]
        kinds = mix_ref.shape[1]
        lines = out_ref.shape[1] * kinds
        row = lax.broadcasted_iota(jnp.int32, (lines, width), 0)
        col = lax.broadcasted_iota(jnp.int32, (lines, width), 1)
        pick = jnp.logical_and(row % kinds == col // rows, row // kinds == col % out_ref.shape[1])
        summed = jnp.dot(
            pick.astype(jnp.float32), pair_ref[...], precision=HIGHEST,
            preferred_element_type=jnp.float32,
        )
        for x in range(out_ref.shape[1]):
            out_ref[t, x] = jnp.dot(
                mix_ref[...], summed[x * kinds : (x + 1) * kinds], precision=HIGHEST,
                preferred_element_type=jnp.float32,
            )


def contract(forward_prop, backward_prop, gamma_table):
    slices = forward_prop.shape[0]
    rows_x = forward_prop.shape[4]
    sites = forward_prop.shape[5]
    inserts = gamma_table.shape[0]
    forward = forward_prop.reshape(slices, 2, 12, 12 * rows_x, sites)
    backward = backward_prop.reshape(slices, 2, 12, 12 * rows_x, sites)
    mat_re, mat_im = gamma_matrices(gamma_table)
    mix = jnp.stack([jnp.stack([mat_re, -mat_im], 2), jnp.stack([mat_im, mat_re], 2)], 1)
    mix = mix.reshape(inserts * 2, 16 * 2)
    out = pl.pallas_call(
        contract_kernel,
        out_shape=jax.ShapeDtypeStruct((slices, rows_x, inserts * 2, sites), jnp.float32),
        in_specs=[pl.BlockSpec(memory_space=pltpu.VMEM)] * 3,
        out_specs=pl.BlockSpec(memory_space=pltpu.VMEM),
        scratch_shapes=[pltpu.VMEM((16 * 2 * 12 * rows_x, sites), jnp.float32)],
    )(mix, forward, backward)
    return out.reshape(slices, rows_x, inserts, 2, sites).transpose(2, 0, 3, 1, 4)


def body(forward_prop, backward_prop, gamma_table, source_site, momenta):
    slices = forward_prop.shape[0]
    rows_x = forward_prop.shape[4]
    rows_y = backward_prop.shape[5] // LZ
    inserts = gamma_table.shape[0]
    fields = contract(forward_prop, backward_prop, gamma_table)
    fields = fields.reshape(inserts * slices, 2, rows_x, rows_y, LZ)
    count = fields.shape[0]
    local_re, local_im = project_sites(fields, source_site, momenta, rows_x, rows_y, L, LZ)
    partial = jnp.stack([local_re, local_im], 0)
    groups_y = lax.axis_size("sy")
    groups_x = lax.axis_size("sx")
    along_z = jnp.einsum(
        "nrxyz,rzsk->nsxyk", fields, dft_matrix(LZ, source_site[2]), precision=HIGHEST
    )
    share_z = LZ // groups_y
    blocks = along_z.reshape(count, 2, rows_x, rows_y, groups_y, share_z)
    blocks = blocks.transpose(4, 0, 1, 2, 3, 5).reshape(groups_y, -1)
    shares = partial.reshape(groups_y, -1)
    blocks, share = exchange(blocks, shares, "sy", 0)
    blocks = blocks.reshape(groups_y, count, 2, rows_x, rows_y, share_z)
    table_y = dft_matrix(rows_y * groups_y, source_site[1]).reshape(2, groups_y, rows_y, 2, -1)
    along_y = jnp.einsum("jnrxyc,rjysk->nsxkc", blocks, table_y, precision=HIGHEST)
    share_y = along_y.shape[3] // groups_x
    blocks = along_y.reshape(count, 2, rows_x, groups_x, share_y, share_z)
    blocks = blocks.transpose(3, 0, 1, 2, 4, 5).reshape(groups_x, -1)
    spread = jnp.broadcast_to(share[None], (groups_x, share.size))
    blocks, share = exchange(blocks, spread, "sx", 1)
    blocks = blocks.reshape(groups_x, count, 2, rows_x, share_y, share_z)
    table_x = dft_matrix(rows_x * groups_x, source_site[0]).reshape(2, groups_x, rows_x, 2, -1)
    spectrum = jnp.einsum("inrxbc,rixsk->nsbck", blocks, table_x, precision=HIGHEST)
    corr = spectrum.reshape(inserts, slices, 2, share_y, -1)
    spread = jnp.broadcast_to(share[None], (groups_y, share.size))
    listed = swap(spread, "sy", 2).reshape(2, inserts, slices, -1)
    return (corr, listed)


def solution(mesh):
    placed = (
        P(None, None, None, None, "sx", "sy"),
        P(None, None, None, None, "sx", "sy"),
        P(),
        P(),
        P(),
    )
    return jax.shard_map(
        body,
        mesh=mesh,
        in_specs=placed,
        out_specs=(P(None, None, None, "sx", "sy"), P()),
        check_vma=False,
    )
```

```python
import functools
import math

import jax
import jax.numpy as jnp
from jax import lax
from jax.experimental import pallas as pl
from jax.experimental.pallas import tpu as pltpu
from jax.sharding import PartitionSpec as P

L = 64
LZ = 64


HIGHEST = lax.Precision.HIGHEST


def gamma_matrices(gamma_table):
    inserts = gamma_table.shape[0]
    columns = gamma_table[:, :, 0]
    powers = gamma_table[:, :, 1]
    spin_ids = jnp.arange(4, dtype=jnp.int32)
    matches = (columns[:, :, None] == spin_ids[None, None, :]).astype(jnp.float32)
    unit_re = (powers == 0).astype(jnp.float32) - (powers == 2).astype(jnp.float32)
    unit_im = (powers == 1).astype(jnp.float32) - (powers == 3).astype(jnp.float32)
    return (
        (matches * unit_re[:, :, None]).reshape(inserts, 16),
        (matches * unit_im[:, :, None]).reshape(inserts, 16),
    )


def dft_table(length, anchor):
    wavenum = jnp.arange(length, dtype=jnp.int32)
    offsets = jnp.mod(wavenum - anchor, length)
    phase_index = jnp.mod(offsets[:, None] * wavenum[None, :], length)
    angles = 2.0 * math.pi / length * phase_index.astype(jnp.float32)
    return (jnp.cos(angles), -jnp.sin(angles))


def dft_matrix(length, anchor):
    table_re, table_im = dft_table(length, anchor)
    rows_re = jnp.stack([table_re, table_im], 1)
    rows_im = jnp.stack([-table_im, table_re], 1)
    return jnp.stack([rows_re, rows_im], 0)


def swap_kernel(axis, blocks_ref, out_ref, send_sem, recv_sem):
    parts = blocks_ref.shape[0]
    me = lax.axis_index(axis)
    mesh_ids = pl.DeviceIdType.MESH
    barrier = pltpu.get_barrier_semaphore()
    for step in range(1, parts):
        pl.semaphore_signal(
            barrier, 1, device_id={axis: lax.rem(me + step, parts)}, device_id_type=mesh_ids
        )
    pl.semaphore_wait(barrier, parts - 1)

    def copy_to(step):
        peer = lax.rem(me + step, parts)
        return pltpu.make_async_remote_copy(
            src_ref=blocks_ref.at[peer],
            dst_ref=out_ref.at[me],
            send_sem=send_sem.at[step],
            recv_sem=recv_sem.at[step],
            device_id={axis: peer},
            device_id_type=mesh_ids,
        )

    def copy_from(step):
        source = lax.rem(me + parts - step, parts)
        return pltpu.make_async_remote_copy(
            src_ref=blocks_ref.at[source],
            dst_ref=out_ref.at[source],
            send_sem=send_sem.at[step],
            recv_sem=recv_sem.at[step],
            device_id={axis: source},
            device_id_type=mesh_ids,
        )

    @pl.loop(1, parts)
    def _(step):
        copy_to(step).start()

    out_ref[me] = blocks_ref[me]

    @pl.loop(1, parts)
    def _(step):
        copy_to(step).wait_send()

    @pl.loop(1, parts)
    def _(step):
        copy_from(step).wait_recv()


def swap(blocks, axis, ident):
    parts = blocks.shape[0]
    lanes = 128
    shaped = blocks.reshape(parts, -1, lanes)
    out = pl.pallas_call(
        functools.partial(swap_kernel, axis),
        out_shape=jax.ShapeDtypeStruct(shaped.shape, shaped.dtype),
        in_specs=[pl.BlockSpec(memory_space=pltpu.VMEM)],
        out_specs=pl.BlockSpec(memory_space=pltpu.VMEM),
        scratch_shapes=[pltpu.SemaphoreType.DMA((parts,)), pltpu.SemaphoreType.DMA((parts,))],
        compiler_params=pltpu.CompilerParams(collective_id=ident, has_side_effects=True),
    )(shaped)
    return out.reshape(blocks.shape)


def exchange(blocks, extra, axis, ident):
    width = blocks.shape[1]
    got = swap(jnp.concatenate([blocks, extra], 1), axis, ident)
    return got[:, :width], got[:, width:].sum(0)


def apply_gammas(mat_re, mat_im, real_part, imag_part):
    extent = real_part.shape
    flat_re = real_part.reshape(extent[0], -1)
    flat_im = imag_part.reshape(extent[0], -1)
    out_re = jnp.dot(mat_re, flat_re, precision=HIGHEST) - jnp.dot(
        mat_im, flat_im, precision=HIGHEST
    )
    out_im = jnp.dot(mat_re, flat_im, precision=HIGHEST) + jnp.dot(
        mat_im, flat_re, precision=HIGHEST
    )
    return (out_re.reshape(extent), out_im.reshape(extent))


def project_sites(fields, source_site, momenta, rows_x, rows_y, length, depth):
    coord_x = lax.axis_index("sx") * rows_x + jnp.arange(rows_x, dtype=jnp.int32) - source_site[0]
    coord_y = lax.axis_index("sy") * rows_y + jnp.arange(rows_y, dtype=jnp.int32) - source_site[1]
    coord_z = jnp.arange(depth, dtype=jnp.int32) - source_site[2]
    part_x = jnp.mod(momenta[:, 0:1] * coord_x[None, :], length)
    part_y = jnp.mod(momenta[:, 1:2] * coord_y[None, :], length)
    part_z = jnp.mod(momenta[:, 2:3] * coord_z[None, :], depth)
    plane = jnp.mod(part_x[:, :, None] + part_y[:, None, :], length).astype(jnp.float32)
    angles = (
        2.0 * math.pi / length * plane[:, :, :, None]
        + 2.0 * math.pi / depth * part_z.astype(jnp.float32)[:, None, None, :]
    )
    angles = angles.reshape(momenta.shape[0], -1)
    cosine = jnp.cos(angles)
    sine = jnp.sin(angles)
    field_re = fields[:, 0].reshape(fields.shape[0], -1)
    field_im = fields[:, 1].reshape(fields.shape[0], -1)
    local_re = jnp.dot(field_re, cosine.T, precision=HIGHEST) + jnp.dot(
        field_im, sine.T, precision=HIGHEST
    )
    local_im = jnp.dot(field_im, cosine.T, precision=HIGHEST) - jnp.dot(
        field_re, sine.T, precision=HIGHEST
    )
    return (local_re, local_im)


def contract_kernel(mix_ref, forward_ref, backward_ref, out_ref, pair_ref):
    slices = forward_ref.shape[0]
    rows = forward_ref.shape[3]
    for t in range(slices):
        for u in range(4):
            f_re = [forward_ref[t, 0, 3 * u + c].astype(jnp.float32) for c in range(3)]
            f_im = [forward_ref[t, 1, 3 * u + c].astype(jnp.float32) for c in range(3)]
            for s in range(4):
                acc_re = None
                acc_im = None
                for c in range(3):
                    b_re = backward_ref[t, 0, 3 * s + c].astype(jnp.float32)
                    b_im = backward_ref[t, 1, 3 * s + c].astype(jnp.float32)
                    term_re = b_re * f_re[c] + b_im * f_im[c]
                    term_im = b_re * f_im[c] - b_im * f_re[c]
                    acc_re = term_re if acc_re is None else acc_re + term_re
                    acc_im = term_im if acc_im is None else acc_im + term_im
                base = (s * 4 + u) * 2 * rows
                pair_ref[base : base + rows, :] = acc_re
                pair_ref[base + rows : base + 2 * rows, :] = acc_im
        width = pair_ref.shape[0]
        kinds = mix_ref.shape[1]
        lines = out_ref.shape[1] * kinds
        row = lax.broadcasted_iota(jnp.int32, (lines, width), 0)
        col = lax.broadcasted_iota(jnp.int32, (lines, width), 1)
        pick = jnp.logical_and(row % kinds == col // rows, row // kinds == col % out_ref.shape[1])
        summed = jnp.dot(
            pick.astype(jnp.float32), pair_ref[...], precision=HIGHEST,
            preferred_element_type=jnp.float32,
        )
        for x in range(out_ref.shape[1]):
            out_ref[t, x] = jnp.dot(
                mix_ref[...], summed[x * kinds : (x + 1) * kinds], precision=HIGHEST,
                preferred_element_type=jnp.float32,
            )


def contract(forward_prop, backward_prop, gamma_table):
    slices = forward_prop.shape[0]
    rows_x = forward_prop.shape[4]
    sites = forward_prop.shape[5]
    inserts = gamma_table.shape[0]
    forward = forward_prop.reshape(slices, 2, 12, 12 * rows_x, sites)
    backward = backward_prop.reshape(slices, 2, 12, 12 * rows_x, sites)
    mat_re, mat_im = gamma_matrices(gamma_table)
    mix = jnp.stack([jnp.stack([mat_re, -mat_im], 2), jnp.stack([mat_im, mat_re], 2)], 1)
    mix = mix.reshape(inserts * 2, 16 * 2)
    out = pl.pallas_call(
        contract_kernel,
        out_shape=jax.ShapeDtypeStruct((slices, rows_x, inserts * 2, sites), jnp.float32),
        in_specs=[pl.BlockSpec(memory_space=pltpu.VMEM)] * 3,
        out_specs=pl.BlockSpec(memory_space=pltpu.VMEM),
        scratch_shapes=[pltpu.VMEM((16 * 2 * 12 * rows_x, sites), jnp.float32)],
    )(mix, forward, backward)
    return out.reshape(slices, rows_x, inserts, 2, sites).transpose(2, 0, 3, 1, 4)


def spectral_kernel(
    sent_ref, table_ref, slab_ref, gathered_ref,
    landed_ref, turned_ref, share_ref, shares_ref, total_ref,
    a_send, a_recv, b_send, b_recv, s_send, s_recv, c_send, c_recv,
):
    parts_y = sent_ref.shape[0]
    parts_x = slab_ref.shape[0]
    depth = sent_ref.shape[1] - 1
    band = slab_ref.shape[1]
    me_y = lax.axis_index("sy")
    me_x = lax.axis_index("sx")
    mesh_ids = pl.DeviceIdType.MESH
    barrier = pltpu.get_barrier_semaphore()
    for step in range(1, parts_y):
        pl.semaphore_signal(
            barrier, 1, device_id={"sy": lax.rem(me_y + step, parts_y)}, device_id_type=mesh_ids
        )
    for step in range(1, parts_x):
        pl.semaphore_signal(
            barrier, 1, device_id={"sx": lax.rem(me_x + step, parts_x)}, device_id_type=mesh_ids
        )
    pl.semaphore_wait(barrier, parts_y + parts_x - 2)

    def send_y(step, src, dst, send_sem, recv_sem):
        peer = lax.rem(me_y + step, parts_y)
        return pltpu.make_async_remote_copy(
            src_ref=src(peer), dst_ref=dst(me_y), send_sem=send_sem.at[step],
            recv_sem=recv_sem.at[step], device_id={"sy": peer}, device_id_type=mesh_ids,
        )

    def recv_y(step, src, dst, send_sem, recv_sem):
        source = lax.rem(me_y + parts_y - step, parts_y)
        return pltpu.make_async_remote_copy(
            src_ref=src(source), dst_ref=dst(source), send_sem=send_sem.at[step],
            recv_sem=recv_sem.at[step], device_id={"sy": source}, device_id_type=mesh_ids,
        )

    def send_x(step, src, dst, send_sem, recv_sem):
        peer = lax.rem(me_x + step, parts_x)
        return pltpu.make_async_remote_copy(
            src_ref=src(peer), dst_ref=dst(me_x), send_sem=send_sem.at[step],
            recv_sem=recv_sem.at[step], device_id={"sx": peer}, device_id_type=mesh_ids,
        )

    def recv_x(step, src, dst, send_sem, recv_sem):
        source = lax.rem(me_x + parts_x - step, parts_x)
        return pltpu.make_async_remote_copy(
            src_ref=src(source), dst_ref=dst(source), send_sem=send_sem.at[step],
            recv_sem=recv_sem.at[step], device_id={"sx": source}, device_id_type=mesh_ids,
        )

    def run(parts, send, recv, src, dst, send_sem, recv_sem):
        @pl.loop(1, parts)
        def _(step):
            send(step, src, dst, send_sem, recv_sem).start()

        @pl.loop(1, parts)
        def _(step):
            send(step, src, dst, send_sem, recv_sem).wait_send()

        @pl.loop(1, parts)
        def _(step):
            recv(step, src, dst, send_sem, recv_sem).wait_recv()

    run(parts_y, send_y, recv_y, lambda i: sent_ref.at[i], lambda i: landed_ref.at[i], a_send, a_recv)
    landed_ref[me_y] = sent_ref[me_y]

    block = landed_ref[:, 0:depth, :].reshape(parts_y * depth, -1)
    turned = jnp.dot(table_ref[...], block, precision=HIGHEST, preferred_element_type=jnp.float32)
    for peer in range(parts_x):
        turned_ref[peer] = turned[peer * band : (peer + 1) * band]
    share = landed_ref[0, depth : depth + 1, :]
    for source in range(1, parts_y):
        share = share + landed_ref[source, depth : depth + 1, :]
    share_ref[...] = share

    run(parts_x, send_x, recv_x, lambda i: turned_ref.at[i], lambda i: slab_ref.at[i], b_send, b_recv)
    run(parts_x, send_x, recv_x, lambda i: share_ref, lambda i: shares_ref.at[i], s_send, s_recv)
    slab_ref[me_x] = turned_ref[me_x]
    shares_ref[me_x] = share_ref[...]

    total = shares_ref[0]
    for source in range(1, parts_x):
        total = total + shares_ref[source]
    total_ref[...] = total

    run(parts_y, send_y, recv_y, lambda i: total_ref, lambda i: gathered_ref.at[i], c_send, c_recv)
    gathered_ref[me_y] = total_ref[...]


def spectral(sent, table, parts_x, band):
    parts_y, rows, width = sent.shape
    depth = rows - 1
    vmem = pl.BlockSpec(memory_space=pltpu.VMEM)
    return pl.pallas_call(
        spectral_kernel,
        out_shape=(
            jax.ShapeDtypeStruct((parts_x, band, width), jnp.float32),
            jax.ShapeDtypeStruct((parts_y, 1, width), jnp.float32),
        ),
        in_specs=[vmem, vmem],
        out_specs=(vmem, vmem),
        scratch_shapes=[
            pltpu.VMEM((parts_y, rows, width), jnp.float32),
            pltpu.VMEM((parts_x, band, width), jnp.float32),
            pltpu.VMEM((1, width), jnp.float32),
            pltpu.VMEM((parts_x, 1, width), jnp.float32),
            pltpu.VMEM((1, width), jnp.float32),
        ]
        + [pltpu.SemaphoreType.DMA((parts_y,))] * 2
        + [pltpu.SemaphoreType.DMA((parts_x,))] * 4
        + [pltpu.SemaphoreType.DMA((parts_y,))] * 2,
        compiler_params=pltpu.CompilerParams(collective_id=0, has_side_effects=True),
    )(sent, table)


def body(forward_prop, backward_prop, gamma_table, source_site, momenta):
    slices = forward_prop.shape[0]
    rows_x = forward_prop.shape[4]
    rows_y = backward_prop.shape[5] // LZ
    inserts = gamma_table.shape[0]
    fields = contract(forward_prop, backward_prop, gamma_table)
    fields = fields.reshape(inserts * slices, 2, rows_x, rows_y, LZ)
    count = fields.shape[0]
    local_re, local_im = project_sites(fields, source_site, momenta, rows_x, rows_y, L, LZ)
    partial = jnp.stack([local_re, local_im], 0)
    groups_y = lax.axis_size("sy")
    groups_x = lax.axis_size("sx")
    share_z = LZ // groups_y
    length_y = rows_y * groups_y
    share_y = length_y // groups_x
    table_z = dft_matrix(LZ, source_site[2]).reshape(2, LZ, 2, groups_y, share_z)
    sent = jnp.einsum("nrxyz,rzsjc->jsynxc", fields, table_z, precision=HIGHEST)
    sent = sent.reshape(groups_y, 2 * rows_y, -1)
    width = sent.shape[2]
    shares = partial.reshape(groups_y, 1, -1)
    shares = jnp.pad(shares, ((0, 0), (0, 0), (0, width - shares.shape[2])))
    sent = jnp.concatenate([sent, shares], 1)
    table_y = dft_matrix(length_y, source_site[1]).reshape(2, groups_y, rows_y, 2, groups_x, share_y)
    table_y = table_y.transpose(4, 5, 3, 1, 0, 2).reshape(2 * length_y, 2 * length_y)
    slab, gathered = spectral(sent, table_y, groups_x, 2 * share_y)
    slab = slab.reshape(groups_x, share_y, 2, count, rows_x, share_z)
    table_x = dft_matrix(rows_x * groups_x, source_site[0]).reshape(2, groups_x, rows_x, 2, -1)
    spectrum = jnp.einsum("ibsnxc,sixtk->ntbck", slab, table_x, precision=HIGHEST)
    corr = spectrum.reshape(inserts, slices, 2, share_y, -1)
    listed = gathered[:, 0, : partial.size // groups_y].reshape(2, inserts, slices, -1)
    return (corr, listed)


def solution(mesh):
    placed = (
        P(None, None, None, None, "sx", "sy"),
        P(None, None, None, None, "sx", "sy"),
        P(),
        P(),
        P(),
    )
    return jax.shard_map(
        body,
        mesh=mesh,
        in_specs=placed,
        out_specs=(P(None, None, None, "sx", "sy"), P()),
        check_vma=False,
    )
```

```python
import functools
import math

import jax
import jax.numpy as jnp
from jax import lax
from jax.experimental import pallas as pl
from jax.experimental.pallas import tpu as pltpu
from jax.sharding import PartitionSpec as P

L = 64
LZ = 64


HIGHEST = lax.Precision.HIGHEST


def gamma_matrices(gamma_table):
    inserts = gamma_table.shape[0]
    columns = gamma_table[:, :, 0]
    powers = gamma_table[:, :, 1]
    spin_ids = jnp.arange(4, dtype=jnp.int32)
    matches = (columns[:, :, None] == spin_ids[None, None, :]).astype(jnp.float32)
    unit_re = (powers == 0).astype(jnp.float32) - (powers == 2).astype(jnp.float32)
    unit_im = (powers == 1).astype(jnp.float32) - (powers == 3).astype(jnp.float32)
    return (
        (matches * unit_re[:, :, None]).reshape(inserts, 16),
        (matches * unit_im[:, :, None]).reshape(inserts, 16),
    )


def dft_table(length, anchor):
    wavenum = jnp.arange(length, dtype=jnp.int32)
    offsets = jnp.mod(wavenum - anchor, length)
    phase_index = jnp.mod(offsets[:, None] * wavenum[None, :], length)
    angles = 2.0 * math.pi / length * phase_index.astype(jnp.float32)
    return (jnp.cos(angles), -jnp.sin(angles))


def dft_matrix(length, anchor):
    table_re, table_im = dft_table(length, anchor)
    rows_re = jnp.stack([table_re, table_im], 1)
    rows_im = jnp.stack([-table_im, table_re], 1)
    return jnp.stack([rows_re, rows_im], 0)


def swap_kernel(axis, blocks_ref, out_ref, send_sem, recv_sem):
    parts = blocks_ref.shape[0]
    me = lax.axis_index(axis)
    mesh_ids = pl.DeviceIdType.MESH
    barrier = pltpu.get_barrier_semaphore()
    for step in range(1, parts):
        pl.semaphore_signal(
            barrier, 1, device_id={axis: lax.rem(me + step, parts)}, device_id_type=mesh_ids
        )
    pl.semaphore_wait(barrier, parts - 1)

    def copy_to(step):
        peer = lax.rem(me + step, parts)
        return pltpu.make_async_remote_copy(
            src_ref=blocks_ref.at[peer],
            dst_ref=out_ref.at[me],
            send_sem=send_sem.at[step],
            recv_sem=recv_sem.at[step],
            device_id={axis: peer},
            device_id_type=mesh_ids,
        )

    def copy_from(step):
        source = lax.rem(me + parts - step, parts)
        return pltpu.make_async_remote_copy(
            src_ref=blocks_ref.at[source],
            dst_ref=out_ref.at[source],
            send_sem=send_sem.at[step],
            recv_sem=recv_sem.at[step],
            device_id={axis: source},
            device_id_type=mesh_ids,
        )

    @pl.loop(1, parts)
    def _(step):
        copy_to(step).start()

    out_ref[me] = blocks_ref[me]

    @pl.loop(1, parts)
    def _(step):
        copy_to(step).wait_send()

    @pl.loop(1, parts)
    def _(step):
        copy_from(step).wait_recv()


def swap(blocks, axis, ident):
    parts = blocks.shape[0]
    lanes = 128
    shaped = blocks.reshape(parts, -1, lanes)
    out = pl.pallas_call(
        functools.partial(swap_kernel, axis),
        out_shape=jax.ShapeDtypeStruct(shaped.shape, shaped.dtype),
        in_specs=[pl.BlockSpec(memory_space=pltpu.VMEM)],
        out_specs=pl.BlockSpec(memory_space=pltpu.VMEM),
        scratch_shapes=[pltpu.SemaphoreType.DMA((parts,)), pltpu.SemaphoreType.DMA((parts,))],
        compiler_params=pltpu.CompilerParams(collective_id=ident, has_side_effects=True),
    )(shaped)
    return out.reshape(blocks.shape)


def exchange(blocks, extra, axis, ident):
    width = blocks.shape[1]
    got = swap(jnp.concatenate([blocks, extra], 1), axis, ident)
    return got[:, :width], got[:, width:].sum(0)


def spread_kernel(blocks_ref, out_ref, gathered_ref, total_ref, b_send, b_recv, c_send, c_recv):
    parts_x = blocks_ref.shape[0]
    parts_y = gathered_ref.shape[0]
    depth = blocks_ref.shape[1] - 1
    me_x = lax.axis_index("sx")
    me_y = lax.axis_index("sy")
    mesh_ids = pl.DeviceIdType.MESH
    barrier = pltpu.get_barrier_semaphore()
    for step in range(1, parts_x):
        pl.semaphore_signal(
            barrier, 1, device_id={"sx": lax.rem(me_x + step, parts_x)}, device_id_type=mesh_ids
        )
    for step in range(1, parts_y):
        pl.semaphore_signal(
            barrier, 1, device_id={"sy": lax.rem(me_y + step, parts_y)}, device_id_type=mesh_ids
        )
    pl.semaphore_wait(barrier, parts_x + parts_y - 2)

    def copy_x(step, outgoing):
        peer = lax.rem(me_x + (step if outgoing else parts_x - step), parts_x)
        return pltpu.make_async_remote_copy(
            src_ref=blocks_ref.at[peer],
            dst_ref=out_ref.at[me_x if outgoing else peer],
            send_sem=b_send.at[step],
            recv_sem=b_recv.at[step],
            device_id={"sx": peer},
            device_id_type=mesh_ids,
        )

    def copy_y(step, outgoing):
        peer = lax.rem(me_y + (step if outgoing else parts_y - step), parts_y)
        return pltpu.make_async_remote_copy(
            src_ref=total_ref,
            dst_ref=gathered_ref.at[me_y if outgoing else peer],
            send_sem=c_send.at[step],
            recv_sem=c_recv.at[step],
            device_id={"sy": peer},
            device_id_type=mesh_ids,
        )

    @pl.loop(1, parts_x)
    def _(step):
        copy_x(step, True).start()

    out_ref[me_x] = blocks_ref[me_x]

    @pl.loop(1, parts_x)
    def _(step):
        copy_x(step, True).wait_send()

    @pl.loop(1, parts_x)
    def _(step):
        copy_x(step, False).wait_recv()

    total = out_ref[0, depth : depth + 1, :]
    for source in range(1, parts_x):
        total = total + out_ref[source, depth : depth + 1, :]
    total_ref[...] = total

    @pl.loop(1, parts_y)
    def _(step):
        copy_y(step, True).start()

    gathered_ref[me_y] = total

    @pl.loop(1, parts_y)
    def _(step):
        copy_y(step, True).wait_send()

    @pl.loop(1, parts_y)
    def _(step):
        copy_y(step, False).wait_recv()


def spread(blocks, share, parts_y):
    parts_x = blocks.shape[0]
    lanes = 128
    width = share.size
    rows = jnp.pad(share, (0, lanes - width)) if width < lanes else share
    shaped = blocks.reshape(parts_x, -1, rows.size)
    shaped = jnp.concatenate(
        [shaped, jnp.broadcast_to(rows.reshape(1, 1, -1), (parts_x, 1, rows.size))], 1
    )
    vmem = pl.BlockSpec(memory_space=pltpu.VMEM)
    got, gathered = pl.pallas_call(
        spread_kernel,
        out_shape=(
            jax.ShapeDtypeStruct(shaped.shape, shaped.dtype),
            jax.ShapeDtypeStruct((parts_y, 1, rows.size), shaped.dtype),
        ),
        in_specs=[vmem],
        out_specs=(vmem, vmem),
        scratch_shapes=[
            pltpu.VMEM((1, rows.size), jnp.float32),
            pltpu.SemaphoreType.DMA((parts_x,)),
            pltpu.SemaphoreType.DMA((parts_x,)),
            pltpu.SemaphoreType.DMA((parts_y,)),
            pltpu.SemaphoreType.DMA((parts_y,)),
        ],
        compiler_params=pltpu.CompilerParams(collective_id=1, has_side_effects=True),
    )(shaped)
    return got[:, :-1].reshape(blocks.shape), gathered[:, 0, :width]


def apply_gammas(mat_re, mat_im, real_part, imag_part):
    extent = real_part.shape
    flat_re = real_part.reshape(extent[0], -1)
    flat_im = imag_part.reshape(extent[0], -1)
    out_re = jnp.dot(mat_re, flat_re, precision=HIGHEST) - jnp.dot(
        mat_im, flat_im, precision=HIGHEST
    )
    out_im = jnp.dot(mat_re, flat_im, precision=HIGHEST) + jnp.dot(
        mat_im, flat_re, precision=HIGHEST
    )
    return (out_re.reshape(extent), out_im.reshape(extent))


def project_sites(fields, source_site, momenta, rows_x, rows_y, length, depth):
    coord_x = lax.axis_index("sx") * rows_x + jnp.arange(rows_x, dtype=jnp.int32) - source_site[0]
    coord_y = lax.axis_index("sy") * rows_y + jnp.arange(rows_y, dtype=jnp.int32) - source_site[1]
    coord_z = jnp.arange(depth, dtype=jnp.int32) - source_site[2]
    part_x = jnp.mod(momenta[:, 0:1] * coord_x[None, :], length)
    part_y = jnp.mod(momenta[:, 1:2] * coord_y[None, :], length)
    part_z = jnp.mod(momenta[:, 2:3] * coord_z[None, :], depth)
    plane = jnp.mod(part_x[:, :, None] + part_y[:, None, :], length).astype(jnp.float32)
    angles = (
        2.0 * math.pi / length * plane[:, :, :, None]
        + 2.0 * math.pi / depth * part_z.astype(jnp.float32)[:, None, None, :]
    )
    angles = angles.reshape(momenta.shape[0], -1)
    cosine = jnp.cos(angles)
    sine = jnp.sin(angles)
    field_re = fields[:, 0].reshape(fields.shape[0], -1)
    field_im = fields[:, 1].reshape(fields.shape[0], -1)
    local_re = jnp.dot(field_re, cosine.T, precision=HIGHEST) + jnp.dot(
        field_im, sine.T, precision=HIGHEST
    )
    local_im = jnp.dot(field_im, cosine.T, precision=HIGHEST) - jnp.dot(
        field_re, sine.T, precision=HIGHEST
    )
    return (local_re, local_im)


def contract_kernel(mix_ref, forward_ref, backward_ref, out_ref, pair_ref):
    slices = forward_ref.shape[0]
    rows = forward_ref.shape[3]
    for t in range(slices):
        for u in range(4):
            f_re = [forward_ref[t, 0, 3 * u + c].astype(jnp.float32) for c in range(3)]
            f_im = [forward_ref[t, 1, 3 * u + c].astype(jnp.float32) for c in range(3)]
            for s in range(4):
                acc_re = None
                acc_im = None
                for c in range(3):
                    b_re = backward_ref[t, 0, 3 * s + c].astype(jnp.float32)
                    b_im = backward_ref[t, 1, 3 * s + c].astype(jnp.float32)
                    term_re = b_re * f_re[c] + b_im * f_im[c]
                    term_im = b_re * f_im[c] - b_im * f_re[c]
                    acc_re = term_re if acc_re is None else acc_re + term_re
                    acc_im = term_im if acc_im is None else acc_im + term_im
                base = (s * 4 + u) * 2 * rows
                pair_ref[base : base + rows, :] = acc_re
                pair_ref[base + rows : base + 2 * rows, :] = acc_im
        width = pair_ref.shape[0]
        kinds = mix_ref.shape[1]
        lines = out_ref.shape[1] * kinds
        row = lax.broadcasted_iota(jnp.int32, (lines, width), 0)
        col = lax.broadcasted_iota(jnp.int32, (lines, width), 1)
        pick = jnp.logical_and(row % kinds == col // rows, row // kinds == col % out_ref.shape[1])
        summed = jnp.dot(
            pick.astype(jnp.float32), pair_ref[...], precision=HIGHEST,
            preferred_element_type=jnp.float32,
        )
        for x in range(out_ref.shape[1]):
            out_ref[t, x] = jnp.dot(
                mix_ref[...], summed[x * kinds : (x + 1) * kinds], precision=HIGHEST,
                preferred_element_type=jnp.float32,
            )


def contract(forward_prop, backward_prop, gamma_table):
    slices = forward_prop.shape[0]
    rows_x = forward_prop.shape[4]
    sites = forward_prop.shape[5]
    inserts = gamma_table.shape[0]
    forward = forward_prop.reshape(slices, 2, 12, 12 * rows_x, sites)
    backward = backward_prop.reshape(slices, 2, 12, 12 * rows_x, sites)
    mat_re, mat_im = gamma_matrices(gamma_table)
    mix = jnp.stack([jnp.stack([mat_re, -mat_im], 2), jnp.stack([mat_im, mat_re], 2)], 1)
    mix = mix.reshape(inserts * 2, 16 * 2)
    out = pl.pallas_call(
        contract_kernel,
        out_shape=jax.ShapeDtypeStruct((slices, rows_x, inserts * 2, sites), jnp.float32),
        in_specs=[pl.BlockSpec(memory_space=pltpu.VMEM)] * 3,
        out_specs=pl.BlockSpec(memory_space=pltpu.VMEM),
        scratch_shapes=[pltpu.VMEM((16 * 2 * 12 * rows_x, sites), jnp.float32)],
    )(mix, forward, backward)
    return out.reshape(slices, rows_x, inserts, 2, sites).transpose(2, 0, 3, 1, 4)


def body(forward_prop, backward_prop, gamma_table, source_site, momenta):
    slices = forward_prop.shape[0]
    rows_x = forward_prop.shape[4]
    rows_y = backward_prop.shape[5] // LZ
    inserts = gamma_table.shape[0]
    fields = contract(forward_prop, backward_prop, gamma_table)
    fields = fields.reshape(inserts * slices, 2, rows_x, rows_y, LZ)
    count = fields.shape[0]
    local_re, local_im = project_sites(fields, source_site, momenta, rows_x, rows_y, L, LZ)
    partial = jnp.stack([local_re, local_im], 0)
    groups_y = lax.axis_size("sy")
    groups_x = lax.axis_size("sx")
    along_z = jnp.einsum(
        "nrxyz,rzsk->nsxyk", fields, dft_matrix(LZ, source_site[2]), precision=HIGHEST
    )
    share_z = LZ // groups_y
    blocks = along_z.reshape(count, 2, rows_x, rows_y, groups_y, share_z)
    blocks = blocks.transpose(4, 0, 1, 2, 3, 5).reshape(groups_y, -1)
    shares = partial.reshape(groups_y, -1)
    blocks, share = exchange(blocks, shares, "sy", 0)
    blocks = blocks.reshape(groups_y, count, 2, rows_x, rows_y, share_z)
    table_y = dft_matrix(rows_y * groups_y, source_site[1]).reshape(2, groups_y, rows_y, 2, -1)
    along_y = jnp.einsum("jnrxyc,rjysk->nsxkc", blocks, table_y, precision=HIGHEST)
    share_y = along_y.shape[3] // groups_x
    blocks = along_y.reshape(count, 2, rows_x, groups_x, share_y, share_z)
    blocks = blocks.transpose(3, 0, 1, 2, 4, 5).reshape(groups_x, -1)
    blocks, gathered = spread(blocks, share, groups_y)
    blocks = blocks.reshape(groups_x, count, 2, rows_x, share_y, share_z)
    table_x = dft_matrix(rows_x * groups_x, source_site[0]).reshape(2, groups_x, rows_x, 2, -1)
    spectrum = jnp.einsum("inrxbc,rixsk->nsbck", blocks, table_x, precision=HIGHEST)
    corr = spectrum.reshape(inserts, slices, 2, share_y, -1)
    listed = gathered.reshape(2, inserts, slices, -1)
    return (corr, listed)


def solution(mesh):
    placed = (
        P(None, None, None, None, "sx", "sy"),
        P(None, None, None, None, "sx", "sy"),
        P(),
        P(),
        P(),
    )
    return jax.shard_map(
        body,
        mesh=mesh,
        in_specs=placed,
        out_specs=(P(None, None, None, "sx", "sy"), P()),
        check_vma=False,
    )
```

```python
import functools
import math

import jax
import jax.numpy as jnp
from jax import lax
from jax.experimental import pallas as pl
from jax.experimental.pallas import tpu as pltpu
from jax.sharding import PartitionSpec as P

L = 64
LZ = 64


HIGHEST = lax.Precision.HIGHEST
HIGH = lax.Precision.HIGH


def gamma_matrices(gamma_table):
    inserts = gamma_table.shape[0]
    columns = gamma_table[:, :, 0]
    powers = gamma_table[:, :, 1]
    spin_ids = jnp.arange(4, dtype=jnp.int32)
    matches = (columns[:, :, None] == spin_ids[None, None, :]).astype(jnp.float32)
    unit_re = (powers == 0).astype(jnp.float32) - (powers == 2).astype(jnp.float32)
    unit_im = (powers == 1).astype(jnp.float32) - (powers == 3).astype(jnp.float32)
    return (
        (matches * unit_re[:, :, None]).reshape(inserts, 16),
        (matches * unit_im[:, :, None]).reshape(inserts, 16),
    )


def dft_table(length, anchor):
    wavenum = jnp.arange(length, dtype=jnp.int32)
    offsets = jnp.mod(wavenum - anchor, length)
    phase_index = jnp.mod(offsets[:, None] * wavenum[None, :], length)
    angles = 2.0 * math.pi / length * phase_index.astype(jnp.float32)
    return (jnp.cos(angles), -jnp.sin(angles))


def dft_matrices(length, anchors):
    wavenum = jnp.arange(length, dtype=jnp.int32)
    offsets = jnp.mod(wavenum[None, :] - anchors[:, None], length)
    phase_index = jnp.mod(offsets[:, :, None] * wavenum[None, None, :], length)
    angles = 2.0 * math.pi / length * phase_index.astype(jnp.float32)
    table_re = jnp.cos(angles)
    table_im = -jnp.sin(angles)
    rows_re = jnp.stack([table_re, table_im], 2)
    rows_im = jnp.stack([-table_im, table_re], 2)
    return jnp.stack([rows_re, rows_im], 1)


def swap_kernel(axis, blocks_ref, out_ref, send_sem, recv_sem):
    parts = blocks_ref.shape[0]
    me = lax.axis_index(axis)
    mesh_ids = pl.DeviceIdType.MESH
    barrier = pltpu.get_barrier_semaphore()
    for step in range(1, parts):
        pl.semaphore_signal(
            barrier, 1, device_id={axis: lax.rem(me + step, parts)}, device_id_type=mesh_ids
        )
    pl.semaphore_wait(barrier, parts - 1)

    def copy_to(step):
        peer = lax.rem(me + step, parts)
        return pltpu.make_async_remote_copy(
            src_ref=blocks_ref.at[peer],
            dst_ref=out_ref.at[me],
            send_sem=send_sem.at[step],
            recv_sem=recv_sem.at[step],
            device_id={axis: peer},
            device_id_type=mesh_ids,
        )

    def copy_from(step):
        source = lax.rem(me + parts - step, parts)
        return pltpu.make_async_remote_copy(
            src_ref=blocks_ref.at[source],
            dst_ref=out_ref.at[source],
            send_sem=send_sem.at[step],
            recv_sem=recv_sem.at[step],
            device_id={axis: source},
            device_id_type=mesh_ids,
        )

    @pl.loop(1, parts)
    def _(step):
        copy_to(step).start()

    out_ref[me] = blocks_ref[me]

    @pl.loop(1, parts)
    def _(step):
        copy_to(step).wait_send()

    @pl.loop(1, parts)
    def _(step):
        copy_from(step).wait_recv()


def swap(blocks, axis, ident):
    parts = blocks.shape[0]
    lanes = 128
    shaped = blocks.reshape(parts, -1, lanes)
    out = pl.pallas_call(
        functools.partial(swap_kernel, axis),
        out_shape=jax.ShapeDtypeStruct(shaped.shape, shaped.dtype),
        in_specs=[pl.BlockSpec(memory_space=pltpu.VMEM)],
        out_specs=pl.BlockSpec(memory_space=pltpu.VMEM),
        scratch_shapes=[pltpu.SemaphoreType.DMA((parts,)), pltpu.SemaphoreType.DMA((parts,))],
        compiler_params=pltpu.CompilerParams(collective_id=ident, has_side_effects=True),
    )(shaped)
    return out.reshape(blocks.shape)


def exchange(blocks, extra, axis, ident):
    width = blocks.shape[1]
    got = swap(jnp.concatenate([blocks, extra], 1), axis, ident)
    return got[:, :width], got[:, width:].sum(0)


def spread_kernel(blocks_ref, out_ref, gathered_ref, total_ref, b_send, b_recv, c_send, c_recv):
    parts_x = blocks_ref.shape[0]
    parts_y = gathered_ref.shape[0]
    depth = blocks_ref.shape[1] - 1
    me_x = lax.axis_index("sx")
    me_y = lax.axis_index("sy")
    mesh_ids = pl.DeviceIdType.MESH
    barrier = pltpu.get_barrier_semaphore()
    for step in range(1, parts_x):
        pl.semaphore_signal(
            barrier, 1, device_id={"sx": lax.rem(me_x + step, parts_x)}, device_id_type=mesh_ids
        )
    for step in range(1, parts_y):
        pl.semaphore_signal(
            barrier, 1, device_id={"sy": lax.rem(me_y + step, parts_y)}, device_id_type=mesh_ids
        )
    pl.semaphore_wait(barrier, parts_x + parts_y - 2)

    def copy_x(step, outgoing):
        peer = lax.rem(me_x + (step if outgoing else parts_x - step), parts_x)
        return pltpu.make_async_remote_copy(
            src_ref=blocks_ref.at[peer],
            dst_ref=out_ref.at[me_x if outgoing else peer],
            send_sem=b_send.at[step],
            recv_sem=b_recv.at[step],
            device_id={"sx": peer},
            device_id_type=mesh_ids,
        )

    def copy_y(step, outgoing):
        peer = lax.rem(me_y + (step if outgoing else parts_y - step), parts_y)
        return pltpu.make_async_remote_copy(
            src_ref=total_ref,
            dst_ref=gathered_ref.at[me_y if outgoing else peer],
            send_sem=c_send.at[step],
            recv_sem=c_recv.at[step],
            device_id={"sy": peer},
            device_id_type=mesh_ids,
        )

    @pl.loop(1, parts_x)
    def _(step):
        copy_x(step, True).start()

    out_ref[me_x] = blocks_ref[me_x]

    @pl.loop(1, parts_x)
    def _(step):
        copy_x(step, True).wait_send()

    @pl.loop(1, parts_x)
    def _(step):
        copy_x(step, False).wait_recv()

    total = out_ref[0, depth : depth + 1, :]
    for source in range(1, parts_x):
        total = total + out_ref[source, depth : depth + 1, :]
    total_ref[...] = total

    @pl.loop(1, parts_y)
    def _(step):
        copy_y(step, True).start()

    gathered_ref[me_y] = total

    @pl.loop(1, parts_y)
    def _(step):
        copy_y(step, True).wait_send()

    @pl.loop(1, parts_y)
    def _(step):
        copy_y(step, False).wait_recv()


def spread(blocks, share, parts_y):
    parts_x = blocks.shape[0]
    lanes = 128
    width = share.size
    rows = jnp.pad(share, (0, lanes - width)) if width < lanes else share
    shaped = blocks.reshape(parts_x, -1, rows.size)
    shaped = jnp.concatenate(
        [shaped, jnp.broadcast_to(rows.reshape(1, 1, -1), (parts_x, 1, rows.size))], 1
    )
    vmem = pl.BlockSpec(memory_space=pltpu.VMEM)
    got, gathered = pl.pallas_call(
        spread_kernel,
        out_shape=(
            jax.ShapeDtypeStruct(shaped.shape, shaped.dtype),
            jax.ShapeDtypeStruct((parts_y, 1, rows.size), shaped.dtype),
        ),
        in_specs=[vmem],
        out_specs=(vmem, vmem),
        scratch_shapes=[
            pltpu.VMEM((1, rows.size), jnp.float32),
            pltpu.SemaphoreType.DMA((parts_x,)),
            pltpu.SemaphoreType.DMA((parts_x,)),
            pltpu.SemaphoreType.DMA((parts_y,)),
            pltpu.SemaphoreType.DMA((parts_y,)),
        ],
        compiler_params=pltpu.CompilerParams(collective_id=1, has_side_effects=True),
    )(shaped)
    return got[:, :-1].reshape(blocks.shape), gathered[:, 0, :width]


def apply_gammas(mat_re, mat_im, real_part, imag_part):
    extent = real_part.shape
    flat_re = real_part.reshape(extent[0], -1)
    flat_im = imag_part.reshape(extent[0], -1)
    out_re = jnp.dot(mat_re, flat_re, precision=HIGHEST) - jnp.dot(
        mat_im, flat_im, precision=HIGHEST
    )
    out_im = jnp.dot(mat_re, flat_im, precision=HIGHEST) + jnp.dot(
        mat_im, flat_re, precision=HIGHEST
    )
    return (out_re.reshape(extent), out_im.reshape(extent))


def project_sites(fields, source_site, momenta, rows_x, rows_y, length, depth):
    coord_x = lax.axis_index("sx") * rows_x + jnp.arange(rows_x, dtype=jnp.int32) - source_site[0]
    coord_y = lax.axis_index("sy") * rows_y + jnp.arange(rows_y, dtype=jnp.int32) - source_site[1]
    coord_z = jnp.arange(depth, dtype=jnp.int32) - source_site[2]
    part_x = jnp.mod(momenta[:, 0:1] * coord_x[None, :], length)
    part_y = jnp.mod(momenta[:, 1:2] * coord_y[None, :], length)
    part_z = jnp.mod(momenta[:, 2:3] * coord_z[None, :], depth)
    plane = jnp.mod(part_x[:, :, None] + part_y[:, None, :], length).astype(jnp.float32)
    angles = (
        2.0 * math.pi / length * plane[:, :, :, None]
        + 2.0 * math.pi / depth * part_z.astype(jnp.float32)[:, None, None, :]
    )
    angles = angles.reshape(momenta.shape[0], -1)
    cosine = jnp.cos(angles)
    sine = jnp.sin(angles)
    field_re = fields[:, 0].reshape(fields.shape[0], -1)
    field_im = fields[:, 1].reshape(fields.shape[0], -1)
    local_re = jnp.dot(field_re, cosine.T, precision=HIGHEST) + jnp.dot(
        field_im, sine.T, precision=HIGHEST
    )
    local_im = jnp.dot(field_im, cosine.T, precision=HIGHEST) - jnp.dot(
        field_re, sine.T, precision=HIGHEST
    )
    return (local_re, local_im)


def contract_kernel(mix_ref, forward_ref, backward_ref, out_ref, pair_ref):
    slices = forward_ref.shape[0]
    rows = forward_ref.shape[3]
    for t in range(slices):
        for u in range(4):
            f_re = [forward_ref[t, 0, 3 * u + c].astype(jnp.float32) for c in range(3)]
            f_im = [forward_ref[t, 1, 3 * u + c].astype(jnp.float32) for c in range(3)]
            for s in range(4):
                acc_re = None
                acc_im = None
                for c in range(3):
                    b_re = backward_ref[t, 0, 3 * s + c].astype(jnp.float32)
                    b_im = backward_ref[t, 1, 3 * s + c].astype(jnp.float32)
                    term_re = b_re * f_re[c] + b_im * f_im[c]
                    term_im = b_re * f_im[c] - b_im * f_re[c]
                    acc_re = term_re if acc_re is None else acc_re + term_re
                    acc_im = term_im if acc_im is None else acc_im + term_im
                base = (s * 4 + u) * 2 * rows
                pair_ref[base : base + rows, :] = acc_re
                pair_ref[base + rows : base + 2 * rows, :] = acc_im
        width = pair_ref.shape[0]
        kinds = mix_ref.shape[1]
        lines = out_ref.shape[1] * kinds
        row = lax.broadcasted_iota(jnp.int32, (lines, width), 0)
        col = lax.broadcasted_iota(jnp.int32, (lines, width), 1)
        pick = jnp.logical_and(row % kinds == col // rows, row // kinds == col % out_ref.shape[1])
        summed = jnp.dot(
            pick.astype(jnp.float32), pair_ref[...], precision=HIGHEST,
            preferred_element_type=jnp.float32,
        )
        for x in range(out_ref.shape[1]):
            out_ref[t, x] = jnp.dot(
                mix_ref[...], summed[x * kinds : (x + 1) * kinds], precision=HIGHEST,
                preferred_element_type=jnp.float32,
            )


def contract(forward_prop, backward_prop, gamma_table):
    slices = forward_prop.shape[0]
    rows_x = forward_prop.shape[4]
    sites = forward_prop.shape[5]
    inserts = gamma_table.shape[0]
    forward = forward_prop.reshape(slices, 2, 12, 12 * rows_x, sites)
    backward = backward_prop.reshape(slices, 2, 12, 12 * rows_x, sites)
    mat_re, mat_im = gamma_matrices(gamma_table)
    mix = jnp.stack([jnp.stack([mat_re, -mat_im], 2), jnp.stack([mat_im, mat_re], 2)], 1)
    mix = mix.reshape(inserts * 2, 16 * 2)
    out = pl.pallas_call(
        contract_kernel,
        out_shape=jax.ShapeDtypeStruct((slices, rows_x, inserts * 2, sites), jnp.float32),
        in_specs=[pl.BlockSpec(memory_space=pltpu.VMEM)] * 3,
        out_specs=pl.BlockSpec(memory_space=pltpu.VMEM),
        scratch_shapes=[pltpu.VMEM((16 * 2 * 12 * rows_x, sites), jnp.float32)],
    )(mix, forward, backward)
    return out.reshape(slices, rows_x, inserts, 2, sites).transpose(2, 0, 3, 1, 4)


def body(forward_prop, backward_prop, gamma_table, source_site, momenta):
    slices = forward_prop.shape[0]
    rows_x = forward_prop.shape[4]
    rows_y = backward_prop.shape[5] // LZ
    inserts = gamma_table.shape[0]
    fields = contract(forward_prop, backward_prop, gamma_table)
    fields = fields.reshape(inserts * slices, 2, rows_x, rows_y, LZ)
    count = fields.shape[0]
    local_re, local_im = project_sites(fields, source_site, momenta, rows_x, rows_y, L, LZ)
    partial = jnp.stack([local_re, local_im], 0)
    groups_y = lax.axis_size("sy")
    groups_x = lax.axis_size("sx")
    tables = dft_matrices(LZ, source_site)
    along_z = jnp.einsum("nrxyz,rzsk->nsxyk", fields, tables[2], precision=HIGH)
    share_z = LZ // groups_y
    blocks = along_z.reshape(count, 2, rows_x, rows_y, groups_y, share_z)
    blocks = blocks.transpose(4, 0, 1, 2, 3, 5).reshape(groups_y, -1)
    shares = partial.reshape(groups_y, -1)
    blocks, share = exchange(blocks, shares, "sy", 0)
    blocks = blocks.reshape(groups_y, count, 2, rows_x, rows_y, share_z)
    table_y = tables[1].reshape(2, groups_y, rows_y, 2, -1)
    along_y = jnp.einsum("jnrxyc,rjysk->nsxkc", blocks, table_y, precision=HIGH)
    share_y = along_y.shape[3] // groups_x
    blocks = along_y.reshape(count, 2, rows_x, groups_x, share_y, share_z)
    blocks = blocks.transpose(3, 0, 1, 2, 4, 5).reshape(groups_x, -1)
    blocks, gathered = spread(blocks, share, groups_y)
    blocks = blocks.reshape(groups_x, count, 2, rows_x, share_y, share_z)
    table_x = tables[0].reshape(2, groups_x, rows_x, 2, -1)
    spectrum = jnp.einsum("inrxbc,rixsk->nsbck", blocks, table_x, precision=HIGH)
    corr = spectrum.reshape(inserts, slices, 2, share_y, -1)
    listed = gathered.reshape(2, inserts, slices, -1)
    return (corr, listed)


def solution(mesh):
    placed = (
        P(None, None, None, None, "sx", "sy"),
        P(None, None, None, None, "sx", "sy"),
        P(),
        P(),
        P(),
    )
    return jax.shard_map(
        body,
        mesh=mesh,
        in_specs=placed,
        out_specs=(P(None, None, None, "sx", "sy"), P()),
        check_vma=False,
    )
```

```python
import functools
import math

import jax
import jax.numpy as jnp
from jax import lax
from jax.experimental import pallas as pl
from jax.experimental.pallas import tpu as pltpu
from jax.sharding import PartitionSpec as P

L = 64
LZ = 64


HIGHEST = lax.Precision.HIGHEST
HIGH = lax.Precision.HIGH


def gamma_matrices(gamma_table):
    inserts = gamma_table.shape[0]
    columns = gamma_table[:, :, 0]
    powers = gamma_table[:, :, 1]
    spin_ids = jnp.arange(4, dtype=jnp.int32)
    matches = (columns[:, :, None] == spin_ids[None, None, :]).astype(jnp.float32)
    unit_re = (powers == 0).astype(jnp.float32) - (powers == 2).astype(jnp.float32)
    unit_im = (powers == 1).astype(jnp.float32) - (powers == 3).astype(jnp.float32)
    return (
        (matches * unit_re[:, :, None]).reshape(inserts, 16),
        (matches * unit_im[:, :, None]).reshape(inserts, 16),
    )


def dft_table(length, anchor):
    wavenum = jnp.arange(length, dtype=jnp.int32)
    offsets = jnp.mod(wavenum - anchor, length)
    phase_index = jnp.mod(offsets[:, None] * wavenum[None, :], length)
    angles = 2.0 * math.pi / length * phase_index.astype(jnp.float32)
    return (jnp.cos(angles), -jnp.sin(angles))


def dft_matrices(length, anchors):
    wavenum = jnp.arange(length, dtype=jnp.int32)
    offsets = jnp.mod(wavenum[None, :] - anchors[:, None], length)
    phase_index = jnp.mod(offsets[:, :, None] * wavenum[None, None, :], length)
    angles = 2.0 * math.pi / length * phase_index.astype(jnp.float32)
    table_re = jnp.cos(angles)
    table_im = -jnp.sin(angles)
    rows_re = jnp.stack([table_re, table_im], 2)
    rows_im = jnp.stack([-table_im, table_re], 2)
    return jnp.stack([rows_re, rows_im], 1)


def swap_kernel(axis, blocks_ref, out_ref, send_sem, recv_sem):
    parts = blocks_ref.shape[0]
    me = lax.axis_index(axis)
    mesh_ids = pl.DeviceIdType.MESH
    barrier = pltpu.get_barrier_semaphore()
    for step in range(1, parts):
        pl.semaphore_signal(
            barrier, 1, device_id={axis: lax.rem(me + step, parts)}, device_id_type=mesh_ids
        )
    pl.semaphore_wait(barrier, parts - 1)

    def copy_to(step):
        peer = lax.rem(me + step, parts)
        return pltpu.make_async_remote_copy(
            src_ref=blocks_ref.at[peer],
            dst_ref=out_ref.at[me],
            send_sem=send_sem.at[step],
            recv_sem=recv_sem.at[step],
            device_id={axis: peer},
            device_id_type=mesh_ids,
        )

    def copy_from(step):
        source = lax.rem(me + parts - step, parts)
        return pltpu.make_async_remote_copy(
            src_ref=blocks_ref.at[source],
            dst_ref=out_ref.at[source],
            send_sem=send_sem.at[step],
            recv_sem=recv_sem.at[step],
            device_id={axis: source},
            device_id_type=mesh_ids,
        )

    @pl.loop(1, parts)
    def _(step):
        copy_to(step).start()

    out_ref[me] = blocks_ref[me]

    @pl.loop(1, parts)
    def _(step):
        copy_to(step).wait_send()

    @pl.loop(1, parts)
    def _(step):
        copy_from(step).wait_recv()


def swap(blocks, axis, ident):
    parts = blocks.shape[0]
    lanes = 128
    shaped = blocks.reshape(parts, -1, lanes)
    out = pl.pallas_call(
        functools.partial(swap_kernel, axis),
        out_shape=jax.ShapeDtypeStruct(shaped.shape, shaped.dtype),
        in_specs=[pl.BlockSpec(memory_space=pltpu.VMEM)],
        out_specs=pl.BlockSpec(memory_space=pltpu.VMEM),
        scratch_shapes=[pltpu.SemaphoreType.DMA((parts,)), pltpu.SemaphoreType.DMA((parts,))],
        compiler_params=pltpu.CompilerParams(collective_id=ident, has_side_effects=True),
    )(shaped)
    return out.reshape(blocks.shape)


def exchange(blocks, extra, axis, ident):
    width = blocks.shape[1]
    got = swap(jnp.concatenate([blocks, extra], 1), axis, ident)
    return got[:, :width], got[:, width:].sum(0)


def turn_kernel(sent_ref, table_ref, ready_ref, landed_ref, send_sem, recv_sem):
    parts = sent_ref.shape[0]
    depth = sent_ref.shape[1] - 1
    band = ready_ref.shape[1] - 1
    me = lax.axis_index("sy")
    mesh_ids = pl.DeviceIdType.MESH
    barrier = pltpu.get_barrier_semaphore()
    for step in range(1, parts):
        pl.semaphore_signal(
            barrier, 1, device_id={"sy": lax.rem(me + step, parts)}, device_id_type=mesh_ids
        )
    pl.semaphore_wait(barrier, parts - 1)

    def copy_y(step, outgoing):
        peer = lax.rem(me + (step if outgoing else parts - step), parts)
        return pltpu.make_async_remote_copy(
            src_ref=sent_ref.at[peer],
            dst_ref=landed_ref.at[me if outgoing else peer],
            send_sem=send_sem.at[step],
            recv_sem=recv_sem.at[step],
            device_id={"sy": peer},
            device_id_type=mesh_ids,
        )

    @pl.loop(1, parts)
    def _(step):
        copy_y(step, True).start()

    landed_ref[me] = sent_ref[me]

    @pl.loop(1, parts)
    def _(step):
        copy_y(step, True).wait_send()

    @pl.loop(1, parts)
    def _(step):
        copy_y(step, False).wait_recv()

    block = landed_ref[:, 0:depth, :].reshape(parts * depth, -1)
    turned = jnp.dot(table_ref[...], block, precision=HIGHEST, preferred_element_type=jnp.float32)
    share = landed_ref[0, depth : depth + 1, :]
    for source in range(1, parts):
        share = share + landed_ref[source, depth : depth + 1, :]
    for peer in range(ready_ref.shape[0]):
        ready_ref[peer, 0:band, :] = turned[peer * band : (peer + 1) * band]
        ready_ref[peer, band : band + 1, :] = share


def turn(sent, table, parts_x, band):
    parts_y, rows, width = sent.shape
    vmem = pl.BlockSpec(memory_space=pltpu.VMEM)
    return pl.pallas_call(
        turn_kernel,
        out_shape=jax.ShapeDtypeStruct((parts_x, band + 1, width), jnp.float32),
        in_specs=[vmem, vmem],
        out_specs=vmem,
        scratch_shapes=[
            pltpu.VMEM((parts_y, rows, width), jnp.float32),
            pltpu.SemaphoreType.DMA((parts_y,)),
            pltpu.SemaphoreType.DMA((parts_y,)),
        ],
        compiler_params=pltpu.CompilerParams(collective_id=0, has_side_effects=True),
    )(sent, table)


def turn_table(length, anchor, rows_y, share_y):
    line = jnp.arange(2 * length, dtype=jnp.int32)
    wave = line[:, None] // 2
    out_part = line[:, None] % 2
    in_part = (line[None, :] // rows_y) % 2
    site = (line[None, :] // (2 * rows_y)) * rows_y + line[None, :] % rows_y
    offset = jnp.mod(site - anchor, length)
    index = jnp.mod(offset * wave + (length // 4) * (out_part - in_part), length)
    return jnp.cos(2.0 * math.pi / length * index.astype(jnp.float32))


def spread_kernel(blocks_ref, out_ref, gathered_ref, total_ref, b_send, b_recv, c_send, c_recv):
    parts_x = blocks_ref.shape[0]
    parts_y = gathered_ref.shape[0]
    depth = blocks_ref.shape[1] - 1
    me_x = lax.axis_index("sx")
    me_y = lax.axis_index("sy")
    mesh_ids = pl.DeviceIdType.MESH
    barrier = pltpu.get_barrier_semaphore()
    for step in range(1, parts_x):
        pl.semaphore_signal(
            barrier, 1, device_id={"sx": lax.rem(me_x + step, parts_x)}, device_id_type=mesh_ids
        )
    for step in range(1, parts_y):
        pl.semaphore_signal(
            barrier, 1, device_id={"sy": lax.rem(me_y + step, parts_y)}, device_id_type=mesh_ids
        )
    pl.semaphore_wait(barrier, parts_x + parts_y - 2)

    def copy_x(step, outgoing):
        peer = lax.rem(me_x + (step if outgoing else parts_x - step), parts_x)
        return pltpu.make_async_remote_copy(
            src_ref=blocks_ref.at[peer],
            dst_ref=out_ref.at[me_x if outgoing else peer],
            send_sem=b_send.at[step],
            recv_sem=b_recv.at[step],
            device_id={"sx": peer},
            device_id_type=mesh_ids,
        )

    def copy_y(step, outgoing):
        peer = lax.rem(me_y + (step if outgoing else parts_y - step), parts_y)
        return pltpu.make_async_remote_copy(
            src_ref=total_ref,
            dst_ref=gathered_ref.at[me_y if outgoing else peer],
            send_sem=c_send.at[step],
            recv_sem=c_recv.at[step],
            device_id={"sy": peer},
            device_id_type=mesh_ids,
        )

    @pl.loop(1, parts_x)
    def _(step):
        copy_x(step, True).start()

    out_ref[me_x] = blocks_ref[me_x]

    @pl.loop(1, parts_x)
    def _(step):
        copy_x(step, True).wait_send()

    @pl.loop(1, parts_x)
    def _(step):
        copy_x(step, False).wait_recv()

    total = out_ref[0, depth : depth + 1, :]
    for source in range(1, parts_x):
        total = total + out_ref[source, depth : depth + 1, :]
    total_ref[...] = total

    @pl.loop(1, parts_y)
    def _(step):
        copy_y(step, True).start()

    gathered_ref[me_y] = total

    @pl.loop(1, parts_y)
    def _(step):
        copy_y(step, True).wait_send()

    @pl.loop(1, parts_y)
    def _(step):
        copy_y(step, False).wait_recv()


def spread_ready(shaped):
    parts_x = shaped.shape[0]
    parts_y = lax.axis_size("sy")
    vmem = pl.BlockSpec(memory_space=pltpu.VMEM)
    got, gathered = pl.pallas_call(
        spread_kernel,
        out_shape=(
            jax.ShapeDtypeStruct(shaped.shape, shaped.dtype),
            jax.ShapeDtypeStruct((parts_y, 1, shaped.shape[2]), shaped.dtype),
        ),
        in_specs=[vmem],
        out_specs=(vmem, vmem),
        scratch_shapes=[
            pltpu.VMEM((1, shaped.shape[2]), jnp.float32),
            pltpu.SemaphoreType.DMA((parts_x,)),
            pltpu.SemaphoreType.DMA((parts_x,)),
            pltpu.SemaphoreType.DMA((parts_y,)),
            pltpu.SemaphoreType.DMA((parts_y,)),
        ],
        compiler_params=pltpu.CompilerParams(collective_id=1, has_side_effects=True),
    )(shaped)
    return got[:, :-1], gathered[:, 0]


def spread(blocks, share, parts_y):
    parts_x = blocks.shape[0]
    lanes = 128
    width = share.size
    rows = jnp.pad(share, (0, lanes - width)) if width < lanes else share
    shaped = blocks.reshape(parts_x, -1, rows.size)
    shaped = jnp.concatenate(
        [shaped, jnp.broadcast_to(rows.reshape(1, 1, -1), (parts_x, 1, rows.size))], 1
    )
    vmem = pl.BlockSpec(memory_space=pltpu.VMEM)
    got, gathered = pl.pallas_call(
        spread_kernel,
        out_shape=(
            jax.ShapeDtypeStruct(shaped.shape, shaped.dtype),
            jax.ShapeDtypeStruct((parts_y, 1, rows.size), shaped.dtype),
        ),
        in_specs=[vmem],
        out_specs=(vmem, vmem),
        scratch_shapes=[
            pltpu.VMEM((1, rows.size), jnp.float32),
            pltpu.SemaphoreType.DMA((parts_x,)),
            pltpu.SemaphoreType.DMA((parts_x,)),
            pltpu.SemaphoreType.DMA((parts_y,)),
            pltpu.SemaphoreType.DMA((parts_y,)),
        ],
        compiler_params=pltpu.CompilerParams(collective_id=1, has_side_effects=True),
    )(shaped)
    return got[:, :-1].reshape(blocks.shape), gathered[:, 0, :width]


def apply_gammas(mat_re, mat_im, real_part, imag_part):
    extent = real_part.shape
    flat_re = real_part.reshape(extent[0], -1)
    flat_im = imag_part.reshape(extent[0], -1)
    out_re = jnp.dot(mat_re, flat_re, precision=HIGHEST) - jnp.dot(
        mat_im, flat_im, precision=HIGHEST
    )
    out_im = jnp.dot(mat_re, flat_im, precision=HIGHEST) + jnp.dot(
        mat_im, flat_re, precision=HIGHEST
    )
    return (out_re.reshape(extent), out_im.reshape(extent))


def project_sites(fields, source_site, momenta, rows_x, rows_y, length, depth):
    coord_x = lax.axis_index("sx") * rows_x + jnp.arange(rows_x, dtype=jnp.int32) - source_site[0]
    coord_y = lax.axis_index("sy") * rows_y + jnp.arange(rows_y, dtype=jnp.int32) - source_site[1]
    coord_z = jnp.arange(depth, dtype=jnp.int32) - source_site[2]
    part_x = jnp.mod(momenta[:, 0:1] * coord_x[None, :], length)
    part_y = jnp.mod(momenta[:, 1:2] * coord_y[None, :], length)
    part_z = jnp.mod(momenta[:, 2:3] * coord_z[None, :], depth)
    plane = jnp.mod(part_x[:, :, None] + part_y[:, None, :], length).astype(jnp.float32)
    angles = (
        2.0 * math.pi / length * plane[:, :, :, None]
        + 2.0 * math.pi / depth * part_z.astype(jnp.float32)[:, None, None, :]
    )
    angles = angles.reshape(momenta.shape[0], -1)
    cosine = jnp.cos(angles)
    sine = jnp.sin(angles)
    field_re = fields[:, 0].reshape(fields.shape[0], -1)
    field_im = fields[:, 1].reshape(fields.shape[0], -1)
    local_re = jnp.dot(field_re, cosine.T, precision=HIGHEST) + jnp.dot(
        field_im, sine.T, precision=HIGHEST
    )
    local_im = jnp.dot(field_im, cosine.T, precision=HIGHEST) - jnp.dot(
        field_re, sine.T, precision=HIGHEST
    )
    return (local_re, local_im)


def contract_kernel(mix_ref, forward_ref, backward_ref, out_ref, pair_ref):
    slices = forward_ref.shape[0]
    rows = forward_ref.shape[3]
    for t in range(slices):
        for u in range(4):
            f_re = [forward_ref[t, 0, 3 * u + c].astype(jnp.float32) for c in range(3)]
            f_im = [forward_ref[t, 1, 3 * u + c].astype(jnp.float32) for c in range(3)]
            for s in range(4):
                acc_re = None
                acc_im = None
                for c in range(3):
                    b_re = backward_ref[t, 0, 3 * s + c].astype(jnp.float32)
                    b_im = backward_ref[t, 1, 3 * s + c].astype(jnp.float32)
                    term_re = b_re * f_re[c] + b_im * f_im[c]
                    term_im = b_re * f_im[c] - b_im * f_re[c]
                    acc_re = term_re if acc_re is None else acc_re + term_re
                    acc_im = term_im if acc_im is None else acc_im + term_im
                base = (s * 4 + u) * 2 * rows
                pair_ref[base : base + rows, :] = acc_re
                pair_ref[base + rows : base + 2 * rows, :] = acc_im
        width = pair_ref.shape[0]
        kinds = mix_ref.shape[1]
        lines = out_ref.shape[1] * kinds
        row = lax.broadcasted_iota(jnp.int32, (lines, width), 0)
        col = lax.broadcasted_iota(jnp.int32, (lines, width), 1)
        pick = jnp.logical_and(row % kinds == col // rows, row // kinds == col % out_ref.shape[1])
        summed = jnp.dot(
            pick.astype(jnp.float32), pair_ref[...], precision=HIGHEST,
            preferred_element_type=jnp.float32,
        )
        for x in range(out_ref.shape[1]):
            out_ref[t, x] = jnp.dot(
                mix_ref[...], summed[x * kinds : (x + 1) * kinds], precision=HIGHEST,
                preferred_element_type=jnp.float32,
            )


def contract(forward_prop, backward_prop, gamma_table):
    slices = forward_prop.shape[0]
    rows_x = forward_prop.shape[4]
    sites = forward_prop.shape[5]
    inserts = gamma_table.shape[0]
    forward = forward_prop.reshape(slices, 2, 12, 12 * rows_x, sites)
    backward = backward_prop.reshape(slices, 2, 12, 12 * rows_x, sites)
    mat_re, mat_im = gamma_matrices(gamma_table)
    mix = jnp.stack([jnp.stack([mat_re, -mat_im], 2), jnp.stack([mat_im, mat_re], 2)], 1)
    mix = mix.reshape(inserts * 2, 16 * 2)
    out = pl.pallas_call(
        contract_kernel,
        out_shape=jax.ShapeDtypeStruct((slices, rows_x, inserts * 2, sites), jnp.float32),
        in_specs=[pl.BlockSpec(memory_space=pltpu.VMEM)] * 3,
        out_specs=pl.BlockSpec(memory_space=pltpu.VMEM),
        scratch_shapes=[pltpu.VMEM((16 * 2 * 12 * rows_x, sites), jnp.float32)],
    )(mix, forward, backward)
    return out.reshape(slices, rows_x, inserts, 2, sites).transpose(2, 0, 3, 1, 4)


def body(forward_prop, backward_prop, gamma_table, source_site, momenta):
    slices = forward_prop.shape[0]
    rows_x = forward_prop.shape[4]
    rows_y = backward_prop.shape[5] // LZ
    inserts = gamma_table.shape[0]
    fields = contract(forward_prop, backward_prop, gamma_table)
    fields = fields.reshape(inserts * slices, 2, rows_x, rows_y, LZ)
    count = fields.shape[0]
    local_re, local_im = project_sites(fields, source_site, momenta, rows_x, rows_y, L, LZ)
    partial = jnp.stack([local_re, local_im], 0)
    groups_y = lax.axis_size("sy")
    groups_x = lax.axis_size("sx")
    tables = dft_matrices(LZ, source_site)
    share_z = LZ // groups_y
    table_z = tables[2].reshape(2, LZ, 2, groups_y, share_z)
    blocks = jnp.einsum("nrxyz,rzsjc->jsynxc", fields, table_z, precision=HIGH)
    blocks = blocks.reshape(groups_y, 2 * rows_y, -1)
    width = blocks.shape[2]
    shares = partial.reshape(groups_y, 1, -1)
    shares = jnp.pad(shares, ((0, 0), (0, 0), (0, width - shares.shape[2])))
    share_y = rows_y * groups_y // groups_x
    table_y = turn_table(rows_y * groups_y, source_site[1], rows_y, share_y)
    ready = turn(jnp.concatenate([blocks, shares], 1), table_y, groups_x, 2 * share_y)
    blocks, gathered = spread_ready(ready)
    blocks = blocks.reshape(groups_x, share_y, 2, count, rows_x, share_z)
    gathered = gathered[:, : partial.size // groups_y]
    table_x = tables[0].reshape(2, groups_x, rows_x, 2, -1)
    spectrum = jnp.einsum("ibsnxc,sixtk->ntbck", blocks, table_x, precision=HIGH)
    corr = spectrum.reshape(inserts, slices, 2, share_y, -1)
    listed = gathered.reshape(2, inserts, slices, -1)
    return (corr, listed)


def solution(mesh):
    placed = (
        P(None, None, None, None, "sx", "sy"),
        P(None, None, None, None, "sx", "sy"),
        P(),
        P(),
        P(),
    )
    return jax.shard_map(
        body,
        mesh=mesh,
        in_specs=placed,
        out_specs=(P(None, None, None, "sx", "sy"), P()),
        check_vma=False,
    )
```

```python
import functools
import math

import jax
import jax.numpy as jnp
from jax import lax
from jax.experimental import pallas as pl
from jax.experimental.pallas import tpu as pltpu
from jax.sharding import PartitionSpec as P

L = 64
LZ = 64


HIGHEST = lax.Precision.HIGHEST
HIGH = lax.Precision.HIGH


def gamma_matrices(gamma_table):
    inserts = gamma_table.shape[0]
    columns = gamma_table[:, :, 0]
    powers = gamma_table[:, :, 1]
    spin_ids = jnp.arange(4, dtype=jnp.int32)
    matches = (columns[:, :, None] == spin_ids[None, None, :]).astype(jnp.float32)
    unit_re = (powers == 0).astype(jnp.float32) - (powers == 2).astype(jnp.float32)
    unit_im = (powers == 1).astype(jnp.float32) - (powers == 3).astype(jnp.float32)
    return (
        (matches * unit_re[:, :, None]).reshape(inserts, 16),
        (matches * unit_im[:, :, None]).reshape(inserts, 16),
    )


def dft_table(length, anchor):
    wavenum = jnp.arange(length, dtype=jnp.int32)
    offsets = jnp.mod(wavenum - anchor, length)
    phase_index = jnp.mod(offsets[:, None] * wavenum[None, :], length)
    angles = 2.0 * math.pi / length * phase_index.astype(jnp.float32)
    return (jnp.cos(angles), -jnp.sin(angles))


def dft_matrices(length, anchors):
    wavenum = jnp.arange(length, dtype=jnp.int32)
    offsets = jnp.mod(wavenum[None, :] - anchors[:, None], length)
    phase_index = jnp.mod(offsets[:, :, None] * wavenum[None, None, :], length)
    angles = 2.0 * math.pi / length * phase_index.astype(jnp.float32)
    table_re = jnp.cos(angles)
    table_im = -jnp.sin(angles)
    rows_re = jnp.stack([table_re, table_im], 2)
    rows_im = jnp.stack([-table_im, table_re], 2)
    return jnp.stack([rows_re, rows_im], 1)


def swap_kernel(axis, blocks_ref, out_ref, send_sem, recv_sem):
    parts = blocks_ref.shape[0]
    me = lax.axis_index(axis)
    mesh_ids = pl.DeviceIdType.MESH
    barrier = pltpu.get_barrier_semaphore()
    for step in range(1, parts):
        pl.semaphore_signal(
            barrier, 1, device_id={axis: lax.rem(me + step, parts)}, device_id_type=mesh_ids
        )
    pl.semaphore_wait(barrier, parts - 1)

    def copy_to(step):
        peer = lax.rem(me + step, parts)
        return pltpu.make_async_remote_copy(
            src_ref=blocks_ref.at[peer],
            dst_ref=out_ref.at[me],
            send_sem=send_sem.at[step],
            recv_sem=recv_sem.at[step],
            device_id={axis: peer},
            device_id_type=mesh_ids,
        )

    def copy_from(step):
        source = lax.rem(me + parts - step, parts)
        return pltpu.make_async_remote_copy(
            src_ref=blocks_ref.at[source],
            dst_ref=out_ref.at[source],
            send_sem=send_sem.at[step],
            recv_sem=recv_sem.at[step],
            device_id={axis: source},
            device_id_type=mesh_ids,
        )

    @pl.loop(1, parts)
    def _(step):
        copy_to(step).start()

    out_ref[me] = blocks_ref[me]

    @pl.loop(1, parts)
    def _(step):
        copy_to(step).wait_send()

    @pl.loop(1, parts)
    def _(step):
        copy_from(step).wait_recv()


def swap(blocks, axis, ident):
    parts = blocks.shape[0]
    lanes = 128
    shaped = blocks.reshape(parts, -1, lanes)
    out = pl.pallas_call(
        functools.partial(swap_kernel, axis),
        out_shape=jax.ShapeDtypeStruct(shaped.shape, shaped.dtype),
        in_specs=[pl.BlockSpec(memory_space=pltpu.VMEM)],
        out_specs=pl.BlockSpec(memory_space=pltpu.VMEM),
        scratch_shapes=[pltpu.SemaphoreType.DMA((parts,)), pltpu.SemaphoreType.DMA((parts,))],
        compiler_params=pltpu.CompilerParams(collective_id=ident, has_side_effects=True),
    )(shaped)
    return out.reshape(blocks.shape)


def exchange(blocks, extra, axis, ident):
    width = blocks.shape[1]
    got = swap(jnp.concatenate([blocks, extra], 1), axis, ident)
    return got[:, :width], got[:, width:].sum(0)


def turn_kernel(sent_ref, table_ref, ready_ref, landed_ref, send_sem, recv_sem):
    parts = sent_ref.shape[0]
    depth = sent_ref.shape[1] - 1
    band = ready_ref.shape[1] - 1
    me = lax.axis_index("sy")
    mesh_ids = pl.DeviceIdType.MESH
    barrier = pltpu.get_barrier_semaphore()
    for step in range(1, parts):
        pl.semaphore_signal(
            barrier, 1, device_id={"sy": lax.rem(me + step, parts)}, device_id_type=mesh_ids
        )
    pl.semaphore_wait(barrier, parts - 1)

    def copy_y(step, outgoing):
        peer = lax.rem(me + (step if outgoing else parts - step), parts)
        return pltpu.make_async_remote_copy(
            src_ref=sent_ref.at[peer],
            dst_ref=landed_ref.at[me if outgoing else peer],
            send_sem=send_sem.at[step],
            recv_sem=recv_sem.at[step],
            device_id={"sy": peer},
            device_id_type=mesh_ids,
        )

    @pl.loop(1, parts)
    def _(step):
        copy_y(step, True).start()

    landed_ref[me] = sent_ref[me]

    @pl.loop(1, parts)
    def _(step):
        copy_y(step, True).wait_send()

    @pl.loop(1, parts)
    def _(step):
        copy_y(step, False).wait_recv()

    lanes = ready_ref.shape[2]
    halves = landed_ref.shape[2] // lanes
    rows = band // halves
    block = landed_ref[:, 0:depth, :].reshape(parts * depth, -1)
    share = landed_ref[0, depth : depth + 1, 0:lanes]
    for source in range(1, parts):
        share = share + landed_ref[source, depth : depth + 1, 0:lanes]
    for half in range(halves):
        turned = jnp.dot(
            table_ref[...], block[:, half * lanes : (half + 1) * lanes], precision=HIGHEST,
            preferred_element_type=jnp.float32,
        )
        for peer in range(ready_ref.shape[0]):
            ready_ref[peer, half * rows : (half + 1) * rows, :] = turned[peer * rows : (peer + 1) * rows]
    for peer in range(ready_ref.shape[0]):
        ready_ref[peer, band : band + 1, :] = share


def turn(sent, table, parts_x, band):
    parts_y, rows, width = sent.shape
    vmem = pl.BlockSpec(memory_space=pltpu.VMEM)
    return pl.pallas_call(
        turn_kernel,
        out_shape=jax.ShapeDtypeStruct((parts_x, band * width // 128 + 1, 128), jnp.float32),
        in_specs=[vmem, vmem],
        out_specs=vmem,
        scratch_shapes=[
            pltpu.VMEM((parts_y, rows, width), jnp.float32),
            pltpu.SemaphoreType.DMA((parts_y,)),
            pltpu.SemaphoreType.DMA((parts_y,)),
        ],
        compiler_params=pltpu.CompilerParams(collective_id=0, has_side_effects=True),
    )(sent, table)


def turn_table(length, anchor, rows_y, share_y):
    line = jnp.arange(2 * length, dtype=jnp.int32)
    wave = line[:, None] // 2
    out_part = line[:, None] % 2
    in_part = (line[None, :] // rows_y) % 2
    site = (line[None, :] // (2 * rows_y)) * rows_y + line[None, :] % rows_y
    offset = jnp.mod(site - anchor, length)
    index = jnp.mod(offset * wave + (length // 4) * (out_part - in_part), length)
    return jnp.cos(2.0 * math.pi / length * index.astype(jnp.float32))


def spread_kernel(blocks_ref, out_ref, gathered_ref, total_ref, b_send, b_recv, c_send, c_recv):
    parts_x = blocks_ref.shape[0]
    parts_y = gathered_ref.shape[0]
    depth = blocks_ref.shape[1] - 1
    me_x = lax.axis_index("sx")
    me_y = lax.axis_index("sy")
    mesh_ids = pl.DeviceIdType.MESH
    barrier = pltpu.get_barrier_semaphore()
    for step in range(1, parts_x):
        pl.semaphore_signal(
            barrier, 1, device_id={"sx": lax.rem(me_x + step, parts_x)}, device_id_type=mesh_ids
        )
    for step in range(1, parts_y):
        pl.semaphore_signal(
            barrier, 1, device_id={"sy": lax.rem(me_y + step, parts_y)}, device_id_type=mesh_ids
        )
    pl.semaphore_wait(barrier, parts_x + parts_y - 2)

    def copy_x(step, outgoing):
        peer = lax.rem(me_x + (step if outgoing else parts_x - step), parts_x)
        return pltpu.make_async_remote_copy(
            src_ref=blocks_ref.at[peer],
            dst_ref=out_ref.at[me_x if outgoing else peer],
            send_sem=b_send.at[step],
            recv_sem=b_recv.at[step],
            device_id={"sx": peer},
            device_id_type=mesh_ids,
        )

    def copy_y(step, outgoing):
        peer = lax.rem(me_y + (step if outgoing else parts_y - step), parts_y)
        return pltpu.make_async_remote_copy(
            src_ref=total_ref,
            dst_ref=gathered_ref.at[me_y if outgoing else peer],
            send_sem=c_send.at[step],
            recv_sem=c_recv.at[step],
            device_id={"sy": peer},
            device_id_type=mesh_ids,
        )

    @pl.loop(1, parts_x)
    def _(step):
        copy_x(step, True).start()

    out_ref[me_x] = blocks_ref[me_x]

    @pl.loop(1, parts_x)
    def _(step):
        copy_x(step, True).wait_send()

    @pl.loop(1, parts_x)
    def _(step):
        copy_x(step, False).wait_recv()

    total = out_ref[0, depth : depth + 1, :]
    for source in range(1, parts_x):
        total = total + out_ref[source, depth : depth + 1, :]
    total_ref[...] = total

    @pl.loop(1, parts_y)
    def _(step):
        copy_y(step, True).start()

    gathered_ref[me_y] = total

    @pl.loop(1, parts_y)
    def _(step):
        copy_y(step, True).wait_send()

    @pl.loop(1, parts_y)
    def _(step):
        copy_y(step, False).wait_recv()


def spread_ready(shaped):
    parts_x = shaped.shape[0]
    parts_y = lax.axis_size("sy")
    vmem = pl.BlockSpec(memory_space=pltpu.VMEM)
    got, gathered = pl.pallas_call(
        spread_kernel,
        out_shape=(
            jax.ShapeDtypeStruct(shaped.shape, shaped.dtype),
            jax.ShapeDtypeStruct((parts_y, 1, shaped.shape[2]), shaped.dtype),
        ),
        in_specs=[vmem],
        out_specs=(vmem, vmem),
        scratch_shapes=[
            pltpu.VMEM((1, shaped.shape[2]), jnp.float32),
            pltpu.SemaphoreType.DMA((parts_x,)),
            pltpu.SemaphoreType.DMA((parts_x,)),
            pltpu.SemaphoreType.DMA((parts_y,)),
            pltpu.SemaphoreType.DMA((parts_y,)),
        ],
        compiler_params=pltpu.CompilerParams(collective_id=1, has_side_effects=True),
    )(shaped)
    return got[:, :-1], gathered[:, 0]


def spread(blocks, share, parts_y):
    parts_x = blocks.shape[0]
    lanes = 128
    width = share.size
    rows = jnp.pad(share, (0, lanes - width)) if width < lanes else share
    shaped = blocks.reshape(parts_x, -1, rows.size)
    shaped = jnp.concatenate(
        [shaped, jnp.broadcast_to(rows.reshape(1, 1, -1), (parts_x, 1, rows.size))], 1
    )
    vmem = pl.BlockSpec(memory_space=pltpu.VMEM)
    got, gathered = pl.pallas_call(
        spread_kernel,
        out_shape=(
            jax.ShapeDtypeStruct(shaped.shape, shaped.dtype),
            jax.ShapeDtypeStruct((parts_y, 1, rows.size), shaped.dtype),
        ),
        in_specs=[vmem],
        out_specs=(vmem, vmem),
        scratch_shapes=[
            pltpu.VMEM((1, rows.size), jnp.float32),
            pltpu.SemaphoreType.DMA((parts_x,)),
            pltpu.SemaphoreType.DMA((parts_x,)),
            pltpu.SemaphoreType.DMA((parts_y,)),
            pltpu.SemaphoreType.DMA((parts_y,)),
        ],
        compiler_params=pltpu.CompilerParams(collective_id=1, has_side_effects=True),
    )(shaped)
    return got[:, :-1].reshape(blocks.shape), gathered[:, 0, :width]


def apply_gammas(mat_re, mat_im, real_part, imag_part):
    extent = real_part.shape
    flat_re = real_part.reshape(extent[0], -1)
    flat_im = imag_part.reshape(extent[0], -1)
    out_re = jnp.dot(mat_re, flat_re, precision=HIGHEST) - jnp.dot(
        mat_im, flat_im, precision=HIGHEST
    )
    out_im = jnp.dot(mat_re, flat_im, precision=HIGHEST) + jnp.dot(
        mat_im, flat_re, precision=HIGHEST
    )
    return (out_re.reshape(extent), out_im.reshape(extent))


def project_sites(fields, source_site, momenta, rows_x, rows_y, length, depth):
    coord_x = lax.axis_index("sx") * rows_x + jnp.arange(rows_x, dtype=jnp.int32) - source_site[0]
    coord_y = lax.axis_index("sy") * rows_y + jnp.arange(rows_y, dtype=jnp.int32) - source_site[1]
    coord_z = jnp.arange(depth, dtype=jnp.int32) - source_site[2]
    part_x = jnp.mod(momenta[:, 0:1] * coord_x[None, :], length)
    part_y = jnp.mod(momenta[:, 1:2] * coord_y[None, :], length)
    part_z = jnp.mod(momenta[:, 2:3] * coord_z[None, :], depth)
    plane = jnp.mod(part_x[:, :, None] + part_y[:, None, :], length).astype(jnp.float32)
    angles = (
        2.0 * math.pi / length * plane[:, :, :, None]
        + 2.0 * math.pi / depth * part_z.astype(jnp.float32)[:, None, None, :]
    )
    angles = angles.reshape(momenta.shape[0], -1)
    cosine = jnp.cos(angles)
    sine = jnp.sin(angles)
    field_re = fields[:, 0].reshape(fields.shape[0], -1)
    field_im = fields[:, 1].reshape(fields.shape[0], -1)
    local_re = jnp.dot(field_re, cosine.T, precision=HIGHEST) + jnp.dot(
        field_im, sine.T, precision=HIGHEST
    )
    local_im = jnp.dot(field_im, cosine.T, precision=HIGHEST) - jnp.dot(
        field_re, sine.T, precision=HIGHEST
    )
    return (local_re, local_im)


def contract_kernel(mix_ref, forward_ref, backward_ref, out_ref, pair_ref):
    slices = forward_ref.shape[0]
    rows = forward_ref.shape[3]
    for t in range(slices):
        for u in range(4):
            f_re = [forward_ref[t, 0, 3 * u + c].astype(jnp.float32) for c in range(3)]
            f_im = [forward_ref[t, 1, 3 * u + c].astype(jnp.float32) for c in range(3)]
            for s in range(4):
                acc_re = None
                acc_im = None
                for c in range(3):
                    b_re = backward_ref[t, 0, 3 * s + c].astype(jnp.float32)
                    b_im = backward_ref[t, 1, 3 * s + c].astype(jnp.float32)
                    term_re = b_re * f_re[c] + b_im * f_im[c]
                    term_im = b_re * f_im[c] - b_im * f_re[c]
                    acc_re = term_re if acc_re is None else acc_re + term_re
                    acc_im = term_im if acc_im is None else acc_im + term_im
                base = (s * 4 + u) * 2 * rows
                pair_ref[base : base + rows, :] = acc_re
                pair_ref[base + rows : base + 2 * rows, :] = acc_im
        width = pair_ref.shape[0]
        kinds = mix_ref.shape[1]
        lines = out_ref.shape[1] * kinds
        row = lax.broadcasted_iota(jnp.int32, (lines, width), 0)
        col = lax.broadcasted_iota(jnp.int32, (lines, width), 1)
        pick = jnp.logical_and(row % kinds == col // rows, row // kinds == col % out_ref.shape[1])
        summed = jnp.dot(
            pick.astype(jnp.float32), pair_ref[...], precision=HIGHEST,
            preferred_element_type=jnp.float32,
        )
        for x in range(out_ref.shape[1]):
            out_ref[t, x] = jnp.dot(
                mix_ref[...], summed[x * kinds : (x + 1) * kinds], precision=HIGHEST,
                preferred_element_type=jnp.float32,
            )


def contract(forward_prop, backward_prop, gamma_table):
    slices = forward_prop.shape[0]
    rows_x = forward_prop.shape[4]
    sites = forward_prop.shape[5]
    inserts = gamma_table.shape[0]
    forward = forward_prop.reshape(slices, 2, 12, 12 * rows_x, sites)
    backward = backward_prop.reshape(slices, 2, 12, 12 * rows_x, sites)
    mat_re, mat_im = gamma_matrices(gamma_table)
    mix = jnp.stack([jnp.stack([mat_re, -mat_im], 2), jnp.stack([mat_im, mat_re], 2)], 1)
    mix = mix.reshape(inserts * 2, 16 * 2)
    out = pl.pallas_call(
        contract_kernel,
        out_shape=jax.ShapeDtypeStruct((slices, rows_x, inserts * 2, sites), jnp.float32),
        in_specs=[pl.BlockSpec(memory_space=pltpu.VMEM)] * 3,
        out_specs=pl.BlockSpec(memory_space=pltpu.VMEM),
        scratch_shapes=[pltpu.VMEM((16 * 2 * 12 * rows_x, sites), jnp.float32)],
    )(mix, forward, backward)
    return out.reshape(slices, rows_x, inserts, 2, sites).transpose(2, 0, 3, 1, 4)


def body(forward_prop, backward_prop, gamma_table, source_site, momenta):
    slices = forward_prop.shape[0]
    rows_x = forward_prop.shape[4]
    rows_y = backward_prop.shape[5] // LZ
    inserts = gamma_table.shape[0]
    fields = contract(forward_prop, backward_prop, gamma_table)
    fields = fields.reshape(inserts * slices, 2, rows_x, rows_y, LZ)
    count = fields.shape[0]
    local_re, local_im = project_sites(fields, source_site, momenta, rows_x, rows_y, L, LZ)
    partial = jnp.stack([local_re, local_im], 0)
    groups_y = lax.axis_size("sy")
    groups_x = lax.axis_size("sx")
    tables = dft_matrices(LZ, source_site)
    share_z = LZ // groups_y
    table_z = tables[2].reshape(2, LZ, 2, groups_y, share_z)
    blocks = jnp.einsum("nrxyz,rzsjc->jsynxc", fields, table_z, precision=HIGH)
    blocks = blocks.reshape(groups_y, 2 * rows_y, -1)
    width = blocks.shape[2]
    shares = partial.reshape(groups_y, 1, -1)
    shares = jnp.pad(shares, ((0, 0), (0, 0), (0, width - shares.shape[2])))
    share_y = rows_y * groups_y // groups_x
    table_y = turn_table(rows_y * groups_y, source_site[1], rows_y, share_y)
    ready = turn(jnp.concatenate([blocks, shares], 1), table_y, groups_x, 2 * share_y)
    blocks, gathered = spread_ready(ready)
    blocks = blocks.reshape(groups_x, width // 128, share_y, 2, 128).transpose(0, 2, 3, 1, 4)
    blocks = blocks.reshape(groups_x, share_y, 2, count, rows_x, share_z)
    gathered = gathered[:, : partial.size // groups_y]
    table_x = tables[0].reshape(2, groups_x, rows_x, 2, -1)
    spectrum = jnp.einsum("ibsnxc,sixtk->ntbck", blocks, table_x, precision=HIGH)
    corr = spectrum.reshape(inserts, slices, 2, share_y, -1)
    listed = gathered.reshape(2, inserts, slices, -1)
    return (corr, listed)


def solution(mesh):
    placed = (
        P(None, None, None, None, "sx", "sy"),
        P(None, None, None, None, "sx", "sy"),
        P(),
        P(),
        P(),
    )
    return jax.shard_map(
        body,
        mesh=mesh,
        in_specs=placed,
        out_specs=(P(None, None, None, "sx", "sy"), P()),
        check_vma=False,
    )
```

```python
import functools
import math

import jax
import jax.numpy as jnp
from jax import lax
from jax.experimental import pallas as pl
from jax.experimental.pallas import tpu as pltpu
from jax.sharding import PartitionSpec as P

L = 64
LZ = 64


HIGHEST = lax.Precision.HIGHEST
HIGH = lax.Precision.HIGH


def gamma_matrices(gamma_table):
    inserts = gamma_table.shape[0]
    columns = gamma_table[:, :, 0]
    powers = gamma_table[:, :, 1]
    spin_ids = jnp.arange(4, dtype=jnp.int32)
    matches = (columns[:, :, None] == spin_ids[None, None, :]).astype(jnp.float32)
    unit_re = (powers == 0).astype(jnp.float32) - (powers == 2).astype(jnp.float32)
    unit_im = (powers == 1).astype(jnp.float32) - (powers == 3).astype(jnp.float32)
    return (
        (matches * unit_re[:, :, None]).reshape(inserts, 16),
        (matches * unit_im[:, :, None]).reshape(inserts, 16),
    )


def dft_table(length, anchor):
    wavenum = jnp.arange(length, dtype=jnp.int32)
    offsets = jnp.mod(wavenum - anchor, length)
    phase_index = jnp.mod(offsets[:, None] * wavenum[None, :], length)
    angles = 2.0 * math.pi / length * phase_index.astype(jnp.float32)
    return (jnp.cos(angles), -jnp.sin(angles))


def dft_matrices(length, anchors):
    wavenum = jnp.arange(length, dtype=jnp.int32)
    offsets = jnp.mod(wavenum[None, :] - anchors[:, None], length)
    phase_index = jnp.mod(offsets[:, :, None] * wavenum[None, None, :], length)
    angles = 2.0 * math.pi / length * phase_index.astype(jnp.float32)
    table_re = jnp.cos(angles)
    table_im = -jnp.sin(angles)
    rows_re = jnp.stack([table_re, table_im], 2)
    rows_im = jnp.stack([-table_im, table_re], 2)
    return jnp.stack([rows_re, rows_im], 1)


def swap_kernel(axis, blocks_ref, out_ref, send_sem, recv_sem):
    parts = blocks_ref.shape[0]
    me = lax.axis_index(axis)
    mesh_ids = pl.DeviceIdType.MESH
    barrier = pltpu.get_barrier_semaphore()
    for step in range(1, parts):
        pl.semaphore_signal(
            barrier, 1, device_id={axis: lax.rem(me + step, parts)}, device_id_type=mesh_ids
        )
    pl.semaphore_wait(barrier, parts - 1)

    def copy_to(step):
        peer = lax.rem(me + step, parts)
        return pltpu.make_async_remote_copy(
            src_ref=blocks_ref.at[peer],
            dst_ref=out_ref.at[me],
            send_sem=send_sem.at[step],
            recv_sem=recv_sem.at[step],
            device_id={axis: peer},
            device_id_type=mesh_ids,
        )

    def copy_from(step):
        source = lax.rem(me + parts - step, parts)
        return pltpu.make_async_remote_copy(
            src_ref=blocks_ref.at[source],
            dst_ref=out_ref.at[source],
            send_sem=send_sem.at[step],
            recv_sem=recv_sem.at[step],
            device_id={axis: source},
            device_id_type=mesh_ids,
        )

    @pl.loop(1, parts)
    def _(step):
        copy_to(step).start()

    out_ref[me] = blocks_ref[me]

    @pl.loop(1, parts)
    def _(step):
        copy_to(step).wait_send()

    @pl.loop(1, parts)
    def _(step):
        copy_from(step).wait_recv()


def swap(blocks, axis, ident):
    parts = blocks.shape[0]
    lanes = 128
    shaped = blocks.reshape(parts, -1, lanes)
    out = pl.pallas_call(
        functools.partial(swap_kernel, axis),
        out_shape=jax.ShapeDtypeStruct(shaped.shape, shaped.dtype),
        in_specs=[pl.BlockSpec(memory_space=pltpu.VMEM)],
        out_specs=pl.BlockSpec(memory_space=pltpu.VMEM),
        scratch_shapes=[pltpu.SemaphoreType.DMA((parts,)), pltpu.SemaphoreType.DMA((parts,))],
        compiler_params=pltpu.CompilerParams(collective_id=ident, has_side_effects=True),
    )(shaped)
    return out.reshape(blocks.shape)


def exchange(blocks, extra, axis, ident):
    width = blocks.shape[1]
    got = swap(jnp.concatenate([blocks, extra], 1), axis, ident)
    return got[:, :width], got[:, width:].sum(0)


def turn_kernel(anchor_ref, sent_ref, ready_ref, landed_ref, table_ref, send_sem, recv_sem):
    parts = sent_ref.shape[0]
    depth = sent_ref.shape[1] - 1
    band = ready_ref.shape[1] - 1
    me = lax.axis_index("sy")
    mesh_ids = pl.DeviceIdType.MESH
    barrier = pltpu.get_barrier_semaphore()
    for step in range(1, parts):
        pl.semaphore_signal(
            barrier, 1, device_id={"sy": lax.rem(me + step, parts)}, device_id_type=mesh_ids
        )
    table_ref[...] = turn_table(
        parts * depth // 2, anchor_ref[0], depth // 2, ready_ref.shape[1] // 2, table_ref.shape
    )
    pl.semaphore_wait(barrier, parts - 1)

    def copy_y(step, outgoing):
        peer = lax.rem(me + (step if outgoing else parts - step), parts)
        return pltpu.make_async_remote_copy(
            src_ref=sent_ref.at[peer],
            dst_ref=landed_ref.at[me if outgoing else peer],
            send_sem=send_sem.at[step],
            recv_sem=recv_sem.at[step],
            device_id={"sy": peer},
            device_id_type=mesh_ids,
        )

    @pl.loop(1, parts)
    def _(step):
        copy_y(step, True).start()

    landed_ref[me] = sent_ref[me]

    @pl.loop(1, parts)
    def _(step):
        copy_y(step, True).wait_send()

    @pl.loop(1, parts)
    def _(step):
        copy_y(step, False).wait_recv()

    lanes = ready_ref.shape[2]
    halves = landed_ref.shape[2] // lanes
    rows = band // halves
    block = landed_ref[:, 0:depth, :].reshape(parts * depth, -1)
    share = landed_ref[0, depth : depth + 1, 0:lanes]
    for source in range(1, parts):
        share = share + landed_ref[source, depth : depth + 1, 0:lanes]
    for half in range(halves):
        turned = jnp.dot(
            table_ref[...], block[:, half * lanes : (half + 1) * lanes], precision=HIGHEST,
            preferred_element_type=jnp.float32,
        )
        for peer in range(ready_ref.shape[0]):
            ready_ref[peer, half * rows : (half + 1) * rows, :] = turned[peer * rows : (peer + 1) * rows]
    for peer in range(ready_ref.shape[0]):
        ready_ref[peer, band : band + 1, :] = share


def turn(sent, anchor, parts_x, band):
    parts_y, rows, width = sent.shape
    vmem = pl.BlockSpec(memory_space=pltpu.VMEM)
    return pl.pallas_call(
        turn_kernel,
        out_shape=jax.ShapeDtypeStruct((parts_x, band * width // 128 + 1, 128), jnp.float32),
        in_specs=[pl.BlockSpec(memory_space=pltpu.SMEM), vmem],
        out_specs=vmem,
        scratch_shapes=[
            pltpu.VMEM((parts_y, rows, width), jnp.float32),
            pltpu.VMEM((parts_y * (rows - 1), parts_y * (rows - 1)), jnp.float32),
            pltpu.SemaphoreType.DMA((parts_y,)),
            pltpu.SemaphoreType.DMA((parts_y,)),
        ],
        compiler_params=pltpu.CompilerParams(collective_id=0, has_side_effects=True),
    )(anchor, sent)


def turn_table(length, anchor, rows_y, share_y, shape):
    line = lax.broadcasted_iota(jnp.int32, shape, 0)
    column = lax.broadcasted_iota(jnp.int32, shape, 1)
    wave = line // 2
    out_part = line % 2
    in_part = (column // rows_y) % 2
    site = (column // (2 * rows_y)) * rows_y + column % rows_y
    offset = (site - anchor + length) % length
    index = (offset * wave + (length // 4) * (out_part - in_part) + length) % length
    return jnp.cos((2.0 * math.pi / length) * index.astype(jnp.float32))


def spread_kernel(blocks_ref, out_ref, gathered_ref, total_ref, b_send, b_recv, c_send, c_recv):
    parts_x = blocks_ref.shape[0]
    parts_y = gathered_ref.shape[0]
    depth = blocks_ref.shape[1] - 1
    me_x = lax.axis_index("sx")
    me_y = lax.axis_index("sy")
    mesh_ids = pl.DeviceIdType.MESH
    barrier = pltpu.get_barrier_semaphore()
    for step in range(1, parts_x):
        pl.semaphore_signal(
            barrier, 1, device_id={"sx": lax.rem(me_x + step, parts_x)}, device_id_type=mesh_ids
        )
    for step in range(1, parts_y):
        pl.semaphore_signal(
            barrier, 1, device_id={"sy": lax.rem(me_y + step, parts_y)}, device_id_type=mesh_ids
        )
    pl.semaphore_wait(barrier, parts_x + parts_y - 2)

    def copy_x(step, outgoing):
        peer = lax.rem(me_x + (step if outgoing else parts_x - step), parts_x)
        return pltpu.make_async_remote_copy(
            src_ref=blocks_ref.at[peer],
            dst_ref=out_ref.at[me_x if outgoing else peer],
            send_sem=b_send.at[step],
            recv_sem=b_recv.at[step],
            device_id={"sx": peer},
            device_id_type=mesh_ids,
        )

    def copy_y(step, outgoing):
        peer = lax.rem(me_y + (step if outgoing else parts_y - step), parts_y)
        return pltpu.make_async_remote_copy(
            src_ref=total_ref,
            dst_ref=gathered_ref.at[me_y if outgoing else peer],
            send_sem=c_send.at[step],
            recv_sem=c_recv.at[step],
            device_id={"sy": peer},
            device_id_type=mesh_ids,
        )

    @pl.loop(1, parts_x)
    def _(step):
        copy_x(step, True).start()

    out_ref[me_x] = blocks_ref[me_x]

    @pl.loop(1, parts_x)
    def _(step):
        copy_x(step, True).wait_send()

    @pl.loop(1, parts_x)
    def _(step):
        copy_x(step, False).wait_recv()

    total = out_ref[0, depth : depth + 1, :]
    for source in range(1, parts_x):
        total = total + out_ref[source, depth : depth + 1, :]
    total_ref[...] = total

    @pl.loop(1, parts_y)
    def _(step):
        copy_y(step, True).start()

    gathered_ref[me_y] = total

    @pl.loop(1, parts_y)
    def _(step):
        copy_y(step, True).wait_send()

    @pl.loop(1, parts_y)
    def _(step):
        copy_y(step, False).wait_recv()


def spread_ready(shaped):
    parts_x = shaped.shape[0]
    parts_y = lax.axis_size("sy")
    vmem = pl.BlockSpec(memory_space=pltpu.VMEM)
    got, gathered = pl.pallas_call(
        spread_kernel,
        out_shape=(
            jax.ShapeDtypeStruct(shaped.shape, shaped.dtype),
            jax.ShapeDtypeStruct((parts_y, 1, shaped.shape[2]), shaped.dtype),
        ),
        in_specs=[vmem],
        out_specs=(vmem, vmem),
        scratch_shapes=[
            pltpu.VMEM((1, shaped.shape[2]), jnp.float32),
            pltpu.SemaphoreType.DMA((parts_x,)),
            pltpu.SemaphoreType.DMA((parts_x,)),
            pltpu.SemaphoreType.DMA((parts_y,)),
            pltpu.SemaphoreType.DMA((parts_y,)),
        ],
        compiler_params=pltpu.CompilerParams(collective_id=1, has_side_effects=True),
    )(shaped)
    return got[:, :-1], gathered[:, 0]


def spread(blocks, share, parts_y):
    parts_x = blocks.shape[0]
    lanes = 128
    width = share.size
    rows = jnp.pad(share, (0, lanes - width)) if width < lanes else share
    shaped = blocks.reshape(parts_x, -1, rows.size)
    shaped = jnp.concatenate(
        [shaped, jnp.broadcast_to(rows.reshape(1, 1, -1), (parts_x, 1, rows.size))], 1
    )
    vmem = pl.BlockSpec(memory_space=pltpu.VMEM)
    got, gathered = pl.pallas_call(
        spread_kernel,
        out_shape=(
            jax.ShapeDtypeStruct(shaped.shape, shaped.dtype),
            jax.ShapeDtypeStruct((parts_y, 1, rows.size), shaped.dtype),
        ),
        in_specs=[vmem],
        out_specs=(vmem, vmem),
        scratch_shapes=[
            pltpu.VMEM((1, rows.size), jnp.float32),
            pltpu.SemaphoreType.DMA((parts_x,)),
            pltpu.SemaphoreType.DMA((parts_x,)),
            pltpu.SemaphoreType.DMA((parts_y,)),
            pltpu.SemaphoreType.DMA((parts_y,)),
        ],
        compiler_params=pltpu.CompilerParams(collective_id=1, has_side_effects=True),
    )(shaped)
    return got[:, :-1].reshape(blocks.shape), gathered[:, 0, :width]


def apply_gammas(mat_re, mat_im, real_part, imag_part):
    extent = real_part.shape
    flat_re = real_part.reshape(extent[0], -1)
    flat_im = imag_part.reshape(extent[0], -1)
    out_re = jnp.dot(mat_re, flat_re, precision=HIGHEST) - jnp.dot(
        mat_im, flat_im, precision=HIGHEST
    )
    out_im = jnp.dot(mat_re, flat_im, precision=HIGHEST) + jnp.dot(
        mat_im, flat_re, precision=HIGHEST
    )
    return (out_re.reshape(extent), out_im.reshape(extent))


def project_sites(fields, source_site, momenta, rows_x, rows_y, length, depth):
    coord_x = lax.axis_index("sx") * rows_x + jnp.arange(rows_x, dtype=jnp.int32) - source_site[0]
    coord_y = lax.axis_index("sy") * rows_y + jnp.arange(rows_y, dtype=jnp.int32) - source_site[1]
    coord_z = jnp.arange(depth, dtype=jnp.int32) - source_site[2]
    part_x = jnp.mod(momenta[:, 0:1] * coord_x[None, :], length)
    part_y = jnp.mod(momenta[:, 1:2] * coord_y[None, :], length)
    part_z = jnp.mod(momenta[:, 2:3] * coord_z[None, :], depth)
    plane = jnp.mod(part_x[:, :, None] + part_y[:, None, :], length).astype(jnp.float32)
    angles = (
        2.0 * math.pi / length * plane[:, :, :, None]
        + 2.0 * math.pi / depth * part_z.astype(jnp.float32)[:, None, None, :]
    )
    angles = angles.reshape(momenta.shape[0], -1)
    cosine = jnp.cos(angles)
    sine = jnp.sin(angles)
    field_re = fields[:, 0].reshape(fields.shape[0], -1)
    field_im = fields[:, 1].reshape(fields.shape[0], -1)
    local_re = jnp.dot(field_re, cosine.T, precision=HIGHEST) + jnp.dot(
        field_im, sine.T, precision=HIGHEST
    )
    local_im = jnp.dot(field_im, cosine.T, precision=HIGHEST) - jnp.dot(
        field_re, sine.T, precision=HIGHEST
    )
    return (local_re, local_im)


def contract_kernel(mix_ref, forward_ref, backward_ref, out_ref, pair_ref):
    slices = forward_ref.shape[0]
    rows = forward_ref.shape[3]
    for t in range(slices):
        for u in range(4):
            f_re = [forward_ref[t, 0, 3 * u + c].astype(jnp.float32) for c in range(3)]
            f_im = [forward_ref[t, 1, 3 * u + c].astype(jnp.float32) for c in range(3)]
            for s in range(4):
                acc_re = None
                acc_im = None
                for c in range(3):
                    b_re = backward_ref[t, 0, 3 * s + c].astype(jnp.float32)
                    b_im = backward_ref[t, 1, 3 * s + c].astype(jnp.float32)
                    term_re = b_re * f_re[c] + b_im * f_im[c]
                    term_im = b_re * f_im[c] - b_im * f_re[c]
                    acc_re = term_re if acc_re is None else acc_re + term_re
                    acc_im = term_im if acc_im is None else acc_im + term_im
                base = (s * 4 + u) * 2 * rows
                pair_ref[base : base + rows, :] = acc_re
                pair_ref[base + rows : base + 2 * rows, :] = acc_im
        width = pair_ref.shape[0]
        kinds = mix_ref.shape[1]
        lines = out_ref.shape[1] * kinds
        row = lax.broadcasted_iota(jnp.int32, (lines, width), 0)
        col = lax.broadcasted_iota(jnp.int32, (lines, width), 1)
        pick = jnp.logical_and(row % kinds == col // rows, row // kinds == col % out_ref.shape[1])
        summed = jnp.dot(
            pick.astype(jnp.float32), pair_ref[...], precision=HIGHEST,
            preferred_element_type=jnp.float32,
        )
        for x in range(out_ref.shape[1]):
            out_ref[t, x] = jnp.dot(
                mix_ref[...], summed[x * kinds : (x + 1) * kinds], precision=HIGHEST,
                preferred_element_type=jnp.float32,
            )


def contract(forward_prop, backward_prop, gamma_table):
    slices = forward_prop.shape[0]
    rows_x = forward_prop.shape[4]
    sites = forward_prop.shape[5]
    inserts = gamma_table.shape[0]
    forward = forward_prop.reshape(slices, 2, 12, 12 * rows_x, sites)
    backward = backward_prop.reshape(slices, 2, 12, 12 * rows_x, sites)
    mat_re, mat_im = gamma_matrices(gamma_table)
    mix = jnp.stack([jnp.stack([mat_re, -mat_im], 2), jnp.stack([mat_im, mat_re], 2)], 1)
    mix = mix.reshape(inserts * 2, 16 * 2)
    out = pl.pallas_call(
        contract_kernel,
        out_shape=jax.ShapeDtypeStruct((slices, rows_x, inserts * 2, sites), jnp.float32),
        in_specs=[pl.BlockSpec(memory_space=pltpu.VMEM)] * 3,
        out_specs=pl.BlockSpec(memory_space=pltpu.VMEM),
        scratch_shapes=[pltpu.VMEM((16 * 2 * 12 * rows_x, sites), jnp.float32)],
    )(mix, forward, backward)
    return out.reshape(slices, rows_x, inserts, 2, sites).transpose(2, 0, 3, 1, 4)


def body(forward_prop, backward_prop, gamma_table, source_site, momenta):
    slices = forward_prop.shape[0]
    rows_x = forward_prop.shape[4]
    rows_y = backward_prop.shape[5] // LZ
    inserts = gamma_table.shape[0]
    fields = contract(forward_prop, backward_prop, gamma_table)
    fields = fields.reshape(inserts * slices, 2, rows_x, rows_y, LZ)
    count = fields.shape[0]
    local_re, local_im = project_sites(fields, source_site, momenta, rows_x, rows_y, L, LZ)
    partial = jnp.stack([local_re, local_im], 0)
    groups_y = lax.axis_size("sy")
    groups_x = lax.axis_size("sx")
    tables = dft_matrices(LZ, source_site)
    share_z = LZ // groups_y
    table_z = tables[2].reshape(2, LZ, 2, groups_y, share_z)
    blocks = jnp.einsum("nrxyz,rzsjc->jsynxc", fields, table_z, precision=HIGH)
    blocks = blocks.reshape(groups_y, 2 * rows_y, -1)
    width = blocks.shape[2]
    shares = partial.reshape(groups_y, 1, -1)
    shares = jnp.pad(shares, ((0, 0), (0, 0), (0, width - shares.shape[2])))
    share_y = rows_y * groups_y // groups_x
    ready = turn(jnp.concatenate([blocks, shares], 1), source_site[1:2], groups_x, 2 * share_y)
    blocks, gathered = spread_ready(ready)
    blocks = blocks.reshape(groups_x, width // 128, share_y, 2, 128).transpose(0, 2, 3, 1, 4)
    blocks = blocks.reshape(groups_x, share_y, 2, count, rows_x, share_z)
    gathered = gathered[:, : partial.size // groups_y]
    table_x = tables[0].reshape(2, groups_x, rows_x, 2, -1)
    spectrum = jnp.einsum("ibsnxc,sixtk->ntbck", blocks, table_x, precision=HIGH)
    corr = spectrum.reshape(inserts, slices, 2, share_y, -1)
    listed = gathered.reshape(2, inserts, slices, -1)
    return (corr, listed)


def solution(mesh):
    placed = (
        P(None, None, None, None, "sx", "sy"),
        P(None, None, None, None, "sx", "sy"),
        P(),
        P(),
        P(),
    )
    return jax.shard_map(
        body,
        mesh=mesh,
        in_specs=placed,
        out_specs=(P(None, None, None, "sx", "sy"), P()),
        check_vma=False,
    )
```

```python
import functools
import math

import jax
import jax.numpy as jnp
from jax import lax
from jax.experimental import pallas as pl
from jax.experimental.pallas import tpu as pltpu
from jax.sharding import PartitionSpec as P

L = 64
LZ = 64


HIGHEST = lax.Precision.HIGHEST
HIGH = lax.Precision.HIGH


def gamma_matrices(gamma_table):
    inserts = gamma_table.shape[0]
    columns = gamma_table[:, :, 0]
    powers = gamma_table[:, :, 1]
    spin_ids = jnp.arange(4, dtype=jnp.int32)
    matches = (columns[:, :, None] == spin_ids[None, None, :]).astype(jnp.float32)
    unit_re = (powers == 0).astype(jnp.float32) - (powers == 2).astype(jnp.float32)
    unit_im = (powers == 1).astype(jnp.float32) - (powers == 3).astype(jnp.float32)
    return (
        (matches * unit_re[:, :, None]).reshape(inserts, 16),
        (matches * unit_im[:, :, None]).reshape(inserts, 16),
    )


def dft_table(length, anchor):
    wavenum = jnp.arange(length, dtype=jnp.int32)
    offsets = jnp.mod(wavenum - anchor, length)
    phase_index = jnp.mod(offsets[:, None] * wavenum[None, :], length)
    angles = 2.0 * math.pi / length * phase_index.astype(jnp.float32)
    return (jnp.cos(angles), -jnp.sin(angles))


def dft_matrices(length, anchors):
    wavenum = jnp.arange(length, dtype=jnp.int32)
    offsets = jnp.mod(wavenum[None, :] - anchors[:, None], length)
    phase_index = jnp.mod(offsets[:, :, None] * wavenum[None, None, :], length)
    angles = 2.0 * math.pi / length * phase_index.astype(jnp.float32)
    table_re = jnp.cos(angles)
    table_im = -jnp.sin(angles)
    rows_re = jnp.stack([table_re, table_im], 2)
    rows_im = jnp.stack([-table_im, table_re], 2)
    return jnp.stack([rows_re, rows_im], 1)


def swap_kernel(axis, blocks_ref, out_ref, send_sem, recv_sem):
    parts = blocks_ref.shape[0]
    me = lax.axis_index(axis)
    mesh_ids = pl.DeviceIdType.MESH
    barrier = pltpu.get_barrier_semaphore()
    for step in range(1, parts):
        pl.semaphore_signal(
            barrier, 1, device_id={axis: lax.rem(me + step, parts)}, device_id_type=mesh_ids
        )
    pl.semaphore_wait(barrier, parts - 1)

    def copy_to(step):
        peer = lax.rem(me + step, parts)
        return pltpu.make_async_remote_copy(
            src_ref=blocks_ref.at[peer],
            dst_ref=out_ref.at[me],
            send_sem=send_sem.at[step],
            recv_sem=recv_sem.at[step],
            device_id={axis: peer},
            device_id_type=mesh_ids,
        )

    def copy_from(step):
        source = lax.rem(me + parts - step, parts)
        return pltpu.make_async_remote_copy(
            src_ref=blocks_ref.at[source],
            dst_ref=out_ref.at[source],
            send_sem=send_sem.at[step],
            recv_sem=recv_sem.at[step],
            device_id={axis: source},
            device_id_type=mesh_ids,
        )

    @pl.loop(1, parts)
    def _(step):
        copy_to(step).start()

    out_ref[me] = blocks_ref[me]

    @pl.loop(1, parts)
    def _(step):
        copy_to(step).wait_send()

    @pl.loop(1, parts)
    def _(step):
        copy_from(step).wait_recv()


def swap(blocks, axis, ident):
    parts = blocks.shape[0]
    lanes = 128
    shaped = blocks.reshape(parts, -1, lanes)
    out = pl.pallas_call(
        functools.partial(swap_kernel, axis),
        out_shape=jax.ShapeDtypeStruct(shaped.shape, shaped.dtype),
        in_specs=[pl.BlockSpec(memory_space=pltpu.VMEM)],
        out_specs=pl.BlockSpec(memory_space=pltpu.VMEM),
        scratch_shapes=[pltpu.SemaphoreType.DMA((parts,)), pltpu.SemaphoreType.DMA((parts,))],
        compiler_params=pltpu.CompilerParams(collective_id=ident, has_side_effects=True),
    )(shaped)
    return out.reshape(blocks.shape)


def exchange(blocks, extra, axis, ident):
    width = blocks.shape[1]
    got = swap(jnp.concatenate([blocks, extra], 1), axis, ident)
    return got[:, :width], got[:, width:].sum(0)


def turn_kernel(anchor_ref, sent_ref, ready_ref, landed_ref, table_ref, send_sem, recv_sem):
    parts = sent_ref.shape[0]
    depth = sent_ref.shape[1] - 1
    band = ready_ref.shape[1] - 1
    me = lax.axis_index("sy")
    mesh_ids = pl.DeviceIdType.MESH
    barrier = pltpu.get_barrier_semaphore()
    for step in range(1, parts):
        pl.semaphore_signal(
            barrier, 1, device_id={"sy": lax.rem(me + step, parts)}, device_id_type=mesh_ids
        )
    table_ref[...] = turn_table(
        parts * depth // 2, anchor_ref[0], depth // 2, ready_ref.shape[1] // 2, table_ref.shape
    )
    pl.semaphore_wait(barrier, parts - 1)

    def copy_y(step, outgoing):
        peer = lax.rem(me + (step if outgoing else parts - step), parts)
        return pltpu.make_async_remote_copy(
            src_ref=sent_ref.at[peer],
            dst_ref=landed_ref.at[me if outgoing else peer],
            send_sem=send_sem.at[step],
            recv_sem=recv_sem.at[step],
            device_id={"sy": peer},
            device_id_type=mesh_ids,
        )

    @pl.loop(1, parts)
    def _(step):
        copy_y(step, True).start()

    landed_ref[me] = sent_ref[me]

    @pl.loop(1, parts)
    def _(step):
        copy_y(step, True).wait_send()

    @pl.loop(1, parts)
    def _(step):
        copy_y(step, False).wait_recv()

    lanes = ready_ref.shape[2]
    halves = landed_ref.shape[2] // lanes
    rows = band // halves
    block = landed_ref[:, 0:depth, :].reshape(parts * depth, -1)
    share = landed_ref[0, depth : depth + 1, 0:lanes]
    for source in range(1, parts):
        share = share + landed_ref[source, depth : depth + 1, 0:lanes]
    for half in range(halves):
        turned = jnp.dot(
            table_ref[...], block[:, half * lanes : (half + 1) * lanes], precision=HIGHEST,
            preferred_element_type=jnp.float32,
        )
        for peer in range(ready_ref.shape[0]):
            ready_ref[peer, half * rows : (half + 1) * rows, :] = turned[peer * rows : (peer + 1) * rows]
    for peer in range(ready_ref.shape[0]):
        ready_ref[peer, band : band + 1, :] = share


def turn(sent, anchor, parts_x, band):
    parts_y, rows, width = sent.shape
    vmem = pl.BlockSpec(memory_space=pltpu.VMEM)
    return pl.pallas_call(
        turn_kernel,
        out_shape=jax.ShapeDtypeStruct((parts_x, band * width // 128 + 1, 128), jnp.float32),
        in_specs=[pl.BlockSpec(memory_space=pltpu.SMEM), vmem],
        out_specs=vmem,
        scratch_shapes=[
            pltpu.VMEM((parts_y, rows, width), jnp.float32),
            pltpu.VMEM((parts_y * (rows - 1), parts_y * (rows - 1)), jnp.float32),
            pltpu.SemaphoreType.DMA((parts_y,)),
            pltpu.SemaphoreType.DMA((parts_y,)),
        ],
        compiler_params=pltpu.CompilerParams(collective_id=0, has_side_effects=True),
    )(anchor, sent)


def turn_table(length, anchor, rows_y, share_y, shape):
    line = lax.broadcasted_iota(jnp.int32, shape, 0)
    column = lax.broadcasted_iota(jnp.int32, shape, 1)
    wave = line // 2
    out_part = line % 2
    in_part = (column // rows_y) % 2
    site = (column // (2 * rows_y)) * rows_y + column % rows_y
    offset = (site - anchor + length) % length
    index = (offset * wave + (length // 4) * (out_part - in_part) + length) % length
    return jnp.cos((2.0 * math.pi / length) * index.astype(jnp.float32))


def spread_kernel(blocks_ref, out_ref, gathered_ref, total_ref, b_send, b_recv, c_send, c_recv):
    parts_x = blocks_ref.shape[0]
    parts_y = gathered_ref.shape[0]
    depth = blocks_ref.shape[1] - 1
    me_x = lax.axis_index("sx")
    me_y = lax.axis_index("sy")
    mesh_ids = pl.DeviceIdType.MESH
    barrier = pltpu.get_barrier_semaphore()
    for step in range(1, parts_x):
        pl.semaphore_signal(
            barrier, 1, device_id={"sx": lax.rem(me_x + step, parts_x)}, device_id_type=mesh_ids
        )
    for step in range(1, parts_y):
        pl.semaphore_signal(
            barrier, 1, device_id={"sy": lax.rem(me_y + step, parts_y)}, device_id_type=mesh_ids
        )
    pl.semaphore_wait(barrier, parts_x + parts_y - 2)

    def copy_x(step, outgoing):
        peer = lax.rem(me_x + (step if outgoing else parts_x - step), parts_x)
        return pltpu.make_async_remote_copy(
            src_ref=blocks_ref.at[peer],
            dst_ref=out_ref.at[me_x if outgoing else peer],
            send_sem=b_send.at[step],
            recv_sem=b_recv.at[step],
            device_id={"sx": peer},
            device_id_type=mesh_ids,
        )

    def copy_y(step, outgoing):
        peer = lax.rem(me_y + (step if outgoing else parts_y - step), parts_y)
        return pltpu.make_async_remote_copy(
            src_ref=total_ref,
            dst_ref=gathered_ref.at[me_y if outgoing else peer],
            send_sem=c_send.at[step],
            recv_sem=c_recv.at[step],
            device_id={"sy": peer},
            device_id_type=mesh_ids,
        )

    @pl.loop(1, parts_x)
    def _(step):
        copy_x(step, True).start()

    out_ref[me_x] = blocks_ref[me_x]

    @pl.loop(1, parts_x)
    def _(step):
        copy_x(step, True).wait_send()

    @pl.loop(1, parts_x)
    def _(step):
        copy_x(step, False).wait_recv()

    total = out_ref[0, depth : depth + 1, :]
    for source in range(1, parts_x):
        total = total + out_ref[source, depth : depth + 1, :]
    total_ref[...] = total

    @pl.loop(1, parts_y)
    def _(step):
        copy_y(step, True).start()

    gathered_ref[me_y] = total

    @pl.loop(1, parts_y)
    def _(step):
        copy_y(step, True).wait_send()

    @pl.loop(1, parts_y)
    def _(step):
        copy_y(step, False).wait_recv()


def spread_ready(shaped):
    parts_x = shaped.shape[0]
    parts_y = lax.axis_size("sy")
    vmem = pl.BlockSpec(memory_space=pltpu.VMEM)
    got, gathered = pl.pallas_call(
        spread_kernel,
        out_shape=(
            jax.ShapeDtypeStruct(shaped.shape, shaped.dtype),
            jax.ShapeDtypeStruct((parts_y, 1, shaped.shape[2]), shaped.dtype),
        ),
        in_specs=[vmem],
        out_specs=(vmem, vmem),
        scratch_shapes=[
            pltpu.VMEM((1, shaped.shape[2]), jnp.float32),
            pltpu.SemaphoreType.DMA((parts_x,)),
            pltpu.SemaphoreType.DMA((parts_x,)),
            pltpu.SemaphoreType.DMA((parts_y,)),
            pltpu.SemaphoreType.DMA((parts_y,)),
        ],
        compiler_params=pltpu.CompilerParams(collective_id=1, has_side_effects=True),
    )(shaped)
    return got[:, :-1], gathered[:, 0]


def spread(blocks, share, parts_y):
    parts_x = blocks.shape[0]
    lanes = 128
    width = share.size
    rows = jnp.pad(share, (0, lanes - width)) if width < lanes else share
    shaped = blocks.reshape(parts_x, -1, rows.size)
    shaped = jnp.concatenate(
        [shaped, jnp.broadcast_to(rows.reshape(1, 1, -1), (parts_x, 1, rows.size))], 1
    )
    vmem = pl.BlockSpec(memory_space=pltpu.VMEM)
    got, gathered = pl.pallas_call(
        spread_kernel,
        out_shape=(
            jax.ShapeDtypeStruct(shaped.shape, shaped.dtype),
            jax.ShapeDtypeStruct((parts_y, 1, rows.size), shaped.dtype),
        ),
        in_specs=[vmem],
        out_specs=(vmem, vmem),
        scratch_shapes=[
            pltpu.VMEM((1, rows.size), jnp.float32),
            pltpu.SemaphoreType.DMA((parts_x,)),
            pltpu.SemaphoreType.DMA((parts_x,)),
            pltpu.SemaphoreType.DMA((parts_y,)),
            pltpu.SemaphoreType.DMA((parts_y,)),
        ],
        compiler_params=pltpu.CompilerParams(collective_id=1, has_side_effects=True),
    )(shaped)
    return got[:, :-1].reshape(blocks.shape), gathered[:, 0, :width]


def apply_gammas(mat_re, mat_im, real_part, imag_part):
    extent = real_part.shape
    flat_re = real_part.reshape(extent[0], -1)
    flat_im = imag_part.reshape(extent[0], -1)
    out_re = jnp.dot(mat_re, flat_re, precision=HIGHEST) - jnp.dot(
        mat_im, flat_im, precision=HIGHEST
    )
    out_im = jnp.dot(mat_re, flat_im, precision=HIGHEST) + jnp.dot(
        mat_im, flat_re, precision=HIGHEST
    )
    return (out_re.reshape(extent), out_im.reshape(extent))


def project_sites(fields, source_site, momenta, rows_x, rows_y, length, depth):
    coord_x = lax.axis_index("sx") * rows_x + jnp.arange(rows_x, dtype=jnp.int32) - source_site[0]
    coord_y = lax.axis_index("sy") * rows_y + jnp.arange(rows_y, dtype=jnp.int32) - source_site[1]
    coord_z = jnp.arange(depth, dtype=jnp.int32) - source_site[2]
    part_x = jnp.mod(momenta[:, 0:1] * coord_x[None, :], length)
    part_y = jnp.mod(momenta[:, 1:2] * coord_y[None, :], length)
    part_z = jnp.mod(momenta[:, 2:3] * coord_z[None, :], depth)
    plane = jnp.mod(part_x[:, :, None] + part_y[:, None, :], length).astype(jnp.float32)
    angles = (
        2.0 * math.pi / length * plane[:, :, :, None]
        + 2.0 * math.pi / depth * part_z.astype(jnp.float32)[:, None, None, :]
    )
    angles = angles.reshape(momenta.shape[0], -1)
    cosine = jnp.cos(angles)
    sine = jnp.sin(angles)
    field_re = fields[:, 0].reshape(fields.shape[0], -1)
    field_im = fields[:, 1].reshape(fields.shape[0], -1)
    local_re = jnp.dot(field_re, cosine.T, precision=HIGHEST) + jnp.dot(
        field_im, sine.T, precision=HIGHEST
    )
    local_im = jnp.dot(field_im, cosine.T, precision=HIGHEST) - jnp.dot(
        field_re, sine.T, precision=HIGHEST
    )
    return (local_re, local_im)


def gamma_mix(table_ref, inserts):
    shape = (inserts * 2, 32)
    line = lax.broadcasted_iota(jnp.int32, shape, 0)
    column = lax.broadcasted_iota(jnp.int32, shape, 1)
    out_part = line % 2
    in_part = column % 2
    same = out_part == in_part
    sign = 2 * out_part - 1
    mix = jnp.zeros(shape, jnp.int32)
    for g in range(inserts):
        for s in range(4):
            target = table_ref[g * 8 + s * 2]
            power = table_ref[g * 8 + s * 2 + 1]
            unit_re = jnp.where(power == 0, 1, 0) - jnp.where(power == 2, 1, 0)
            unit_im = jnp.where(power == 1, 1, 0) - jnp.where(power == 3, 1, 0)
            hit = (line // 2 == g) & (column // 2 == s * 4 + target)
            mix = jnp.where(hit, jnp.where(same, unit_re, sign * unit_im), mix)
    return mix.astype(jnp.float32)


def contract_kernel(gamma_ref, forward_ref, backward_ref, out_ref, pair_ref):
    slices = forward_ref.shape[0]
    rows = forward_ref.shape[3]
    mix = gamma_mix(gamma_ref, out_ref.shape[2] // 2)
    for t in range(slices):
        for u in range(4):
            f_re = [forward_ref[t, 0, 3 * u + c].astype(jnp.float32) for c in range(3)]
            f_im = [forward_ref[t, 1, 3 * u + c].astype(jnp.float32) for c in range(3)]
            for s in range(4):
                acc_re = None
                acc_im = None
                for c in range(3):
                    b_re = backward_ref[t, 0, 3 * s + c].astype(jnp.float32)
                    b_im = backward_ref[t, 1, 3 * s + c].astype(jnp.float32)
                    term_re = b_re * f_re[c] + b_im * f_im[c]
                    term_im = b_re * f_im[c] - b_im * f_re[c]
                    acc_re = term_re if acc_re is None else acc_re + term_re
                    acc_im = term_im if acc_im is None else acc_im + term_im
                base = (s * 4 + u) * 2 * rows
                pair_ref[base : base + rows, :] = acc_re
                pair_ref[base + rows : base + 2 * rows, :] = acc_im
        width = pair_ref.shape[0]
        kinds = mix.shape[1]
        lines = out_ref.shape[1] * kinds
        row = lax.broadcasted_iota(jnp.int32, (lines, width), 0)
        col = lax.broadcasted_iota(jnp.int32, (lines, width), 1)
        pick = jnp.logical_and(row % kinds == col // rows, row // kinds == col % out_ref.shape[1])
        summed = jnp.dot(
            pick.astype(jnp.float32), pair_ref[...], precision=HIGHEST,
            preferred_element_type=jnp.float32,
        )
        for x in range(out_ref.shape[1]):
            out_ref[t, x] = jnp.dot(
                mix, summed[x * kinds : (x + 1) * kinds], precision=HIGHEST,
                preferred_element_type=jnp.float32,
            )


def contract(forward_prop, backward_prop, gamma_table):
    slices = forward_prop.shape[0]
    rows_x = forward_prop.shape[4]
    sites = forward_prop.shape[5]
    inserts = gamma_table.shape[0]
    forward = forward_prop.reshape(slices, 2, 12, 12 * rows_x, sites)
    backward = backward_prop.reshape(slices, 2, 12, 12 * rows_x, sites)
    out = pl.pallas_call(
        contract_kernel,
        out_shape=jax.ShapeDtypeStruct((slices, rows_x, inserts * 2, sites), jnp.float32),
        in_specs=[pl.BlockSpec(memory_space=pltpu.SMEM)]
        + [pl.BlockSpec(memory_space=pltpu.VMEM)] * 2,
        out_specs=pl.BlockSpec(memory_space=pltpu.VMEM),
        scratch_shapes=[pltpu.VMEM((16 * 2 * 12 * rows_x, sites), jnp.float32)],
    )(gamma_table.reshape(-1), forward, backward)
    return out.reshape(slices, rows_x, inserts, 2, sites).transpose(2, 0, 3, 1, 4)


def body(forward_prop, backward_prop, gamma_table, source_site, momenta):
    slices = forward_prop.shape[0]
    rows_x = forward_prop.shape[4]
    rows_y = backward_prop.shape[5] // LZ
    inserts = gamma_table.shape[0]
    fields = contract(forward_prop, backward_prop, gamma_table)
    fields = fields.reshape(inserts * slices, 2, rows_x, rows_y, LZ)
    count = fields.shape[0]
    local_re, local_im = project_sites(fields, source_site, momenta, rows_x, rows_y, L, LZ)
    partial = jnp.stack([local_re, local_im], 0)
    groups_y = lax.axis_size("sy")
    groups_x = lax.axis_size("sx")
    tables = dft_matrices(LZ, source_site)
    share_z = LZ // groups_y
    table_z = tables[2].reshape(2, LZ, 2, groups_y, share_z)
    blocks = jnp.einsum("nrxyz,rzsjc->jsynxc", fields, table_z, precision=HIGH)
    blocks = blocks.reshape(groups_y, 2 * rows_y, -1)
    width = blocks.shape[2]
    shares = partial.reshape(groups_y, 1, -1)
    shares = jnp.pad(shares, ((0, 0), (0, 0), (0, width - shares.shape[2])))
    share_y = rows_y * groups_y // groups_x
    ready = turn(jnp.concatenate([blocks, shares], 1), source_site[1:2], groups_x, 2 * share_y)
    blocks, gathered = spread_ready(ready)
    blocks = blocks.reshape(groups_x, width // 128, share_y, 2, 128).transpose(0, 2, 3, 1, 4)
    blocks = blocks.reshape(groups_x, share_y, 2, count, rows_x, share_z)
    gathered = gathered[:, : partial.size // groups_y]
    table_x = tables[0].reshape(2, groups_x, rows_x, 2, -1)
    spectrum = jnp.einsum("ibsnxc,sixtk->ntbck", blocks, table_x, precision=HIGH)
    corr = spectrum.reshape(inserts, slices, 2, share_y, -1)
    listed = gathered.reshape(2, inserts, slices, -1)
    return (corr, listed)


def solution(mesh):
    placed = (
        P(None, None, None, None, "sx", "sy"),
        P(None, None, None, None, "sx", "sy"),
        P(),
        P(),
        P(),
    )
    return jax.shard_map(
        body,
        mesh=mesh,
        in_specs=placed,
        out_specs=(P(None, None, None, "sx", "sy"), P()),
        check_vma=False,
    )
```

```python
import functools
import math

import jax
import jax.numpy as jnp
from jax import lax
from jax.experimental import pallas as pl
from jax.experimental.pallas import tpu as pltpu
from jax.sharding import PartitionSpec as P

L = 64
LZ = 64


HIGHEST = lax.Precision.HIGHEST
HIGH = lax.Precision.HIGH


def gamma_matrices(gamma_table):
    inserts = gamma_table.shape[0]
    columns = gamma_table[:, :, 0]
    powers = gamma_table[:, :, 1]
    spin_ids = jnp.arange(4, dtype=jnp.int32)
    matches = (columns[:, :, None] == spin_ids[None, None, :]).astype(jnp.float32)
    unit_re = (powers == 0).astype(jnp.float32) - (powers == 2).astype(jnp.float32)
    unit_im = (powers == 1).astype(jnp.float32) - (powers == 3).astype(jnp.float32)
    return (
        (matches * unit_re[:, :, None]).reshape(inserts, 16),
        (matches * unit_im[:, :, None]).reshape(inserts, 16),
    )


def dft_table(length, anchor):
    wavenum = jnp.arange(length, dtype=jnp.int32)
    offsets = jnp.mod(wavenum - anchor, length)
    phase_index = jnp.mod(offsets[:, None] * wavenum[None, :], length)
    angles = 2.0 * math.pi / length * phase_index.astype(jnp.float32)
    return (jnp.cos(angles), -jnp.sin(angles))


def dft_matrices(length, anchors):
    wavenum = jnp.arange(length, dtype=jnp.int32)
    offsets = jnp.mod(wavenum[None, :] - anchors[:, None], length)
    phase_index = jnp.mod(offsets[:, :, None] * wavenum[None, None, :], length)
    angles = 2.0 * math.pi / length * phase_index.astype(jnp.float32)
    table_re = jnp.cos(angles)
    table_im = -jnp.sin(angles)
    rows_re = jnp.stack([table_re, table_im], 2)
    rows_im = jnp.stack([-table_im, table_re], 2)
    return jnp.stack([rows_re, rows_im], 1)


def swap_kernel(axis, blocks_ref, out_ref, send_sem, recv_sem):
    parts = blocks_ref.shape[0]
    me = lax.axis_index(axis)
    mesh_ids = pl.DeviceIdType.MESH
    barrier = pltpu.get_barrier_semaphore()
    for step in range(1, parts):
        pl.semaphore_signal(
            barrier, 1, device_id={axis: lax.rem(me + step, parts)}, device_id_type=mesh_ids
        )
    pl.semaphore_wait(barrier, parts - 1)

    def copy_to(step):
        peer = lax.rem(me + step, parts)
        return pltpu.make_async_remote_copy(
            src_ref=blocks_ref.at[peer],
            dst_ref=out_ref.at[me],
            send_sem=send_sem.at[step],
            recv_sem=recv_sem.at[step],
            device_id={axis: peer},
            device_id_type=mesh_ids,
        )

    def copy_from(step):
        source = lax.rem(me + parts - step, parts)
        return pltpu.make_async_remote_copy(
            src_ref=blocks_ref.at[source],
            dst_ref=out_ref.at[source],
            send_sem=send_sem.at[step],
            recv_sem=recv_sem.at[step],
            device_id={axis: source},
            device_id_type=mesh_ids,
        )

    @pl.loop(1, parts)
    def _(step):
        copy_to(step).start()

    out_ref[me] = blocks_ref[me]

    @pl.loop(1, parts)
    def _(step):
        copy_to(step).wait_send()

    @pl.loop(1, parts)
    def _(step):
        copy_from(step).wait_recv()


def swap(blocks, axis, ident):
    parts = blocks.shape[0]
    lanes = 128
    shaped = blocks.reshape(parts, -1, lanes)
    out = pl.pallas_call(
        functools.partial(swap_kernel, axis),
        out_shape=jax.ShapeDtypeStruct(shaped.shape, shaped.dtype),
        in_specs=[pl.BlockSpec(memory_space=pltpu.VMEM)],
        out_specs=pl.BlockSpec(memory_space=pltpu.VMEM),
        scratch_shapes=[pltpu.SemaphoreType.DMA((parts,)), pltpu.SemaphoreType.DMA((parts,))],
        compiler_params=pltpu.CompilerParams(collective_id=ident, has_side_effects=True),
    )(shaped)
    return out.reshape(blocks.shape)


def exchange(blocks, extra, axis, ident):
    width = blocks.shape[1]
    got = swap(jnp.concatenate([blocks, extra], 1), axis, ident)
    return got[:, :width], got[:, width:].sum(0)


def turn_kernel(anchor_ref, sent_ref, ready_ref, landed_ref, table_ref, send_sem, recv_sem):
    parts = sent_ref.shape[0]
    depth = sent_ref.shape[1] - 1
    band = ready_ref.shape[1] - 1
    me = lax.axis_index("sy")
    mesh_ids = pl.DeviceIdType.MESH
    barrier = pltpu.get_barrier_semaphore()
    for step in range(1, parts):
        pl.semaphore_signal(
            barrier, 1, device_id={"sy": lax.rem(me + step, parts)}, device_id_type=mesh_ids
        )
    table_ref[...] = turn_table(
        parts * depth // 2, anchor_ref[0], depth // 2, ready_ref.shape[1] // 2, table_ref.shape
    )
    pl.semaphore_wait(barrier, parts - 1)

    def copy_y(step, outgoing):
        peer = lax.rem(me + (step if outgoing else parts - step), parts)
        return pltpu.make_async_remote_copy(
            src_ref=sent_ref.at[peer],
            dst_ref=landed_ref.at[me if outgoing else peer],
            send_sem=send_sem.at[step],
            recv_sem=recv_sem.at[step],
            device_id={"sy": peer},
            device_id_type=mesh_ids,
        )

    @pl.loop(1, parts)
    def _(step):
        copy_y(step, True).start()

    landed_ref[me] = sent_ref[me]

    @pl.loop(1, parts)
    def _(step):
        copy_y(step, True).wait_send()

    @pl.loop(1, parts)
    def _(step):
        copy_y(step, False).wait_recv()

    lanes = ready_ref.shape[2]
    halves = landed_ref.shape[2] // lanes
    rows = band // halves
    block = landed_ref[:, 0:depth, :].reshape(parts * depth, -1)
    share = landed_ref[0, depth : depth + 1, 0:lanes]
    for source in range(1, parts):
        share = share + landed_ref[source, depth : depth + 1, 0:lanes]
    for half in range(halves):
        turned = jnp.dot(
            table_ref[...], block[:, half * lanes : (half + 1) * lanes], precision=HIGHEST,
            preferred_element_type=jnp.float32,
        )
        for peer in range(ready_ref.shape[0]):
            ready_ref[peer, half * rows : (half + 1) * rows, :] = turned[peer * rows : (peer + 1) * rows]
    for peer in range(ready_ref.shape[0]):
        ready_ref[peer, band : band + 1, :] = share


def turn(sent, anchor, parts_x, band):
    parts_y, rows, width = sent.shape
    vmem = pl.BlockSpec(memory_space=pltpu.VMEM)
    return pl.pallas_call(
        turn_kernel,
        out_shape=jax.ShapeDtypeStruct((parts_x, band * width // 128 + 1, 128), jnp.float32),
        in_specs=[pl.BlockSpec(memory_space=pltpu.SMEM), vmem],
        out_specs=vmem,
        scratch_shapes=[
            pltpu.VMEM((parts_y, rows, width), jnp.float32),
            pltpu.VMEM((parts_y * (rows - 1), parts_y * (rows - 1)), jnp.float32),
            pltpu.SemaphoreType.DMA((parts_y,)),
            pltpu.SemaphoreType.DMA((parts_y,)),
        ],
        compiler_params=pltpu.CompilerParams(collective_id=0, has_side_effects=True),
    )(anchor, sent)


def turn_table(length, anchor, rows_y, share_y, shape):
    line = lax.broadcasted_iota(jnp.int32, shape, 0)
    column = lax.broadcasted_iota(jnp.int32, shape, 1)
    wave = line // 2
    out_part = line % 2
    in_part = (column // rows_y) % 2
    site = (column // (2 * rows_y)) * rows_y + column % rows_y
    offset = (site - anchor + length) % length
    index = (offset * wave + (length // 4) * (out_part - in_part) + length) % length
    return jnp.cos((2.0 * math.pi / length) * index.astype(jnp.float32))


def spread_kernel(blocks_ref, out_ref, gathered_ref, total_ref, b_send, b_recv, c_send, c_recv):
    parts_x = blocks_ref.shape[0]
    parts_y = gathered_ref.shape[0]
    depth = blocks_ref.shape[1] - 1
    me_x = lax.axis_index("sx")
    me_y = lax.axis_index("sy")
    mesh_ids = pl.DeviceIdType.MESH
    barrier = pltpu.get_barrier_semaphore()
    for step in range(1, parts_x):
        pl.semaphore_signal(
            barrier, 1, device_id={"sx": lax.rem(me_x + step, parts_x)}, device_id_type=mesh_ids
        )
    for step in range(1, parts_y):
        pl.semaphore_signal(
            barrier, 1, device_id={"sy": lax.rem(me_y + step, parts_y)}, device_id_type=mesh_ids
        )
    pl.semaphore_wait(barrier, parts_x + parts_y - 2)

    def copy_x(step, outgoing):
        peer = lax.rem(me_x + (step if outgoing else parts_x - step), parts_x)
        return pltpu.make_async_remote_copy(
            src_ref=blocks_ref.at[peer],
            dst_ref=out_ref.at[me_x if outgoing else peer],
            send_sem=b_send.at[step],
            recv_sem=b_recv.at[step],
            device_id={"sx": peer},
            device_id_type=mesh_ids,
        )

    def copy_y(step, outgoing):
        peer = lax.rem(me_y + (step if outgoing else parts_y - step), parts_y)
        return pltpu.make_async_remote_copy(
            src_ref=total_ref,
            dst_ref=gathered_ref.at[me_y if outgoing else peer],
            send_sem=c_send.at[step],
            recv_sem=c_recv.at[step],
            device_id={"sy": peer},
            device_id_type=mesh_ids,
        )

    @pl.loop(1, parts_x)
    def _(step):
        copy_x(step, True).start()

    out_ref[me_x] = blocks_ref[me_x]

    @pl.loop(1, parts_x)
    def _(step):
        copy_x(step, True).wait_send()

    @pl.loop(1, parts_x)
    def _(step):
        copy_x(step, False).wait_recv()

    total = out_ref[0, depth : depth + 1, :]
    for source in range(1, parts_x):
        total = total + out_ref[source, depth : depth + 1, :]
    total_ref[...] = total

    @pl.loop(1, parts_y)
    def _(step):
        copy_y(step, True).start()

    gathered_ref[me_y] = total

    @pl.loop(1, parts_y)
    def _(step):
        copy_y(step, True).wait_send()

    @pl.loop(1, parts_y)
    def _(step):
        copy_y(step, False).wait_recv()


def spread_ready(shaped):
    parts_x = shaped.shape[0]
    parts_y = lax.axis_size("sy")
    vmem = pl.BlockSpec(memory_space=pltpu.VMEM)
    got, gathered = pl.pallas_call(
        spread_kernel,
        out_shape=(
            jax.ShapeDtypeStruct(shaped.shape, shaped.dtype),
            jax.ShapeDtypeStruct((parts_y, 1, shaped.shape[2]), shaped.dtype),
        ),
        in_specs=[vmem],
        out_specs=(vmem, vmem),
        scratch_shapes=[
            pltpu.VMEM((1, shaped.shape[2]), jnp.float32),
            pltpu.SemaphoreType.DMA((parts_x,)),
            pltpu.SemaphoreType.DMA((parts_x,)),
            pltpu.SemaphoreType.DMA((parts_y,)),
            pltpu.SemaphoreType.DMA((parts_y,)),
        ],
        compiler_params=pltpu.CompilerParams(collective_id=1, has_side_effects=True),
    )(shaped)
    return got[:, :-1], gathered[:, 0]


def spread(blocks, share, parts_y):
    parts_x = blocks.shape[0]
    lanes = 128
    width = share.size
    rows = jnp.pad(share, (0, lanes - width)) if width < lanes else share
    shaped = blocks.reshape(parts_x, -1, rows.size)
    shaped = jnp.concatenate(
        [shaped, jnp.broadcast_to(rows.reshape(1, 1, -1), (parts_x, 1, rows.size))], 1
    )
    vmem = pl.BlockSpec(memory_space=pltpu.VMEM)
    got, gathered = pl.pallas_call(
        spread_kernel,
        out_shape=(
            jax.ShapeDtypeStruct(shaped.shape, shaped.dtype),
            jax.ShapeDtypeStruct((parts_y, 1, rows.size), shaped.dtype),
        ),
        in_specs=[vmem],
        out_specs=(vmem, vmem),
        scratch_shapes=[
            pltpu.VMEM((1, rows.size), jnp.float32),
            pltpu.SemaphoreType.DMA((parts_x,)),
            pltpu.SemaphoreType.DMA((parts_x,)),
            pltpu.SemaphoreType.DMA((parts_y,)),
            pltpu.SemaphoreType.DMA((parts_y,)),
        ],
        compiler_params=pltpu.CompilerParams(collective_id=1, has_side_effects=True),
    )(shaped)
    return got[:, :-1].reshape(blocks.shape), gathered[:, 0, :width]


def apply_gammas(mat_re, mat_im, real_part, imag_part):
    extent = real_part.shape
    flat_re = real_part.reshape(extent[0], -1)
    flat_im = imag_part.reshape(extent[0], -1)
    out_re = jnp.dot(mat_re, flat_re, precision=HIGHEST) - jnp.dot(
        mat_im, flat_im, precision=HIGHEST
    )
    out_im = jnp.dot(mat_re, flat_im, precision=HIGHEST) + jnp.dot(
        mat_im, flat_re, precision=HIGHEST
    )
    return (out_re.reshape(extent), out_im.reshape(extent))


def project_sites(fields, source_site, momenta, rows_x, rows_y, length, depth):
    coord_x = lax.axis_index("sx") * rows_x + jnp.arange(rows_x, dtype=jnp.int32) - source_site[0]
    coord_y = lax.axis_index("sy") * rows_y + jnp.arange(rows_y, dtype=jnp.int32) - source_site[1]
    coord_z = jnp.arange(depth, dtype=jnp.int32) - source_site[2]
    part_x = jnp.mod(momenta[:, 0:1] * coord_x[None, :], length)
    part_y = jnp.mod(momenta[:, 1:2] * coord_y[None, :], length)
    part_z = jnp.mod(momenta[:, 2:3] * coord_z[None, :], depth)
    plane = jnp.mod(part_x[:, :, None] + part_y[:, None, :], length).astype(jnp.float32)
    angles = (
        2.0 * math.pi / length * plane[:, :, :, None]
        + 2.0 * math.pi / depth * part_z.astype(jnp.float32)[:, None, None, :]
    )
    angles = angles.reshape(momenta.shape[0], -1)
    cosine = jnp.cos(angles)
    sine = jnp.sin(angles)
    field_re = fields[:, 0].reshape(fields.shape[0], -1)
    field_im = fields[:, 1].reshape(fields.shape[0], -1)
    local_re = jnp.dot(field_re, cosine.T, precision=HIGHEST) + jnp.dot(
        field_im, sine.T, precision=HIGHEST
    )
    local_im = jnp.dot(field_im, cosine.T, precision=HIGHEST) - jnp.dot(
        field_re, sine.T, precision=HIGHEST
    )
    return (local_re, local_im)


def gamma_mix(table_ref, inserts):
    shape = (inserts * 2, 32)
    line = lax.broadcasted_iota(jnp.int32, shape, 0)
    column = lax.broadcasted_iota(jnp.int32, shape, 1)
    out_part = line // inserts
    in_part = column % 2
    same = out_part == in_part
    sign = 2 * out_part - 1
    mix = jnp.zeros(shape, jnp.int32)
    for g in range(inserts):
        for s in range(4):
            target = table_ref[g * 8 + s * 2]
            power = table_ref[g * 8 + s * 2 + 1]
            unit_re = jnp.where(power == 0, 1, 0) - jnp.where(power == 2, 1, 0)
            unit_im = jnp.where(power == 1, 1, 0) - jnp.where(power == 3, 1, 0)
            hit = (line % inserts == g) & (column // 2 == s * 4 + target)
            mix = jnp.where(hit, jnp.where(same, unit_re, sign * unit_im), mix)
    return mix.astype(jnp.float32)


def phase_tables(moment_ref, site_ref, x, sites, count):
    span = lax.broadcasted_iota(jnp.int32, (1, count), 1)
    wave = [jnp.zeros((1, count), jnp.int32) for _ in range(3)]
    for m in range(count):
        for axis in range(3):
            wave[axis] = jnp.where(span == m, moment_ref[m * 3 + axis], wave[axis])
    rows_y = sites // LZ
    place = lax.broadcasted_iota(jnp.int32, (sites, 1), 0)
    coord_x = x - site_ref[0]
    coord_y = lax.axis_index("sy") * rows_y + place // LZ - site_ref[1]
    coord_z = place % LZ - site_ref[2]
    phase = wave[0] * coord_x + wave[1] * coord_y + wave[2] * coord_z
    phase = (phase % L + L) % L
    angle = (2.0 * math.pi / L) * phase.astype(jnp.float32)
    return jnp.cos(angle), jnp.sin(angle)


def contract_kernel(
    gamma_ref, moment_ref, site_ref, forward_ref, backward_ref, out_ref, local_ref, pair_ref
):
    slices = forward_ref.shape[0]
    rows = forward_ref.shape[3]
    inserts = out_ref.shape[2] // 2
    mix = gamma_mix(gamma_ref, inserts)
    rows_x = out_ref.shape[1]
    tables = [
        phase_tables(
            moment_ref, site_ref, lax.axis_index("sx") * rows_x + x, out_ref.shape[3],
            local_ref.shape[3],
        )
        for x in range(rows_x)
    ]
    for t in range(slices):
        for u in range(4):
            f_re = [forward_ref[t, 0, 3 * u + c].astype(jnp.float32) for c in range(3)]
            f_im = [forward_ref[t, 1, 3 * u + c].astype(jnp.float32) for c in range(3)]
            for s in range(4):
                acc_re = None
                acc_im = None
                for c in range(3):
                    b_re = backward_ref[t, 0, 3 * s + c].astype(jnp.float32)
                    b_im = backward_ref[t, 1, 3 * s + c].astype(jnp.float32)
                    term_re = b_re * f_re[c] + b_im * f_im[c]
                    term_im = b_re * f_im[c] - b_im * f_re[c]
                    acc_re = term_re if acc_re is None else acc_re + term_re
                    acc_im = term_im if acc_im is None else acc_im + term_im
                base = (s * 4 + u) * 2 * rows
                pair_ref[base : base + rows, :] = acc_re
                pair_ref[base + rows : base + 2 * rows, :] = acc_im
        width = pair_ref.shape[0]
        kinds = mix.shape[1]
        lines = out_ref.shape[1] * kinds
        row = lax.broadcasted_iota(jnp.int32, (lines, width), 0)
        col = lax.broadcasted_iota(jnp.int32, (lines, width), 1)
        pick = jnp.logical_and(row % kinds == col // rows, row // kinds == col % out_ref.shape[1])
        summed = jnp.dot(
            pick.astype(jnp.float32), pair_ref[...], precision=HIGHEST,
            preferred_element_type=jnp.float32,
        )
        local_re = None
        local_im = None
        for x in range(out_ref.shape[1]):
            field = jnp.dot(
                mix, summed[x * kinds : (x + 1) * kinds], precision=HIGHEST,
                preferred_element_type=jnp.float32,
            )
            out_ref[t, x] = field
            cosine, sine = tables[x]
            with_cos = jnp.dot(field, cosine, precision=HIGHEST, preferred_element_type=jnp.float32)
            with_sin = jnp.dot(field, sine, precision=HIGHEST, preferred_element_type=jnp.float32)
            part_re = with_cos[0:inserts] + with_sin[inserts:]
            part_im = with_cos[inserts:] - with_sin[0:inserts]
            local_re = part_re if local_re is None else local_re + part_re
            local_im = part_im if local_im is None else local_im + part_im
        local_ref[0, t] = local_re
        local_ref[1, t] = local_im


def contract(forward_prop, backward_prop, gamma_table, momenta, source_site):
    slices = forward_prop.shape[0]
    rows_x = forward_prop.shape[4]
    sites = forward_prop.shape[5]
    inserts = gamma_table.shape[0]
    forward = forward_prop.reshape(slices, 2, 12, 12 * rows_x, sites)
    backward = backward_prop.reshape(slices, 2, 12, 12 * rows_x, sites)
    smem = pl.BlockSpec(memory_space=pltpu.SMEM)
    vmem = pl.BlockSpec(memory_space=pltpu.VMEM)
    out, local = pl.pallas_call(
        contract_kernel,
        out_shape=(
            jax.ShapeDtypeStruct((slices, rows_x, inserts * 2, sites), jnp.float32),
            jax.ShapeDtypeStruct((2, slices, inserts, momenta.shape[0]), jnp.float32),
        ),
        in_specs=[smem, smem, smem, vmem, vmem],
        out_specs=(vmem, vmem),
        scratch_shapes=[pltpu.VMEM((16 * 2 * 12 * rows_x, sites), jnp.float32)],
    )(gamma_table.reshape(-1), momenta.reshape(-1), source_site, forward, backward)
    fields = out.reshape(slices, rows_x, 2, inserts, sites).transpose(3, 0, 2, 1, 4)
    return fields, local


def body(forward_prop, backward_prop, gamma_table, source_site, momenta):
    slices = forward_prop.shape[0]
    rows_x = forward_prop.shape[4]
    rows_y = backward_prop.shape[5] // LZ
    inserts = gamma_table.shape[0]
    fields, partial = contract(forward_prop, backward_prop, gamma_table, momenta, source_site)
    fields = fields.reshape(inserts * slices, 2, rows_x, rows_y, LZ)
    count = fields.shape[0]
    groups_y = lax.axis_size("sy")
    groups_x = lax.axis_size("sx")
    tables = dft_matrices(LZ, source_site)
    share_z = LZ // groups_y
    table_z = tables[2].reshape(2, LZ, 2, groups_y, share_z)
    blocks = jnp.einsum("nrxyz,rzsjc->jsynxc", fields, table_z, precision=HIGH)
    blocks = blocks.reshape(groups_y, 2 * rows_y, -1)
    width = blocks.shape[2]
    shares = partial.reshape(groups_y, 1, -1)
    shares = jnp.pad(shares, ((0, 0), (0, 0), (0, width - shares.shape[2])))
    share_y = rows_y * groups_y // groups_x
    ready = turn(jnp.concatenate([blocks, shares], 1), source_site[1:2], groups_x, 2 * share_y)
    blocks, gathered = spread_ready(ready)
    blocks = blocks.reshape(groups_x, width // 128, share_y, 2, 128).transpose(0, 2, 3, 1, 4)
    blocks = blocks.reshape(groups_x, share_y, 2, count, rows_x, share_z)
    gathered = gathered[:, : partial.size // groups_y]
    table_x = tables[0].reshape(2, groups_x, rows_x, 2, -1)
    spectrum = jnp.einsum("ibsnxc,sixtk->ntbck", blocks, table_x, precision=HIGH)
    corr = spectrum.reshape(inserts, slices, 2, share_y, -1)
    listed = gathered.reshape(2, slices, inserts, -1).transpose(0, 2, 1, 3)
    return (corr, listed)


def solution(mesh):
    placed = (
        P(None, None, None, None, "sx", "sy"),
        P(None, None, None, None, "sx", "sy"),
        P(),
        P(),
        P(),
    )
    return jax.shard_map(
        body,
        mesh=mesh,
        in_specs=placed,
        out_specs=(P(None, None, None, "sx", "sy"), P()),
        check_vma=False,
    )
```

```python
import functools
import math

import jax
import jax.numpy as jnp
from jax import lax
from jax.experimental import pallas as pl
from jax.experimental.pallas import tpu as pltpu
from jax.sharding import PartitionSpec as P

L = 64
LZ = 64


HIGHEST = lax.Precision.HIGHEST
HIGH = lax.Precision.HIGH


def gamma_matrices(gamma_table):
    inserts = gamma_table.shape[0]
    columns = gamma_table[:, :, 0]
    powers = gamma_table[:, :, 1]
    spin_ids = jnp.arange(4, dtype=jnp.int32)
    matches = (columns[:, :, None] == spin_ids[None, None, :]).astype(jnp.float32)
    unit_re = (powers == 0).astype(jnp.float32) - (powers == 2).astype(jnp.float32)
    unit_im = (powers == 1).astype(jnp.float32) - (powers == 3).astype(jnp.float32)
    return (
        (matches * unit_re[:, :, None]).reshape(inserts, 16),
        (matches * unit_im[:, :, None]).reshape(inserts, 16),
    )


def dft_table(length, anchor):
    wavenum = jnp.arange(length, dtype=jnp.int32)
    offsets = jnp.mod(wavenum - anchor, length)
    phase_index = jnp.mod(offsets[:, None] * wavenum[None, :], length)
    angles = 2.0 * math.pi / length * phase_index.astype(jnp.float32)
    return (jnp.cos(angles), -jnp.sin(angles))


def dft_matrices(length, anchors):
    wavenum = jnp.arange(length, dtype=jnp.int32)
    offsets = jnp.mod(wavenum[None, :] - anchors[:, None], length)
    phase_index = jnp.mod(offsets[:, :, None] * wavenum[None, None, :], length)
    angles = 2.0 * math.pi / length * phase_index.astype(jnp.float32)
    table_re = jnp.cos(angles)
    table_im = -jnp.sin(angles)
    rows_re = jnp.stack([table_re, table_im], 2)
    rows_im = jnp.stack([-table_im, table_re], 2)
    return jnp.stack([rows_re, rows_im], 1)


def swap_kernel(axis, blocks_ref, out_ref, send_sem, recv_sem):
    parts = blocks_ref.shape[0]
    me = lax.axis_index(axis)
    mesh_ids = pl.DeviceIdType.MESH
    barrier = pltpu.get_barrier_semaphore()
    for step in range(1, parts):
        pl.semaphore_signal(
            barrier, 1, device_id={axis: lax.rem(me + step, parts)}, device_id_type=mesh_ids
        )
    pl.semaphore_wait(barrier, parts - 1)

    def copy_to(step):
        peer = lax.rem(me + step, parts)
        return pltpu.make_async_remote_copy(
            src_ref=blocks_ref.at[peer],
            dst_ref=out_ref.at[me],
            send_sem=send_sem.at[step],
            recv_sem=recv_sem.at[step],
            device_id={axis: peer},
            device_id_type=mesh_ids,
        )

    def copy_from(step):
        source = lax.rem(me + parts - step, parts)
        return pltpu.make_async_remote_copy(
            src_ref=blocks_ref.at[source],
            dst_ref=out_ref.at[source],
            send_sem=send_sem.at[step],
            recv_sem=recv_sem.at[step],
            device_id={axis: source},
            device_id_type=mesh_ids,
        )

    @pl.loop(1, parts)
    def _(step):
        copy_to(step).start()

    out_ref[me] = blocks_ref[me]

    @pl.loop(1, parts)
    def _(step):
        copy_to(step).wait_send()

    @pl.loop(1, parts)
    def _(step):
        copy_from(step).wait_recv()


def swap(blocks, axis, ident):
    parts = blocks.shape[0]
    lanes = 128
    shaped = blocks.reshape(parts, -1, lanes)
    out = pl.pallas_call(
        functools.partial(swap_kernel, axis),
        out_shape=jax.ShapeDtypeStruct(shaped.shape, shaped.dtype),
        in_specs=[pl.BlockSpec(memory_space=pltpu.VMEM)],
        out_specs=pl.BlockSpec(memory_space=pltpu.VMEM),
        scratch_shapes=[pltpu.SemaphoreType.DMA((parts,)), pltpu.SemaphoreType.DMA((parts,))],
        compiler_params=pltpu.CompilerParams(collective_id=ident, has_side_effects=True),
    )(shaped)
    return out.reshape(blocks.shape)


def exchange(blocks, extra, axis, ident):
    width = blocks.shape[1]
    got = swap(jnp.concatenate([blocks, extra], 1), axis, ident)
    return got[:, :width], got[:, width:].sum(0)


def turn_kernel(anchor_ref, sent_ref, ready_ref, landed_ref, table_ref, send_sem, recv_sem):
    parts = sent_ref.shape[0]
    depth = sent_ref.shape[1] - 1
    band = ready_ref.shape[1] - 1
    me = lax.axis_index("sy")
    mesh_ids = pl.DeviceIdType.MESH
    barrier = pltpu.get_barrier_semaphore()
    for step in range(1, parts):
        pl.semaphore_signal(
            barrier, 1, device_id={"sy": lax.rem(me + step, parts)}, device_id_type=mesh_ids
        )
    table_ref[...] = turn_table(
        parts * depth // 2, anchor_ref[0], depth // 2, ready_ref.shape[1] // 2, table_ref.shape
    )
    pl.semaphore_wait(barrier, parts - 1)

    def copy_y(step, outgoing):
        peer = lax.rem(me + (step if outgoing else parts - step), parts)
        return pltpu.make_async_remote_copy(
            src_ref=sent_ref.at[peer],
            dst_ref=landed_ref.at[me if outgoing else peer],
            send_sem=send_sem.at[step],
            recv_sem=recv_sem.at[step],
            device_id={"sy": peer},
            device_id_type=mesh_ids,
        )

    @pl.loop(1, parts)
    def _(step):
        copy_y(step, True).start()

    landed_ref[me] = sent_ref[me]

    @pl.loop(1, parts)
    def _(step):
        copy_y(step, False).wait_recv()

    lanes = ready_ref.shape[2]
    halves = landed_ref.shape[2] // lanes
    rows = band // halves
    block = landed_ref[:, 0:depth, :].reshape(parts * depth, -1)
    share = landed_ref[0, depth : depth + 1, 0:lanes]
    for source in range(1, parts):
        share = share + landed_ref[source, depth : depth + 1, 0:lanes]
    for half in range(halves):
        turned = jnp.dot(
            table_ref[...], block[:, half * lanes : (half + 1) * lanes], precision=HIGHEST,
            preferred_element_type=jnp.float32,
        )
        for peer in range(ready_ref.shape[0]):
            ready_ref[peer, half * rows : (half + 1) * rows, :] = turned[peer * rows : (peer + 1) * rows]
    for peer in range(ready_ref.shape[0]):
        ready_ref[peer, band : band + 1, :] = share

    @pl.loop(1, parts)
    def _(step):
        copy_y(step, True).wait_send()


def turn(sent, anchor, parts_x, band):
    parts_y, rows, width = sent.shape
    vmem = pl.BlockSpec(memory_space=pltpu.VMEM)
    return pl.pallas_call(
        turn_kernel,
        out_shape=jax.ShapeDtypeStruct((parts_x, band * width // 128 + 1, 128), jnp.float32),
        in_specs=[pl.BlockSpec(memory_space=pltpu.SMEM), vmem],
        out_specs=vmem,
        scratch_shapes=[
            pltpu.VMEM((parts_y, rows, width), jnp.float32),
            pltpu.VMEM((parts_y * (rows - 1), parts_y * (rows - 1)), jnp.float32),
            pltpu.SemaphoreType.DMA((parts_y,)),
            pltpu.SemaphoreType.DMA((parts_y,)),
        ],
        compiler_params=pltpu.CompilerParams(collective_id=0, has_side_effects=True),
    )(anchor, sent)


def turn_table(length, anchor, rows_y, share_y, shape):
    line = lax.broadcasted_iota(jnp.int32, shape, 0)
    column = lax.broadcasted_iota(jnp.int32, shape, 1)
    wave = line // 2
    out_part = line % 2
    in_part = (column // rows_y) % 2
    site = (column // (2 * rows_y)) * rows_y + column % rows_y
    offset = (site - anchor + length) % length
    index = (offset * wave + (length // 4) * (out_part - in_part) + length) % length
    return jnp.cos((2.0 * math.pi / length) * index.astype(jnp.float32))


def spread_kernel(blocks_ref, out_ref, gathered_ref, total_ref, b_send, b_recv, c_send, c_recv):
    parts_x = blocks_ref.shape[0]
    parts_y = gathered_ref.shape[0]
    depth = blocks_ref.shape[1] - 1
    me_x = lax.axis_index("sx")
    me_y = lax.axis_index("sy")
    mesh_ids = pl.DeviceIdType.MESH
    barrier = pltpu.get_barrier_semaphore()
    for step in range(1, parts_x):
        pl.semaphore_signal(
            barrier, 1, device_id={"sx": lax.rem(me_x + step, parts_x)}, device_id_type=mesh_ids
        )
    for step in range(1, parts_y):
        pl.semaphore_signal(
            barrier, 1, device_id={"sy": lax.rem(me_y + step, parts_y)}, device_id_type=mesh_ids
        )
    pl.semaphore_wait(barrier, parts_x + parts_y - 2)

    def copy_x(step, outgoing):
        peer = lax.rem(me_x + (step if outgoing else parts_x - step), parts_x)
        return pltpu.make_async_remote_copy(
            src_ref=blocks_ref.at[peer],
            dst_ref=out_ref.at[me_x if outgoing else peer],
            send_sem=b_send.at[step],
            recv_sem=b_recv.at[step],
            device_id={"sx": peer},
            device_id_type=mesh_ids,
        )

    def copy_y(step, outgoing):
        peer = lax.rem(me_y + (step if outgoing else parts_y - step), parts_y)
        return pltpu.make_async_remote_copy(
            src_ref=total_ref,
            dst_ref=gathered_ref.at[me_y if outgoing else peer],
            send_sem=c_send.at[step],
            recv_sem=c_recv.at[step],
            device_id={"sy": peer},
            device_id_type=mesh_ids,
        )

    @pl.loop(1, parts_x)
    def _(step):
        copy_x(step, True).start()

    out_ref[me_x] = blocks_ref[me_x]

    @pl.loop(1, parts_x)
    def _(step):
        copy_x(step, False).wait_recv()

    total = out_ref[0, depth : depth + 1, :]
    for source in range(1, parts_x):
        total = total + out_ref[source, depth : depth + 1, :]
    total_ref[...] = total

    @pl.loop(1, parts_y)
    def _(step):
        copy_y(step, True).start()

    gathered_ref[me_y] = total

    @pl.loop(1, parts_x)
    def _(step):
        copy_x(step, True).wait_send()

    @pl.loop(1, parts_y)
    def _(step):
        copy_y(step, True).wait_send()

    @pl.loop(1, parts_y)
    def _(step):
        copy_y(step, False).wait_recv()


def spread_ready(shaped):
    parts_x = shaped.shape[0]
    parts_y = lax.axis_size("sy")
    vmem = pl.BlockSpec(memory_space=pltpu.VMEM)
    got, gathered = pl.pallas_call(
        spread_kernel,
        out_shape=(
            jax.ShapeDtypeStruct(shaped.shape, shaped.dtype),
            jax.ShapeDtypeStruct((parts_y, 1, shaped.shape[2]), shaped.dtype),
        ),
        in_specs=[vmem],
        out_specs=(vmem, vmem),
        scratch_shapes=[
            pltpu.VMEM((1, shaped.shape[2]), jnp.float32),
            pltpu.SemaphoreType.DMA((parts_x,)),
            pltpu.SemaphoreType.DMA((parts_x,)),
            pltpu.SemaphoreType.DMA((parts_y,)),
            pltpu.SemaphoreType.DMA((parts_y,)),
        ],
        compiler_params=pltpu.CompilerParams(collective_id=1, has_side_effects=True),
    )(shaped)
    return got[:, :-1], gathered[:, 0]


def spread(blocks, share, parts_y):
    parts_x = blocks.shape[0]
    lanes = 128
    width = share.size
    rows = jnp.pad(share, (0, lanes - width)) if width < lanes else share
    shaped = blocks.reshape(parts_x, -1, rows.size)
    shaped = jnp.concatenate(
        [shaped, jnp.broadcast_to(rows.reshape(1, 1, -1), (parts_x, 1, rows.size))], 1
    )
    vmem = pl.BlockSpec(memory_space=pltpu.VMEM)
    got, gathered = pl.pallas_call(
        spread_kernel,
        out_shape=(
            jax.ShapeDtypeStruct(shaped.shape, shaped.dtype),
            jax.ShapeDtypeStruct((parts_y, 1, rows.size), shaped.dtype),
        ),
        in_specs=[vmem],
        out_specs=(vmem, vmem),
        scratch_shapes=[
            pltpu.VMEM((1, rows.size), jnp.float32),
            pltpu.SemaphoreType.DMA((parts_x,)),
            pltpu.SemaphoreType.DMA((parts_x,)),
            pltpu.SemaphoreType.DMA((parts_y,)),
            pltpu.SemaphoreType.DMA((parts_y,)),
        ],
        compiler_params=pltpu.CompilerParams(collective_id=1, has_side_effects=True),
    )(shaped)
    return got[:, :-1].reshape(blocks.shape), gathered[:, 0, :width]


def apply_gammas(mat_re, mat_im, real_part, imag_part):
    extent = real_part.shape
    flat_re = real_part.reshape(extent[0], -1)
    flat_im = imag_part.reshape(extent[0], -1)
    out_re = jnp.dot(mat_re, flat_re, precision=HIGHEST) - jnp.dot(
        mat_im, flat_im, precision=HIGHEST
    )
    out_im = jnp.dot(mat_re, flat_im, precision=HIGHEST) + jnp.dot(
        mat_im, flat_re, precision=HIGHEST
    )
    return (out_re.reshape(extent), out_im.reshape(extent))


def project_sites(fields, source_site, momenta, rows_x, rows_y, length, depth):
    coord_x = lax.axis_index("sx") * rows_x + jnp.arange(rows_x, dtype=jnp.int32) - source_site[0]
    coord_y = lax.axis_index("sy") * rows_y + jnp.arange(rows_y, dtype=jnp.int32) - source_site[1]
    coord_z = jnp.arange(depth, dtype=jnp.int32) - source_site[2]
    part_x = jnp.mod(momenta[:, 0:1] * coord_x[None, :], length)
    part_y = jnp.mod(momenta[:, 1:2] * coord_y[None, :], length)
    part_z = jnp.mod(momenta[:, 2:3] * coord_z[None, :], depth)
    plane = jnp.mod(part_x[:, :, None] + part_y[:, None, :], length).astype(jnp.float32)
    angles = (
        2.0 * math.pi / length * plane[:, :, :, None]
        + 2.0 * math.pi / depth * part_z.astype(jnp.float32)[:, None, None, :]
    )
    angles = angles.reshape(momenta.shape[0], -1)
    cosine = jnp.cos(angles)
    sine = jnp.sin(angles)
    field_re = fields[:, 0].reshape(fields.shape[0], -1)
    field_im = fields[:, 1].reshape(fields.shape[0], -1)
    local_re = jnp.dot(field_re, cosine.T, precision=HIGHEST) + jnp.dot(
        field_im, sine.T, precision=HIGHEST
    )
    local_im = jnp.dot(field_im, cosine.T, precision=HIGHEST) - jnp.dot(
        field_re, sine.T, precision=HIGHEST
    )
    return (local_re, local_im)


def gamma_mix(table_ref, inserts):
    shape = (inserts * 2, 32)
    line = lax.broadcasted_iota(jnp.int32, shape, 0)
    column = lax.broadcasted_iota(jnp.int32, shape, 1)
    out_part = line % 2
    in_part = column % 2
    same = out_part == in_part
    sign = 2 * out_part - 1
    mix = jnp.zeros(shape, jnp.int32)
    for g in range(inserts):
        for s in range(4):
            target = table_ref[g * 8 + s * 2]
            power = table_ref[g * 8 + s * 2 + 1]
            unit_re = jnp.where(power == 0, 1, 0) - jnp.where(power == 2, 1, 0)
            unit_im = jnp.where(power == 1, 1, 0) - jnp.where(power == 3, 1, 0)
            hit = (line // 2 == g) & (column // 2 == s * 4 + target)
            mix = jnp.where(hit, jnp.where(same, unit_re, sign * unit_im), mix)
    return mix.astype(jnp.float32)


def contract_kernel(gamma_ref, forward_ref, backward_ref, out_ref, pair_ref):
    slices = forward_ref.shape[0]
    rows = forward_ref.shape[3]
    mix = gamma_mix(gamma_ref, out_ref.shape[2] // 2)
    for t in range(slices):
        for u in range(4):
            f_re = [forward_ref[t, 0, 3 * u + c].astype(jnp.float32) for c in range(3)]
            f_im = [forward_ref[t, 1, 3 * u + c].astype(jnp.float32) for c in range(3)]
            for s in range(4):
                acc_re = None
                acc_im = None
                for c in range(3):
                    b_re = backward_ref[t, 0, 3 * s + c].astype(jnp.float32)
                    b_im = backward_ref[t, 1, 3 * s + c].astype(jnp.float32)
                    term_re = b_re * f_re[c] + b_im * f_im[c]
                    term_im = b_re * f_im[c] - b_im * f_re[c]
                    acc_re = term_re if acc_re is None else acc_re + term_re
                    acc_im = term_im if acc_im is None else acc_im + term_im
                base = (s * 4 + u) * 2 * rows
                pair_ref[base : base + rows, :] = acc_re
                pair_ref[base + rows : base + 2 * rows, :] = acc_im
        width = pair_ref.shape[0]
        kinds = mix.shape[1]
        lines = out_ref.shape[1] * kinds
        row = lax.broadcasted_iota(jnp.int32, (lines, width), 0)
        col = lax.broadcasted_iota(jnp.int32, (lines, width), 1)
        pick = jnp.logical_and(row % kinds == col // rows, row // kinds == col % out_ref.shape[1])
        summed = jnp.dot(
            pick.astype(jnp.float32), pair_ref[...], precision=HIGHEST,
            preferred_element_type=jnp.float32,
        )
        for x in range(out_ref.shape[1]):
            out_ref[t, x] = jnp.dot(
                mix, summed[x * kinds : (x + 1) * kinds], precision=HIGHEST,
                preferred_element_type=jnp.float32,
            )


def contract(forward_prop, backward_prop, gamma_table):
    slices = forward_prop.shape[0]
    rows_x = forward_prop.shape[4]
    sites = forward_prop.shape[5]
    inserts = gamma_table.shape[0]
    forward = forward_prop.reshape(slices, 2, 12, 12 * rows_x, sites)
    backward = backward_prop.reshape(slices, 2, 12, 12 * rows_x, sites)
    out = pl.pallas_call(
        contract_kernel,
        out_shape=jax.ShapeDtypeStruct((slices, rows_x, inserts * 2, sites), jnp.float32),
        in_specs=[pl.BlockSpec(memory_space=pltpu.SMEM)]
        + [pl.BlockSpec(memory_space=pltpu.VMEM)] * 2,
        out_specs=pl.BlockSpec(memory_space=pltpu.VMEM),
        scratch_shapes=[pltpu.VMEM((16 * 2 * 12 * rows_x, sites), jnp.float32)],
    )(gamma_table.reshape(-1), forward, backward)
    return out.reshape(slices, rows_x, inserts, 2, sites).transpose(2, 0, 3, 1, 4)


def body(forward_prop, backward_prop, gamma_table, source_site, momenta):
    slices = forward_prop.shape[0]
    rows_x = forward_prop.shape[4]
    rows_y = backward_prop.shape[5] // LZ
    inserts = gamma_table.shape[0]
    fields = contract(forward_prop, backward_prop, gamma_table)
    fields = fields.reshape(inserts * slices, 2, rows_x, rows_y, LZ)
    count = fields.shape[0]
    local_re, local_im = project_sites(fields, source_site, momenta, rows_x, rows_y, L, LZ)
    partial = jnp.stack([local_re, local_im], 0)
    groups_y = lax.axis_size("sy")
    groups_x = lax.axis_size("sx")
    tables = dft_matrices(LZ, source_site)
    share_z = LZ // groups_y
    table_z = tables[2].reshape(2, LZ, 2, groups_y, share_z)
    blocks = jnp.einsum("nrxyz,rzsjc->jsynxc", fields, table_z, precision=HIGH)
    blocks = blocks.reshape(groups_y, 2 * rows_y, -1)
    width = blocks.shape[2]
    shares = partial.reshape(groups_y, 1, -1)
    shares = jnp.pad(shares, ((0, 0), (0, 0), (0, width - shares.shape[2])))
    share_y = rows_y * groups_y // groups_x
    ready = turn(jnp.concatenate([blocks, shares], 1), source_site[1:2], groups_x, 2 * share_y)
    blocks, gathered = spread_ready(ready)
    blocks = blocks.reshape(groups_x, width // 128, share_y, 2, 128).transpose(0, 2, 3, 1, 4)
    blocks = blocks.reshape(groups_x, share_y, 2, count, rows_x, share_z)
    gathered = gathered[:, : partial.size // groups_y]
    table_x = tables[0].reshape(2, groups_x, rows_x, 2, -1)
    spectrum = jnp.einsum("ibsnxc,sixtk->ntbck", blocks, table_x, precision=HIGH)
    corr = spectrum.reshape(inserts, slices, 2, share_y, -1)
    listed = gathered.reshape(2, inserts, slices, -1)
    return (corr, listed)


def solution(mesh):
    placed = (
        P(None, None, None, None, "sx", "sy"),
        P(None, None, None, None, "sx", "sy"),
        P(),
        P(),
        P(),
    )
    return jax.shard_map(
        body,
        mesh=mesh,
        in_specs=placed,
        out_specs=(P(None, None, None, "sx", "sy"), P()),
        check_vma=False,
    )
```

```python
import functools
import math

import jax
import jax.numpy as jnp
from jax import lax
from jax.experimental import pallas as pl
from jax.experimental.pallas import tpu as pltpu
from jax.sharding import PartitionSpec as P

L = 64
LZ = 64


HIGHEST = lax.Precision.HIGHEST
HIGH = lax.Precision.HIGH


def gamma_matrices(gamma_table):
    inserts = gamma_table.shape[0]
    columns = gamma_table[:, :, 0]
    powers = gamma_table[:, :, 1]
    spin_ids = jnp.arange(4, dtype=jnp.int32)
    matches = (columns[:, :, None] == spin_ids[None, None, :]).astype(jnp.float32)
    unit_re = (powers == 0).astype(jnp.float32) - (powers == 2).astype(jnp.float32)
    unit_im = (powers == 1).astype(jnp.float32) - (powers == 3).astype(jnp.float32)
    return (
        (matches * unit_re[:, :, None]).reshape(inserts, 16),
        (matches * unit_im[:, :, None]).reshape(inserts, 16),
    )


def dft_table(length, anchor):
    wavenum = jnp.arange(length, dtype=jnp.int32)
    offsets = jnp.mod(wavenum - anchor, length)
    phase_index = jnp.mod(offsets[:, None] * wavenum[None, :], length)
    angles = 2.0 * math.pi / length * phase_index.astype(jnp.float32)
    return (jnp.cos(angles), -jnp.sin(angles))


def dft_matrices(length, anchors):
    wavenum = jnp.arange(length, dtype=jnp.int32)
    offsets = jnp.mod(wavenum[None, :] - anchors[:, None], length)
    phase_index = jnp.mod(offsets[:, :, None] * wavenum[None, None, :], length)
    angles = 2.0 * math.pi / length * phase_index.astype(jnp.float32)
    table_re = jnp.cos(angles)
    table_im = -jnp.sin(angles)
    rows_re = jnp.stack([table_re, table_im], 2)
    rows_im = jnp.stack([-table_im, table_re], 2)
    return jnp.stack([rows_re, rows_im], 1)


def swap_kernel(axis, blocks_ref, out_ref, send_sem, recv_sem):
    parts = blocks_ref.shape[0]
    me = lax.axis_index(axis)
    mesh_ids = pl.DeviceIdType.MESH
    barrier = pltpu.get_barrier_semaphore()
    for step in range(1, parts):
        pl.semaphore_signal(
            barrier, 1, device_id={axis: lax.rem(me + step, parts)}, device_id_type=mesh_ids
        )
    pl.semaphore_wait(barrier, parts - 1)

    def copy_to(step):
        peer = lax.rem(me + step, parts)
        return pltpu.make_async_remote_copy(
            src_ref=blocks_ref.at[peer],
            dst_ref=out_ref.at[me],
            send_sem=send_sem.at[step],
            recv_sem=recv_sem.at[step],
            device_id={axis: peer},
            device_id_type=mesh_ids,
        )

    def copy_from(step):
        source = lax.rem(me + parts - step, parts)
        return pltpu.make_async_remote_copy(
            src_ref=blocks_ref.at[source],
            dst_ref=out_ref.at[source],
            send_sem=send_sem.at[step],
            recv_sem=recv_sem.at[step],
            device_id={axis: source},
            device_id_type=mesh_ids,
        )

    @pl.loop(1, parts)
    def _(step):
        copy_to(step).start()

    out_ref[me] = blocks_ref[me]

    @pl.loop(1, parts)
    def _(step):
        copy_to(step).wait_send()

    @pl.loop(1, parts)
    def _(step):
        copy_from(step).wait_recv()


def swap(blocks, axis, ident):
    parts = blocks.shape[0]
    lanes = 128
    shaped = blocks.reshape(parts, -1, lanes)
    out = pl.pallas_call(
        functools.partial(swap_kernel, axis),
        out_shape=jax.ShapeDtypeStruct(shaped.shape, shaped.dtype),
        in_specs=[pl.BlockSpec(memory_space=pltpu.VMEM)],
        out_specs=pl.BlockSpec(memory_space=pltpu.VMEM),
        scratch_shapes=[pltpu.SemaphoreType.DMA((parts,)), pltpu.SemaphoreType.DMA((parts,))],
        compiler_params=pltpu.CompilerParams(collective_id=ident, has_side_effects=True),
    )(shaped)
    return out.reshape(blocks.shape)


def exchange(blocks, extra, axis, ident):
    width = blocks.shape[1]
    got = swap(jnp.concatenate([blocks, extra], 1), axis, ident)
    return got[:, :width], got[:, width:].sum(0)


def turn_kernel(anchor_ref, sent_ref, ready_ref, landed_ref, table_ref, send_sem, recv_sem):
    parts = sent_ref.shape[0]
    depth = sent_ref.shape[1] - 1
    band = ready_ref.shape[1] - 1
    me = lax.axis_index("sy")
    mesh_ids = pl.DeviceIdType.MESH
    barrier = pltpu.get_barrier_semaphore()
    for step in range(1, parts):
        pl.semaphore_signal(
            barrier, 1, device_id={"sy": lax.rem(me + step, parts)}, device_id_type=mesh_ids
        )
    table_ref[...] = turn_table(
        parts * depth // 2, anchor_ref[0], depth // 2, ready_ref.shape[1] // 2, table_ref.shape
    )
    pl.semaphore_wait(barrier, parts - 1)

    def copy_y(step, outgoing):
        peer = lax.rem(me + (step if outgoing else parts - step), parts)
        return pltpu.make_async_remote_copy(
            src_ref=sent_ref.at[peer],
            dst_ref=landed_ref.at[me if outgoing else peer],
            send_sem=send_sem.at[step],
            recv_sem=recv_sem.at[step],
            device_id={"sy": peer},
            device_id_type=mesh_ids,
        )

    @pl.loop(1, parts)
    def _(step):
        copy_y(step, True).start()

    landed_ref[me] = sent_ref[me]

    @pl.loop(1, parts)
    def _(step):
        copy_y(step, True).wait_send()

    @pl.loop(1, parts)
    def _(step):
        copy_y(step, False).wait_recv()

    lanes = ready_ref.shape[2]
    halves = landed_ref.shape[2] // lanes
    rows = band // halves
    block = landed_ref[:, 0:depth, :].reshape(parts * depth, -1)
    share = landed_ref[0, depth : depth + 1, 0:lanes]
    for source in range(1, parts):
        share = share + landed_ref[source, depth : depth + 1, 0:lanes]
    for half in range(halves):
        turned = jnp.dot(
            table_ref[...], block[:, half * lanes : (half + 1) * lanes], precision=HIGH,
            preferred_element_type=jnp.float32,
        )
        for peer in range(ready_ref.shape[0]):
            ready_ref[peer, half * rows : (half + 1) * rows, :] = turned[peer * rows : (peer + 1) * rows]
    for peer in range(ready_ref.shape[0]):
        ready_ref[peer, band : band + 1, :] = share


def turn(sent, anchor, parts_x, band):
    parts_y, rows, width = sent.shape
    vmem = pl.BlockSpec(memory_space=pltpu.VMEM)
    return pl.pallas_call(
        turn_kernel,
        out_shape=jax.ShapeDtypeStruct((parts_x, band * width // 128 + 1, 128), jnp.float32),
        in_specs=[pl.BlockSpec(memory_space=pltpu.SMEM), vmem],
        out_specs=vmem,
        scratch_shapes=[
            pltpu.VMEM((parts_y, rows, width), jnp.float32),
            pltpu.VMEM((parts_y * (rows - 1), parts_y * (rows - 1)), jnp.float32),
            pltpu.SemaphoreType.DMA((parts_y,)),
            pltpu.SemaphoreType.DMA((parts_y,)),
        ],
        compiler_params=pltpu.CompilerParams(collective_id=0, has_side_effects=True),
    )(anchor, sent)


def turn_table(length, anchor, rows_y, share_y, shape):
    line = lax.broadcasted_iota(jnp.int32, shape, 0)
    column = lax.broadcasted_iota(jnp.int32, shape, 1)
    wave = line // 2
    out_part = line % 2
    in_part = (column // rows_y) % 2
    site = (column // (2 * rows_y)) * rows_y + column % rows_y
    offset = (site - anchor + length) % length
    index = (offset * wave + (length // 4) * (out_part - in_part) + length) % length
    return jnp.cos((2.0 * math.pi / length) * index.astype(jnp.float32))


def spread_kernel(blocks_ref, out_ref, gathered_ref, total_ref, b_send, b_recv, c_send, c_recv):
    parts_x = blocks_ref.shape[0]
    parts_y = gathered_ref.shape[0]
    depth = blocks_ref.shape[1] - 1
    me_x = lax.axis_index("sx")
    me_y = lax.axis_index("sy")
    mesh_ids = pl.DeviceIdType.MESH
    barrier = pltpu.get_barrier_semaphore()
    for step in range(1, parts_x):
        pl.semaphore_signal(
            barrier, 1, device_id={"sx": lax.rem(me_x + step, parts_x)}, device_id_type=mesh_ids
        )
    for step in range(1, parts_y):
        pl.semaphore_signal(
            barrier, 1, device_id={"sy": lax.rem(me_y + step, parts_y)}, device_id_type=mesh_ids
        )
    pl.semaphore_wait(barrier, parts_x + parts_y - 2)

    def copy_x(step, outgoing):
        peer = lax.rem(me_x + (step if outgoing else parts_x - step), parts_x)
        return pltpu.make_async_remote_copy(
            src_ref=blocks_ref.at[peer],
            dst_ref=out_ref.at[me_x if outgoing else peer],
            send_sem=b_send.at[step],
            recv_sem=b_recv.at[step],
            device_id={"sx": peer},
            device_id_type=mesh_ids,
        )

    def copy_y(step, outgoing):
        peer = lax.rem(me_y + (step if outgoing else parts_y - step), parts_y)
        return pltpu.make_async_remote_copy(
            src_ref=total_ref,
            dst_ref=gathered_ref.at[me_y if outgoing else peer],
            send_sem=c_send.at[step],
            recv_sem=c_recv.at[step],
            device_id={"sy": peer},
            device_id_type=mesh_ids,
        )

    @pl.loop(1, parts_x)
    def _(step):
        copy_x(step, True).start()

    out_ref[me_x] = blocks_ref[me_x]

    @pl.loop(1, parts_x)
    def _(step):
        copy_x(step, True).wait_send()

    @pl.loop(1, parts_x)
    def _(step):
        copy_x(step, False).wait_recv()

    total = out_ref[0, depth : depth + 1, :]
    for source in range(1, parts_x):
        total = total + out_ref[source, depth : depth + 1, :]
    total_ref[...] = total

    @pl.loop(1, parts_y)
    def _(step):
        copy_y(step, True).start()

    gathered_ref[me_y] = total

    @pl.loop(1, parts_y)
    def _(step):
        copy_y(step, True).wait_send()

    @pl.loop(1, parts_y)
    def _(step):
        copy_y(step, False).wait_recv()


def spread_ready(shaped):
    parts_x = shaped.shape[0]
    parts_y = lax.axis_size("sy")
    vmem = pl.BlockSpec(memory_space=pltpu.VMEM)
    got, gathered = pl.pallas_call(
        spread_kernel,
        out_shape=(
            jax.ShapeDtypeStruct(shaped.shape, shaped.dtype),
            jax.ShapeDtypeStruct((parts_y, 1, shaped.shape[2]), shaped.dtype),
        ),
        in_specs=[vmem],
        out_specs=(vmem, vmem),
        scratch_shapes=[
            pltpu.VMEM((1, shaped.shape[2]), jnp.float32),
            pltpu.SemaphoreType.DMA((parts_x,)),
            pltpu.SemaphoreType.DMA((parts_x,)),
            pltpu.SemaphoreType.DMA((parts_y,)),
            pltpu.SemaphoreType.DMA((parts_y,)),
        ],
        compiler_params=pltpu.CompilerParams(collective_id=1, has_side_effects=True),
    )(shaped)
    return got[:, :-1], gathered[:, 0]


def spread(blocks, share, parts_y):
    parts_x = blocks.shape[0]
    lanes = 128
    width = share.size
    rows = jnp.pad(share, (0, lanes - width)) if width < lanes else share
    shaped = blocks.reshape(parts_x, -1, rows.size)
    shaped = jnp.concatenate(
        [shaped, jnp.broadcast_to(rows.reshape(1, 1, -1), (parts_x, 1, rows.size))], 1
    )
    vmem = pl.BlockSpec(memory_space=pltpu.VMEM)
    got, gathered = pl.pallas_call(
        spread_kernel,
        out_shape=(
            jax.ShapeDtypeStruct(shaped.shape, shaped.dtype),
            jax.ShapeDtypeStruct((parts_y, 1, rows.size), shaped.dtype),
        ),
        in_specs=[vmem],
        out_specs=(vmem, vmem),
        scratch_shapes=[
            pltpu.VMEM((1, rows.size), jnp.float32),
            pltpu.SemaphoreType.DMA((parts_x,)),
            pltpu.SemaphoreType.DMA((parts_x,)),
            pltpu.SemaphoreType.DMA((parts_y,)),
            pltpu.SemaphoreType.DMA((parts_y,)),
        ],
        compiler_params=pltpu.CompilerParams(collective_id=1, has_side_effects=True),
    )(shaped)
    return got[:, :-1].reshape(blocks.shape), gathered[:, 0, :width]


def apply_gammas(mat_re, mat_im, real_part, imag_part):
    extent = real_part.shape
    flat_re = real_part.reshape(extent[0], -1)
    flat_im = imag_part.reshape(extent[0], -1)
    out_re = jnp.dot(mat_re, flat_re, precision=HIGHEST) - jnp.dot(
        mat_im, flat_im, precision=HIGHEST
    )
    out_im = jnp.dot(mat_re, flat_im, precision=HIGHEST) + jnp.dot(
        mat_im, flat_re, precision=HIGHEST
    )
    return (out_re.reshape(extent), out_im.reshape(extent))


def project_sites(fields, source_site, momenta, rows_x, rows_y, length, depth):
    coord_x = lax.axis_index("sx") * rows_x + jnp.arange(rows_x, dtype=jnp.int32) - source_site[0]
    coord_y = lax.axis_index("sy") * rows_y + jnp.arange(rows_y, dtype=jnp.int32) - source_site[1]
    coord_z = jnp.arange(depth, dtype=jnp.int32) - source_site[2]
    part_x = jnp.mod(momenta[:, 0:1] * coord_x[None, :], length)
    part_y = jnp.mod(momenta[:, 1:2] * coord_y[None, :], length)
    part_z = jnp.mod(momenta[:, 2:3] * coord_z[None, :], depth)
    plane = jnp.mod(part_x[:, :, None] + part_y[:, None, :], length).astype(jnp.float32)
    angles = (
        2.0 * math.pi / length * plane[:, :, :, None]
        + 2.0 * math.pi / depth * part_z.astype(jnp.float32)[:, None, None, :]
    )
    angles = angles.reshape(momenta.shape[0], -1)
    cosine = jnp.cos(angles)
    sine = jnp.sin(angles)
    field_re = fields[:, 0].reshape(fields.shape[0], -1)
    field_im = fields[:, 1].reshape(fields.shape[0], -1)
    local_re = jnp.dot(field_re, cosine.T, precision=HIGHEST) + jnp.dot(
        field_im, sine.T, precision=HIGHEST
    )
    local_im = jnp.dot(field_im, cosine.T, precision=HIGHEST) - jnp.dot(
        field_re, sine.T, precision=HIGHEST
    )
    return (local_re, local_im)


def gamma_mix(table_ref, inserts):
    shape = (inserts * 2, 32)
    line = lax.broadcasted_iota(jnp.int32, shape, 0)
    column = lax.broadcasted_iota(jnp.int32, shape, 1)
    out_part = line % 2
    in_part = column % 2
    same = out_part == in_part
    sign = 2 * out_part - 1
    mix = jnp.zeros(shape, jnp.int32)
    for g in range(inserts):
        for s in range(4):
            target = table_ref[g * 8 + s * 2]
            power = table_ref[g * 8 + s * 2 + 1]
            unit_re = jnp.where(power == 0, 1, 0) - jnp.where(power == 2, 1, 0)
            unit_im = jnp.where(power == 1, 1, 0) - jnp.where(power == 3, 1, 0)
            hit = (line // 2 == g) & (column // 2 == s * 4 + target)
            mix = jnp.where(hit, jnp.where(same, unit_re, sign * unit_im), mix)
    return mix.astype(jnp.float32)


def contract_kernel(gamma_ref, forward_ref, backward_ref, out_ref, pair_ref):
    slices = forward_ref.shape[0]
    rows = forward_ref.shape[3]
    mix = gamma_mix(gamma_ref, out_ref.shape[2] // 2)
    for t in range(slices):
        for u in range(4):
            f_re = [forward_ref[t, 0, 3 * u + c].astype(jnp.float32) for c in range(3)]
            f_im = [forward_ref[t, 1, 3 * u + c].astype(jnp.float32) for c in range(3)]
            for s in range(4):
                acc_re = None
                acc_im = None
                for c in range(3):
                    b_re = backward_ref[t, 0, 3 * s + c].astype(jnp.float32)
                    b_im = backward_ref[t, 1, 3 * s + c].astype(jnp.float32)
                    term_re = b_re * f_re[c] + b_im * f_im[c]
                    term_im = b_re * f_im[c] - b_im * f_re[c]
                    acc_re = term_re if acc_re is None else acc_re + term_re
                    acc_im = term_im if acc_im is None else acc_im + term_im
                base = (s * 4 + u) * 2 * rows
                pair_ref[base : base + rows, :] = acc_re
                pair_ref[base + rows : base + 2 * rows, :] = acc_im
        width = pair_ref.shape[0]
        kinds = mix.shape[1]
        lines = out_ref.shape[1] * kinds
        row = lax.broadcasted_iota(jnp.int32, (lines, width), 0)
        col = lax.broadcasted_iota(jnp.int32, (lines, width), 1)
        pick = jnp.logical_and(row % kinds == col // rows, row // kinds == col % out_ref.shape[1])
        summed = jnp.dot(
            pick.astype(jnp.float32), pair_ref[...], precision=HIGH,
            preferred_element_type=jnp.float32,
        )
        for x in range(out_ref.shape[1]):
            out_ref[t, x] = jnp.dot(
                mix, summed[x * kinds : (x + 1) * kinds], precision=HIGH,
                preferred_element_type=jnp.float32,
            )


def contract(forward_prop, backward_prop, gamma_table):
    slices = forward_prop.shape[0]
    rows_x = forward_prop.shape[4]
    sites = forward_prop.shape[5]
    inserts = gamma_table.shape[0]
    forward = forward_prop.reshape(slices, 2, 12, 12 * rows_x, sites)
    backward = backward_prop.reshape(slices, 2, 12, 12 * rows_x, sites)
    out = pl.pallas_call(
        contract_kernel,
        out_shape=jax.ShapeDtypeStruct((slices, rows_x, inserts * 2, sites), jnp.float32),
        in_specs=[pl.BlockSpec(memory_space=pltpu.SMEM)]
        + [pl.BlockSpec(memory_space=pltpu.VMEM)] * 2,
        out_specs=pl.BlockSpec(memory_space=pltpu.VMEM),
        scratch_shapes=[pltpu.VMEM((16 * 2 * 12 * rows_x, sites), jnp.float32)],
    )(gamma_table.reshape(-1), forward, backward)
    return out.reshape(slices, rows_x, inserts, 2, sites).transpose(2, 0, 3, 1, 4)


def body(forward_prop, backward_prop, gamma_table, source_site, momenta):
    slices = forward_prop.shape[0]
    rows_x = forward_prop.shape[4]
    rows_y = backward_prop.shape[5] // LZ
    inserts = gamma_table.shape[0]
    fields = contract(forward_prop, backward_prop, gamma_table)
    fields = fields.reshape(inserts * slices, 2, rows_x, rows_y, LZ)
    count = fields.shape[0]
    local_re, local_im = project_sites(fields, source_site, momenta, rows_x, rows_y, L, LZ)
    partial = jnp.stack([local_re, local_im], 0)
    groups_y = lax.axis_size("sy")
    groups_x = lax.axis_size("sx")
    tables = dft_matrices(LZ, source_site)
    share_z = LZ // groups_y
    table_z = tables[2].reshape(2, LZ, 2, groups_y, share_z)
    blocks = jnp.einsum("nrxyz,rzsjc->jsynxc", fields, table_z, precision=HIGH)
    blocks = blocks.reshape(groups_y, 2 * rows_y, -1)
    width = blocks.shape[2]
    shares = partial.reshape(groups_y, 1, -1)
    shares = jnp.pad(shares, ((0, 0), (0, 0), (0, width - shares.shape[2])))
    share_y = rows_y * groups_y // groups_x
    ready = turn(jnp.concatenate([blocks, shares], 1), source_site[1:2], groups_x, 2 * share_y)
    blocks, gathered = spread_ready(ready)
    blocks = blocks.reshape(groups_x, width // 128, share_y, 2, 128).transpose(0, 2, 3, 1, 4)
    blocks = blocks.reshape(groups_x, share_y, 2, count, rows_x, share_z)
    gathered = gathered[:, : partial.size // groups_y]
    table_x = tables[0].reshape(2, groups_x, rows_x, 2, -1)
    spectrum = jnp.einsum("ibsnxc,sixtk->ntbck", blocks, table_x, precision=HIGH)
    corr = spectrum.reshape(inserts, slices, 2, share_y, -1)
    listed = gathered.reshape(2, inserts, slices, -1)
    return (corr, listed)


def solution(mesh):
    placed = (
        P(None, None, None, None, "sx", "sy"),
        P(None, None, None, None, "sx", "sy"),
        P(),
        P(),
        P(),
    )
    return jax.shard_map(
        body,
        mesh=mesh,
        in_specs=placed,
        out_specs=(P(None, None, None, "sx", "sy"), P()),
        check_vma=False,
    )
```

```python
import functools
import math

import jax
import jax.numpy as jnp
from jax import lax
from jax.experimental import pallas as pl
from jax.experimental.pallas import tpu as pltpu
from jax.sharding import PartitionSpec as P

L = 64
LZ = 64


HIGHEST = lax.Precision.HIGHEST
HIGH = lax.Precision.HIGH


def gamma_matrices(gamma_table):
    inserts = gamma_table.shape[0]
    columns = gamma_table[:, :, 0]
    powers = gamma_table[:, :, 1]
    spin_ids = jnp.arange(4, dtype=jnp.int32)
    matches = (columns[:, :, None] == spin_ids[None, None, :]).astype(jnp.float32)
    unit_re = (powers == 0).astype(jnp.float32) - (powers == 2).astype(jnp.float32)
    unit_im = (powers == 1).astype(jnp.float32) - (powers == 3).astype(jnp.float32)
    return (
        (matches * unit_re[:, :, None]).reshape(inserts, 16),
        (matches * unit_im[:, :, None]).reshape(inserts, 16),
    )


def dft_table(length, anchor):
    wavenum = jnp.arange(length, dtype=jnp.int32)
    offsets = jnp.mod(wavenum - anchor, length)
    phase_index = jnp.mod(offsets[:, None] * wavenum[None, :], length)
    angles = 2.0 * math.pi / length * phase_index.astype(jnp.float32)
    return (jnp.cos(angles), -jnp.sin(angles))


def dft_matrices(length, anchors):
    wavenum = jnp.arange(length, dtype=jnp.int32)
    offsets = jnp.mod(wavenum[None, :] - anchors[:, None], length)
    phase_index = jnp.mod(offsets[:, :, None] * wavenum[None, None, :], length)
    angles = 2.0 * math.pi / length * phase_index.astype(jnp.float32)
    table_re = jnp.cos(angles)
    table_im = -jnp.sin(angles)
    rows_re = jnp.stack([table_re, table_im], 2)
    rows_im = jnp.stack([-table_im, table_re], 2)
    return jnp.stack([rows_re, rows_im], 1)


def swap_kernel(axis, blocks_ref, out_ref, send_sem, recv_sem):
    parts = blocks_ref.shape[0]
    me = lax.axis_index(axis)
    mesh_ids = pl.DeviceIdType.MESH
    barrier = pltpu.get_barrier_semaphore()
    for step in range(1, parts):
        pl.semaphore_signal(
            barrier, 1, device_id={axis: lax.rem(me + step, parts)}, device_id_type=mesh_ids
        )
    pl.semaphore_wait(barrier, parts - 1)

    def copy_to(step):
        peer = lax.rem(me + step, parts)
        return pltpu.make_async_remote_copy(
            src_ref=blocks_ref.at[peer],
            dst_ref=out_ref.at[me],
            send_sem=send_sem.at[step],
            recv_sem=recv_sem.at[step],
            device_id={axis: peer},
            device_id_type=mesh_ids,
        )

    def copy_from(step):
        source = lax.rem(me + parts - step, parts)
        return pltpu.make_async_remote_copy(
            src_ref=blocks_ref.at[source],
            dst_ref=out_ref.at[source],
            send_sem=send_sem.at[step],
            recv_sem=recv_sem.at[step],
            device_id={axis: source},
            device_id_type=mesh_ids,
        )

    @pl.loop(1, parts)
    def _(step):
        copy_to(step).start()

    out_ref[me] = blocks_ref[me]

    @pl.loop(1, parts)
    def _(step):
        copy_to(step).wait_send()

    @pl.loop(1, parts)
    def _(step):
        copy_from(step).wait_recv()


def swap(blocks, axis, ident):
    parts = blocks.shape[0]
    lanes = 128
    shaped = blocks.reshape(parts, -1, lanes)
    out = pl.pallas_call(
        functools.partial(swap_kernel, axis),
        out_shape=jax.ShapeDtypeStruct(shaped.shape, shaped.dtype),
        in_specs=[pl.BlockSpec(memory_space=pltpu.VMEM)],
        out_specs=pl.BlockSpec(memory_space=pltpu.VMEM),
        scratch_shapes=[pltpu.SemaphoreType.DMA((parts,)), pltpu.SemaphoreType.DMA((parts,))],
        compiler_params=pltpu.CompilerParams(collective_id=ident, has_side_effects=True),
    )(shaped)
    return out.reshape(blocks.shape)


def exchange(blocks, extra, axis, ident):
    width = blocks.shape[1]
    got = swap(jnp.concatenate([blocks, extra], 1), axis, ident)
    return got[:, :width], got[:, width:].sum(0)


def turn_kernel(anchor_ref, sent_ref, ready_ref, landed_ref, table_ref, send_sem, recv_sem):
    parts = sent_ref.shape[0]
    depth = sent_ref.shape[1] - 1
    band = ready_ref.shape[1] - 1
    me = lax.axis_index("sy")
    mesh_ids = pl.DeviceIdType.MESH
    barrier = pltpu.get_barrier_semaphore()
    for step in range(1, parts):
        pl.semaphore_signal(
            barrier, 1, device_id={"sy": lax.rem(me + step, parts)}, device_id_type=mesh_ids
        )
    table_ref[...] = turn_table(
        parts * depth // 2, anchor_ref[0], depth // 2, ready_ref.shape[1] // 2, table_ref.shape
    )
    pl.semaphore_wait(barrier, parts - 1)

    def copy_y(step, outgoing):
        peer = lax.rem(me + (step if outgoing else parts - step), parts)
        return pltpu.make_async_remote_copy(
            src_ref=sent_ref.at[peer],
            dst_ref=landed_ref.at[me if outgoing else peer],
            send_sem=send_sem.at[step],
            recv_sem=recv_sem.at[step],
            device_id={"sy": peer},
            device_id_type=mesh_ids,
        )

    @pl.loop(1, parts)
    def _(step):
        copy_y(step, True).start()

    landed_ref[me] = sent_ref[me]

    @pl.loop(1, parts)
    def _(step):
        copy_y(step, True).wait_send()

    @pl.loop(1, parts)
    def _(step):
        copy_y(step, False).wait_recv()

    lanes = ready_ref.shape[2]
    halves = landed_ref.shape[2] // lanes
    rows = band // halves
    block = landed_ref[:, 0:depth, :].reshape(parts * depth, -1)
    share = landed_ref[0, depth : depth + 1, 0:lanes]
    for source in range(1, parts):
        share = share + landed_ref[source, depth : depth + 1, 0:lanes]
    for half in range(halves):
        turned = jnp.dot(
            table_ref[...], block[:, half * lanes : (half + 1) * lanes], precision=HIGH,
            preferred_element_type=jnp.float32,
        )
        for peer in range(ready_ref.shape[0]):
            ready_ref[peer, half * rows : (half + 1) * rows, :] = turned[peer * rows : (peer + 1) * rows]
    for peer in range(ready_ref.shape[0]):
        ready_ref[peer, band : band + 1, :] = share


def turn(sent, anchor, parts_x, band):
    parts_y, rows, width = sent.shape
    vmem = pl.BlockSpec(memory_space=pltpu.VMEM)
    return pl.pallas_call(
        turn_kernel,
        out_shape=jax.ShapeDtypeStruct((parts_x, band * width // 128 + 1, 128), jnp.float32),
        in_specs=[pl.BlockSpec(memory_space=pltpu.SMEM), vmem],
        out_specs=vmem,
        scratch_shapes=[
            pltpu.VMEM((parts_y, rows, width), jnp.float32),
            pltpu.VMEM((parts_y * (rows - 1), parts_y * (rows - 1)), jnp.float32),
            pltpu.SemaphoreType.DMA((parts_y,)),
            pltpu.SemaphoreType.DMA((parts_y,)),
        ],
        compiler_params=pltpu.CompilerParams(collective_id=0, has_side_effects=True),
    )(anchor, sent)


def turn_table(length, anchor, rows_y, share_y, shape):
    line = lax.broadcasted_iota(jnp.int32, shape, 0)
    column = lax.broadcasted_iota(jnp.int32, shape, 1)
    wave = line // 2
    out_part = line % 2
    in_part = (column // rows_y) % 2
    site = (column // (2 * rows_y)) * rows_y + column % rows_y
    offset = (site - anchor + length) % length
    index = (offset * wave + (length // 4) * (out_part - in_part) + length) % length
    return jnp.cos((2.0 * math.pi / length) * index.astype(jnp.float32))


def spread_kernel(blocks_ref, out_ref, gathered_ref, total_ref, b_send, b_recv, c_send, c_recv):
    parts_x = blocks_ref.shape[0]
    parts_y = gathered_ref.shape[0]
    depth = blocks_ref.shape[1] - 1
    me_x = lax.axis_index("sx")
    me_y = lax.axis_index("sy")
    mesh_ids = pl.DeviceIdType.MESH
    barrier = pltpu.get_barrier_semaphore()
    for step in range(1, parts_x):
        pl.semaphore_signal(
            barrier, 1, device_id={"sx": lax.rem(me_x + step, parts_x)}, device_id_type=mesh_ids
        )
    for step in range(1, parts_y):
        pl.semaphore_signal(
            barrier, 1, device_id={"sy": lax.rem(me_y + step, parts_y)}, device_id_type=mesh_ids
        )
    pl.semaphore_wait(barrier, parts_x + parts_y - 2)

    def copy_x(step, outgoing):
        peer = lax.rem(me_x + (step if outgoing else parts_x - step), parts_x)
        return pltpu.make_async_remote_copy(
            src_ref=blocks_ref.at[peer],
            dst_ref=out_ref.at[me_x if outgoing else peer],
            send_sem=b_send.at[step],
            recv_sem=b_recv.at[step],
            device_id={"sx": peer},
            device_id_type=mesh_ids,
        )

    def copy_y(step, outgoing):
        peer = lax.rem(me_y + (step if outgoing else parts_y - step), parts_y)
        return pltpu.make_async_remote_copy(
            src_ref=total_ref.at[0],
            dst_ref=gathered_ref.at[me_y if outgoing else peer],
            send_sem=c_send.at[step],
            recv_sem=c_recv.at[step],
            device_id={"sy": peer},
            device_id_type=mesh_ids,
        )

    @pl.loop(1, parts_x)
    def _(step):
        copy_x(step, True).start()

    out_ref[me_x] = blocks_ref[me_x]

    @pl.loop(1, parts_x)
    def _(step):
        copy_x(step, True).wait_send()

    @pl.loop(1, parts_x)
    def _(step):
        copy_x(step, False).wait_recv()

    total = out_ref[0, depth : depth + 1, :]
    for source in range(1, parts_x):
        total = total + out_ref[source, depth : depth + 1, :]
    total_ref[...] = total

    @pl.loop(1, parts_y)
    def _(step):
        copy_y(step, True).start()

    gathered_ref[pl.ds(me_y, 1), :] = total

    @pl.loop(1, parts_y)
    def _(step):
        copy_y(step, True).wait_send()

    @pl.loop(1, parts_y)
    def _(step):
        copy_y(step, False).wait_recv()


def spread_ready(shaped):
    parts_x = shaped.shape[0]
    parts_y = lax.axis_size("sy")
    vmem = pl.BlockSpec(memory_space=pltpu.VMEM)
    got, gathered = pl.pallas_call(
        spread_kernel,
        out_shape=(
            jax.ShapeDtypeStruct(shaped.shape, shaped.dtype),
            jax.ShapeDtypeStruct((parts_y, shaped.shape[2]), shaped.dtype),
        ),
        in_specs=[vmem],
        out_specs=(vmem, vmem),
        scratch_shapes=[
            pltpu.VMEM((1, shaped.shape[2]), jnp.float32),
            pltpu.SemaphoreType.DMA((parts_x,)),
            pltpu.SemaphoreType.DMA((parts_x,)),
            pltpu.SemaphoreType.DMA((parts_y,)),
            pltpu.SemaphoreType.DMA((parts_y,)),
        ],
        compiler_params=pltpu.CompilerParams(collective_id=1, has_side_effects=True),
    )(shaped)
    return got[:, :-1], gathered


def spread(blocks, share, parts_y):
    parts_x = blocks.shape[0]
    lanes = 128
    width = share.size
    rows = jnp.pad(share, (0, lanes - width)) if width < lanes else share
    shaped = blocks.reshape(parts_x, -1, rows.size)
    shaped = jnp.concatenate(
        [shaped, jnp.broadcast_to(rows.reshape(1, 1, -1), (parts_x, 1, rows.size))], 1
    )
    vmem = pl.BlockSpec(memory_space=pltpu.VMEM)
    got, gathered = pl.pallas_call(
        spread_kernel,
        out_shape=(
            jax.ShapeDtypeStruct(shaped.shape, shaped.dtype),
            jax.ShapeDtypeStruct((parts_y, 1, rows.size), shaped.dtype),
        ),
        in_specs=[vmem],
        out_specs=(vmem, vmem),
        scratch_shapes=[
            pltpu.VMEM((1, rows.size), jnp.float32),
            pltpu.SemaphoreType.DMA((parts_x,)),
            pltpu.SemaphoreType.DMA((parts_x,)),
            pltpu.SemaphoreType.DMA((parts_y,)),
            pltpu.SemaphoreType.DMA((parts_y,)),
        ],
        compiler_params=pltpu.CompilerParams(collective_id=1, has_side_effects=True),
    )(shaped)
    return got[:, :-1].reshape(blocks.shape), gathered[:, 0, :width]


def apply_gammas(mat_re, mat_im, real_part, imag_part):
    extent = real_part.shape
    flat_re = real_part.reshape(extent[0], -1)
    flat_im = imag_part.reshape(extent[0], -1)
    out_re = jnp.dot(mat_re, flat_re, precision=HIGHEST) - jnp.dot(
        mat_im, flat_im, precision=HIGHEST
    )
    out_im = jnp.dot(mat_re, flat_im, precision=HIGHEST) + jnp.dot(
        mat_im, flat_re, precision=HIGHEST
    )
    return (out_re.reshape(extent), out_im.reshape(extent))


def project_sites(fields, source_site, momenta, rows_x, rows_y, length, depth):
    coord_x = lax.axis_index("sx") * rows_x + jnp.arange(rows_x, dtype=jnp.int32) - source_site[0]
    coord_y = lax.axis_index("sy") * rows_y + jnp.arange(rows_y, dtype=jnp.int32) - source_site[1]
    coord_z = jnp.arange(depth, dtype=jnp.int32) - source_site[2]
    part_x = jnp.mod(momenta[:, 0:1] * coord_x[None, :], length)
    part_y = jnp.mod(momenta[:, 1:2] * coord_y[None, :], length)
    part_z = jnp.mod(momenta[:, 2:3] * coord_z[None, :], depth)
    plane = jnp.mod(part_x[:, :, None] + part_y[:, None, :], length).astype(jnp.float32)
    angles = (
        2.0 * math.pi / length * plane[:, :, :, None]
        + 2.0 * math.pi / depth * part_z.astype(jnp.float32)[:, None, None, :]
    )
    angles = angles.reshape(momenta.shape[0], -1)
    cosine = jnp.cos(angles)
    sine = jnp.sin(angles)
    field_re = fields[:, 0].reshape(fields.shape[0], -1)
    field_im = fields[:, 1].reshape(fields.shape[0], -1)
    local_re = jnp.dot(field_re, cosine.T, precision=HIGHEST) + jnp.dot(
        field_im, sine.T, precision=HIGHEST
    )
    local_im = jnp.dot(field_im, cosine.T, precision=HIGHEST) - jnp.dot(
        field_re, sine.T, precision=HIGHEST
    )
    return (local_re, local_im)


def gamma_mix(table_ref, inserts):
    shape = (inserts * 2, 32)
    line = lax.broadcasted_iota(jnp.int32, shape, 0)
    column = lax.broadcasted_iota(jnp.int32, shape, 1)
    out_part = line % 2
    in_part = column % 2
    same = out_part == in_part
    sign = 2 * out_part - 1
    mix = jnp.zeros(shape, jnp.int32)
    for g in range(inserts):
        for s in range(4):
            target = table_ref[g * 8 + s * 2]
            power = table_ref[g * 8 + s * 2 + 1]
            unit_re = jnp.where(power == 0, 1, 0) - jnp.where(power == 2, 1, 0)
            unit_im = jnp.where(power == 1, 1, 0) - jnp.where(power == 3, 1, 0)
            hit = (line // 2 == g) & (column // 2 == s * 4 + target)
            mix = jnp.where(hit, jnp.where(same, unit_re, sign * unit_im), mix)
    return mix.astype(jnp.float32)


def contract_kernel(gamma_ref, forward_ref, backward_ref, out_ref, pair_ref):
    slices = forward_ref.shape[0]
    rows = forward_ref.shape[3]
    mix = gamma_mix(gamma_ref, out_ref.shape[2] // 2)
    for t in range(slices):
        for u in range(4):
            f_re = [forward_ref[t, 0, 3 * u + c].astype(jnp.float32) for c in range(3)]
            f_im = [forward_ref[t, 1, 3 * u + c].astype(jnp.float32) for c in range(3)]
            for s in range(4):
                acc_re = None
                acc_im = None
                for c in range(3):
                    b_re = backward_ref[t, 0, 3 * s + c].astype(jnp.float32)
                    b_im = backward_ref[t, 1, 3 * s + c].astype(jnp.float32)
                    term_re = b_re * f_re[c] + b_im * f_im[c]
                    term_im = b_re * f_im[c] - b_im * f_re[c]
                    acc_re = term_re if acc_re is None else acc_re + term_re
                    acc_im = term_im if acc_im is None else acc_im + term_im
                base = (s * 4 + u) * 2 * rows
                pair_ref[base : base + rows, :] = acc_re
                pair_ref[base + rows : base + 2 * rows, :] = acc_im
        width = pair_ref.shape[0]
        kinds = mix.shape[1]
        lines = out_ref.shape[1] * kinds
        row = lax.broadcasted_iota(jnp.int32, (lines, width), 0)
        col = lax.broadcasted_iota(jnp.int32, (lines, width), 1)
        pick = jnp.logical_and(row % kinds == col // rows, row // kinds == col % out_ref.shape[1])
        summed = jnp.dot(
            pick.astype(jnp.float32), pair_ref[...], precision=HIGH,
            preferred_element_type=jnp.float32,
        )
        for x in range(out_ref.shape[1]):
            out_ref[t, x] = jnp.dot(
                mix, summed[x * kinds : (x + 1) * kinds], precision=HIGH,
                preferred_element_type=jnp.float32,
            )


def contract(forward_prop, backward_prop, gamma_table):
    slices = forward_prop.shape[0]
    rows_x = forward_prop.shape[4]
    sites = forward_prop.shape[5]
    inserts = gamma_table.shape[0]
    forward = forward_prop.reshape(slices, 2, 12, 12 * rows_x, sites)
    backward = backward_prop.reshape(slices, 2, 12, 12 * rows_x, sites)
    out = pl.pallas_call(
        contract_kernel,
        out_shape=jax.ShapeDtypeStruct((slices, rows_x, inserts * 2, sites), jnp.float32),
        in_specs=[pl.BlockSpec(memory_space=pltpu.SMEM)]
        + [pl.BlockSpec(memory_space=pltpu.VMEM)] * 2,
        out_specs=pl.BlockSpec(memory_space=pltpu.VMEM),
        scratch_shapes=[pltpu.VMEM((16 * 2 * 12 * rows_x, sites), jnp.float32)],
    )(gamma_table.reshape(-1), forward, backward)
    return out.reshape(slices, rows_x, inserts, 2, sites).transpose(2, 0, 3, 1, 4)


def body(forward_prop, backward_prop, gamma_table, source_site, momenta):
    slices = forward_prop.shape[0]
    rows_x = forward_prop.shape[4]
    rows_y = backward_prop.shape[5] // LZ
    inserts = gamma_table.shape[0]
    fields = contract(forward_prop, backward_prop, gamma_table)
    fields = fields.reshape(inserts * slices, 2, rows_x, rows_y, LZ)
    count = fields.shape[0]
    local_re, local_im = project_sites(fields, source_site, momenta, rows_x, rows_y, L, LZ)
    partial = jnp.stack([local_re, local_im], 0)
    groups_y = lax.axis_size("sy")
    groups_x = lax.axis_size("sx")
    tables = dft_matrices(LZ, source_site)
    share_z = LZ // groups_y
    table_z = tables[2].reshape(2, LZ, 2, groups_y, share_z)
    blocks = jnp.einsum("nrxyz,rzsjc->jsynxc", fields, table_z, precision=HIGH)
    blocks = blocks.reshape(groups_y, 2 * rows_y, -1)
    width = blocks.shape[2]
    shares = partial.reshape(groups_y, 1, -1)
    shares = jnp.pad(shares, ((0, 0), (0, 0), (0, width - shares.shape[2])))
    share_y = rows_y * groups_y // groups_x
    ready = turn(jnp.concatenate([blocks, shares], 1), source_site[1:2], groups_x, 2 * share_y)
    blocks, gathered = spread_ready(ready)
    blocks = blocks.reshape(groups_x, width // 128, share_y, 2, 128).transpose(0, 2, 3, 1, 4)
    blocks = blocks.reshape(groups_x, share_y, 2, count, rows_x, share_z)
    gathered = gathered[:, : partial.size // groups_y]
    table_x = tables[0].reshape(2, groups_x, rows_x, 2, -1)
    spectrum = jnp.einsum("ibsnxc,sixtk->ntbck", blocks, table_x, precision=HIGH)
    corr = spectrum.reshape(inserts, slices, 2, share_y, -1)
    listed = gathered.reshape(2, inserts, slices, -1)
    return (corr, listed)


def solution(mesh):
    placed = (
        P(None, None, None, None, "sx", "sy"),
        P(None, None, None, None, "sx", "sy"),
        P(),
        P(),
        P(),
    )
    return jax.shard_map(
        body,
        mesh=mesh,
        in_specs=placed,
        out_specs=(P(None, None, None, "sx", "sy"), P()),
        check_vma=False,
    )
```

```python
import functools
import math

import jax
import jax.numpy as jnp
from jax import lax
from jax.experimental import pallas as pl
from jax.experimental.pallas import tpu as pltpu
from jax.sharding import PartitionSpec as P

L = 64
LZ = 64


HIGHEST = lax.Precision.HIGHEST
HIGH = lax.Precision.HIGH


def gamma_matrices(gamma_table):
    inserts = gamma_table.shape[0]
    columns = gamma_table[:, :, 0]
    powers = gamma_table[:, :, 1]
    spin_ids = jnp.arange(4, dtype=jnp.int32)
    matches = (columns[:, :, None] == spin_ids[None, None, :]).astype(jnp.float32)
    unit_re = (powers == 0).astype(jnp.float32) - (powers == 2).astype(jnp.float32)
    unit_im = (powers == 1).astype(jnp.float32) - (powers == 3).astype(jnp.float32)
    return (
        (matches * unit_re[:, :, None]).reshape(inserts, 16),
        (matches * unit_im[:, :, None]).reshape(inserts, 16),
    )


def dft_table(length, anchor):
    wavenum = jnp.arange(length, dtype=jnp.int32)
    offsets = jnp.mod(wavenum - anchor, length)
    phase_index = jnp.mod(offsets[:, None] * wavenum[None, :], length)
    angles = 2.0 * math.pi / length * phase_index.astype(jnp.float32)
    return (jnp.cos(angles), -jnp.sin(angles))


def dft_matrices(length, anchors):
    wavenum = jnp.arange(length, dtype=jnp.int32)
    offsets = jnp.mod(wavenum[None, :] - anchors[:, None], length)
    phase_index = jnp.mod(offsets[:, :, None] * wavenum[None, None, :], length)
    angles = 2.0 * math.pi / length * phase_index.astype(jnp.float32)
    table_re = jnp.cos(angles)
    table_im = -jnp.sin(angles)
    rows_re = jnp.stack([table_re, table_im], 2)
    rows_im = jnp.stack([-table_im, table_re], 2)
    return jnp.stack([rows_re, rows_im], 1)


def swap_kernel(axis, blocks_ref, out_ref, send_sem, recv_sem):
    parts = blocks_ref.shape[0]
    me = lax.axis_index(axis)
    mesh_ids = pl.DeviceIdType.MESH
    barrier = pltpu.get_barrier_semaphore()
    for step in range(1, parts):
        pl.semaphore_signal(
            barrier, 1, device_id={axis: lax.rem(me + step, parts)}, device_id_type=mesh_ids
        )
    pl.semaphore_wait(barrier, parts - 1)

    def copy_to(step):
        peer = lax.rem(me + step, parts)
        return pltpu.make_async_remote_copy(
            src_ref=blocks_ref.at[peer],
            dst_ref=out_ref.at[me],
            send_sem=send_sem.at[step],
            recv_sem=recv_sem.at[step],
            device_id={axis: peer},
            device_id_type=mesh_ids,
        )

    def copy_from(step):
        source = lax.rem(me + parts - step, parts)
        return pltpu.make_async_remote_copy(
            src_ref=blocks_ref.at[source],
            dst_ref=out_ref.at[source],
            send_sem=send_sem.at[step],
            recv_sem=recv_sem.at[step],
            device_id={axis: source},
            device_id_type=mesh_ids,
        )

    @pl.loop(1, parts)
    def _(step):
        copy_to(step).start()

    out_ref[me] = blocks_ref[me]

    @pl.loop(1, parts)
    def _(step):
        copy_to(step).wait_send()

    @pl.loop(1, parts)
    def _(step):
        copy_from(step).wait_recv()


def swap(blocks, axis, ident):
    parts = blocks.shape[0]
    lanes = 128
    shaped = blocks.reshape(parts, -1, lanes)
    out = pl.pallas_call(
        functools.partial(swap_kernel, axis),
        out_shape=jax.ShapeDtypeStruct(shaped.shape, shaped.dtype),
        in_specs=[pl.BlockSpec(memory_space=pltpu.VMEM)],
        out_specs=pl.BlockSpec(memory_space=pltpu.VMEM),
        scratch_shapes=[pltpu.SemaphoreType.DMA((parts,)), pltpu.SemaphoreType.DMA((parts,))],
        compiler_params=pltpu.CompilerParams(collective_id=ident, has_side_effects=True),
    )(shaped)
    return out.reshape(blocks.shape)


def exchange(blocks, extra, axis, ident):
    width = blocks.shape[1]
    got = swap(jnp.concatenate([blocks, extra], 1), axis, ident)
    return got[:, :width], got[:, width:].sum(0)


def turn_kernel(anchor_ref, sent_ref, ready_ref, landed_ref, table_ref, send_sem, recv_sem):
    parts = sent_ref.shape[0]
    depth = sent_ref.shape[1] - 1
    band = ready_ref.shape[1] - 1
    me = lax.axis_index("sy")
    mesh_ids = pl.DeviceIdType.MESH
    barrier = pltpu.get_barrier_semaphore()
    for step in range(1, parts):
        pl.semaphore_signal(
            barrier, 1, device_id={"sy": lax.rem(me + step, parts)}, device_id_type=mesh_ids
        )
    table_ref[...] = turn_table(
        parts * depth // 2, anchor_ref[0], depth // 2, ready_ref.shape[1] // 2, table_ref.shape
    )
    pl.semaphore_wait(barrier, parts - 1)

    def copy_y(step, outgoing):
        peer = lax.rem(me + (step if outgoing else parts - step), parts)
        return pltpu.make_async_remote_copy(
            src_ref=sent_ref.at[peer],
            dst_ref=landed_ref.at[me if outgoing else peer],
            send_sem=send_sem.at[step],
            recv_sem=recv_sem.at[step],
            device_id={"sy": peer},
            device_id_type=mesh_ids,
        )

    @pl.loop(1, parts)
    def _(step):
        copy_y(step, True).start()

    landed_ref[me] = sent_ref[me]

    @pl.loop(1, parts)
    def _(step):
        copy_y(step, True).wait_send()

    @pl.loop(1, parts)
    def _(step):
        copy_y(step, False).wait_recv()

    lanes = ready_ref.shape[2]
    halves = landed_ref.shape[2] // lanes
    rows = band // halves
    block = landed_ref[:, 0:depth, :].reshape(parts * depth, -1)
    share = landed_ref[0, depth : depth + 1, 0:lanes]
    for source in range(1, parts):
        share = share + landed_ref[source, depth : depth + 1, 0:lanes]
    for half in range(halves):
        turned = jnp.dot(
            table_ref[...], block[:, half * lanes : (half + 1) * lanes], precision=HIGH,
            preferred_element_type=jnp.float32,
        )
        for peer in range(ready_ref.shape[0]):
            ready_ref[peer, half * rows : (half + 1) * rows, :] = turned[peer * rows : (peer + 1) * rows]
    for peer in range(ready_ref.shape[0]):
        ready_ref[peer, band : band + 1, :] = share


def turn(sent, anchor, parts_x, band):
    parts_y, rows, width = sent.shape
    vmem = pl.BlockSpec(memory_space=pltpu.VMEM)
    return pl.pallas_call(
        turn_kernel,
        out_shape=jax.ShapeDtypeStruct((parts_x, band * width // 128 + 1, 128), jnp.float32),
        in_specs=[pl.BlockSpec(memory_space=pltpu.SMEM), vmem],
        out_specs=vmem,
        scratch_shapes=[
            pltpu.VMEM((parts_y, rows, width), jnp.float32),
            pltpu.VMEM((parts_y * (rows - 1), parts_y * (rows - 1)), jnp.float32),
            pltpu.SemaphoreType.DMA((parts_y,)),
            pltpu.SemaphoreType.DMA((parts_y,)),
        ],
        compiler_params=pltpu.CompilerParams(collective_id=0, has_side_effects=True),
    )(anchor, sent)


def turn_table(length, anchor, rows_y, share_y, shape):
    line = lax.broadcasted_iota(jnp.int32, shape, 0)
    column = lax.broadcasted_iota(jnp.int32, shape, 1)
    wave = line // 2
    out_part = line % 2
    in_part = (column // rows_y) % 2
    site = (column // (2 * rows_y)) * rows_y + column % rows_y
    offset = (site - anchor + length) % length
    index = (offset * wave + (length // 4) * (out_part - in_part) + length) % length
    return jnp.cos((2.0 * math.pi / length) * index.astype(jnp.float32))


def spread_kernel(blocks_ref, out_ref, gathered_ref, total_ref, b_send, b_recv, c_send, c_recv):
    parts_x = blocks_ref.shape[0]
    parts_y = gathered_ref.shape[0]
    depth = blocks_ref.shape[1] - 1
    me_x = lax.axis_index("sx")
    me_y = lax.axis_index("sy")
    mesh_ids = pl.DeviceIdType.MESH
    barrier = pltpu.get_barrier_semaphore()
    for step in range(1, parts_x):
        pl.semaphore_signal(
            barrier, 1, device_id={"sx": lax.rem(me_x + step, parts_x)}, device_id_type=mesh_ids
        )
    for step in range(1, parts_y):
        pl.semaphore_signal(
            barrier, 1, device_id={"sy": lax.rem(me_y + step, parts_y)}, device_id_type=mesh_ids
        )
    pl.semaphore_wait(barrier, parts_x + parts_y - 2)

    def copy_x(step, outgoing):
        peer = lax.rem(me_x + (step if outgoing else parts_x - step), parts_x)
        return pltpu.make_async_remote_copy(
            src_ref=blocks_ref.at[peer],
            dst_ref=out_ref.at[me_x if outgoing else peer],
            send_sem=b_send.at[step],
            recv_sem=b_recv.at[step],
            device_id={"sx": peer},
            device_id_type=mesh_ids,
        )

    def copy_y(step, outgoing):
        peer = lax.rem(me_y + (step if outgoing else parts_y - step), parts_y)
        return pltpu.make_async_remote_copy(
            src_ref=total_ref.at[0],
            dst_ref=gathered_ref.at[me_y if outgoing else peer],
            send_sem=c_send.at[step],
            recv_sem=c_recv.at[step],
            device_id={"sy": peer},
            device_id_type=mesh_ids,
        )

    @pl.loop(1, parts_x)
    def _(step):
        copy_x(step, True).start()

    out_ref[me_x] = blocks_ref[me_x]

    @pl.loop(1, parts_x)
    def _(step):
        copy_x(step, True).wait_send()

    @pl.loop(1, parts_x)
    def _(step):
        copy_x(step, False).wait_recv()

    total = out_ref[0, depth : depth + 1, :]
    for source in range(1, parts_x):
        total = total + out_ref[source, depth : depth + 1, :]
    total_ref[...] = total

    @pl.loop(1, parts_y)
    def _(step):
        copy_y(step, True).start()

    gathered_ref[pl.ds(me_y, 1), :] = total

    @pl.loop(1, parts_y)
    def _(step):
        copy_y(step, True).wait_send()

    @pl.loop(1, parts_y)
    def _(step):
        copy_y(step, False).wait_recv()


def spread_ready(shaped):
    parts_x = shaped.shape[0]
    parts_y = lax.axis_size("sy")
    vmem = pl.BlockSpec(memory_space=pltpu.VMEM)
    got, gathered = pl.pallas_call(
        spread_kernel,
        out_shape=(
            jax.ShapeDtypeStruct(shaped.shape, shaped.dtype),
            jax.ShapeDtypeStruct((parts_y, shaped.shape[2]), shaped.dtype),
        ),
        in_specs=[vmem],
        out_specs=(vmem, vmem),
        scratch_shapes=[
            pltpu.VMEM((1, shaped.shape[2]), jnp.float32),
            pltpu.SemaphoreType.DMA((parts_x,)),
            pltpu.SemaphoreType.DMA((parts_x,)),
            pltpu.SemaphoreType.DMA((parts_y,)),
            pltpu.SemaphoreType.DMA((parts_y,)),
        ],
        compiler_params=pltpu.CompilerParams(collective_id=1, has_side_effects=True),
    )(shaped)
    return got[:, :-1], gathered


def spread(blocks, share, parts_y):
    parts_x = blocks.shape[0]
    lanes = 128
    width = share.size
    rows = jnp.pad(share, (0, lanes - width)) if width < lanes else share
    shaped = blocks.reshape(parts_x, -1, rows.size)
    shaped = jnp.concatenate(
        [shaped, jnp.broadcast_to(rows.reshape(1, 1, -1), (parts_x, 1, rows.size))], 1
    )
    vmem = pl.BlockSpec(memory_space=pltpu.VMEM)
    got, gathered = pl.pallas_call(
        spread_kernel,
        out_shape=(
            jax.ShapeDtypeStruct(shaped.shape, shaped.dtype),
            jax.ShapeDtypeStruct((parts_y, 1, rows.size), shaped.dtype),
        ),
        in_specs=[vmem],
        out_specs=(vmem, vmem),
        scratch_shapes=[
            pltpu.VMEM((1, rows.size), jnp.float32),
            pltpu.SemaphoreType.DMA((parts_x,)),
            pltpu.SemaphoreType.DMA((parts_x,)),
            pltpu.SemaphoreType.DMA((parts_y,)),
            pltpu.SemaphoreType.DMA((parts_y,)),
        ],
        compiler_params=pltpu.CompilerParams(collective_id=1, has_side_effects=True),
    )(shaped)
    return got[:, :-1].reshape(blocks.shape), gathered[:, 0, :width]


def apply_gammas(mat_re, mat_im, real_part, imag_part):
    extent = real_part.shape
    flat_re = real_part.reshape(extent[0], -1)
    flat_im = imag_part.reshape(extent[0], -1)
    out_re = jnp.dot(mat_re, flat_re, precision=HIGHEST) - jnp.dot(
        mat_im, flat_im, precision=HIGHEST
    )
    out_im = jnp.dot(mat_re, flat_im, precision=HIGHEST) + jnp.dot(
        mat_im, flat_re, precision=HIGHEST
    )
    return (out_re.reshape(extent), out_im.reshape(extent))


def project_sites(fields, source_site, momenta, rows_x, rows_y, length, depth):
    coord_x = lax.axis_index("sx") * rows_x + jnp.arange(rows_x, dtype=jnp.int32) - source_site[0]
    coord_y = lax.axis_index("sy") * rows_y + jnp.arange(rows_y, dtype=jnp.int32) - source_site[1]
    coord_z = jnp.arange(depth, dtype=jnp.int32) - source_site[2]
    part_x = jnp.mod(momenta[:, 0:1] * coord_x[None, :], length)
    part_y = jnp.mod(momenta[:, 1:2] * coord_y[None, :], length)
    part_z = jnp.mod(momenta[:, 2:3] * coord_z[None, :], depth)
    plane = jnp.mod(part_x[:, :, None] + part_y[:, None, :], length).astype(jnp.float32)
    angles = (
        2.0 * math.pi / length * plane[:, :, :, None]
        + 2.0 * math.pi / depth * part_z.astype(jnp.float32)[:, None, None, :]
    )
    cosine = jnp.cos(angles)
    sine = jnp.sin(angles)
    field_re = fields[:, :, :, 0]
    field_im = fields[:, :, :, 1]
    pattern = "txgyz,mxyz->gtm"
    local_re = jnp.einsum(pattern, field_re, cosine, precision=HIGHEST) + jnp.einsum(
        pattern, field_im, sine, precision=HIGHEST
    )
    local_im = jnp.einsum(pattern, field_im, cosine, precision=HIGHEST) - jnp.einsum(
        pattern, field_re, sine, precision=HIGHEST
    )
    count = local_re.shape[0] * local_re.shape[1]
    return (local_re.reshape(count, -1), local_im.reshape(count, -1))


def gamma_mix(table_ref, inserts):
    shape = (inserts * 2, 32)
    line = lax.broadcasted_iota(jnp.int32, shape, 0)
    column = lax.broadcasted_iota(jnp.int32, shape, 1)
    out_part = line % 2
    in_part = column % 2
    same = out_part == in_part
    sign = 2 * out_part - 1
    mix = jnp.zeros(shape, jnp.int32)
    for g in range(inserts):
        for s in range(4):
            target = table_ref[g * 8 + s * 2]
            power = table_ref[g * 8 + s * 2 + 1]
            unit_re = jnp.where(power == 0, 1, 0) - jnp.where(power == 2, 1, 0)
            unit_im = jnp.where(power == 1, 1, 0) - jnp.where(power == 3, 1, 0)
            hit = (line // 2 == g) & (column // 2 == s * 4 + target)
            mix = jnp.where(hit, jnp.where(same, unit_re, sign * unit_im), mix)
    return mix.astype(jnp.float32)


def contract_kernel(gamma_ref, forward_ref, backward_ref, out_ref, pair_ref):
    slices = forward_ref.shape[0]
    rows = forward_ref.shape[3]
    mix = gamma_mix(gamma_ref, out_ref.shape[2] // 2)
    for t in range(slices):
        for u in range(4):
            f_re = [forward_ref[t, 0, 3 * u + c].astype(jnp.float32) for c in range(3)]
            f_im = [forward_ref[t, 1, 3 * u + c].astype(jnp.float32) for c in range(3)]
            for s in range(4):
                acc_re = None
                acc_im = None
                for c in range(3):
                    b_re = backward_ref[t, 0, 3 * s + c].astype(jnp.float32)
                    b_im = backward_ref[t, 1, 3 * s + c].astype(jnp.float32)
                    term_re = b_re * f_re[c] + b_im * f_im[c]
                    term_im = b_re * f_im[c] - b_im * f_re[c]
                    acc_re = term_re if acc_re is None else acc_re + term_re
                    acc_im = term_im if acc_im is None else acc_im + term_im
                base = (s * 4 + u) * 2 * rows
                pair_ref[base : base + rows, :] = acc_re
                pair_ref[base + rows : base + 2 * rows, :] = acc_im
        width = pair_ref.shape[0]
        kinds = mix.shape[1]
        lines = out_ref.shape[1] * kinds
        row = lax.broadcasted_iota(jnp.int32, (lines, width), 0)
        col = lax.broadcasted_iota(jnp.int32, (lines, width), 1)
        pick = jnp.logical_and(row % kinds == col // rows, row // kinds == col % out_ref.shape[1])
        summed = jnp.dot(
            pick.astype(jnp.float32), pair_ref[...], precision=HIGH,
            preferred_element_type=jnp.float32,
        )
        for x in range(out_ref.shape[1]):
            out_ref[t, x] = jnp.dot(
                mix, summed[x * kinds : (x + 1) * kinds], precision=HIGH,
                preferred_element_type=jnp.float32,
            )


def contract(forward_prop, backward_prop, gamma_table):
    slices = forward_prop.shape[0]
    rows_x = forward_prop.shape[4]
    sites = forward_prop.shape[5]
    inserts = gamma_table.shape[0]
    forward = forward_prop.reshape(slices, 2, 12, 12 * rows_x, sites)
    backward = backward_prop.reshape(slices, 2, 12, 12 * rows_x, sites)
    out = pl.pallas_call(
        contract_kernel,
        out_shape=jax.ShapeDtypeStruct((slices, rows_x, inserts * 2, sites), jnp.float32),
        in_specs=[pl.BlockSpec(memory_space=pltpu.SMEM)]
        + [pl.BlockSpec(memory_space=pltpu.VMEM)] * 2,
        out_specs=pl.BlockSpec(memory_space=pltpu.VMEM),
        scratch_shapes=[pltpu.VMEM((16 * 2 * 12 * rows_x, sites), jnp.float32)],
    )(gamma_table.reshape(-1), forward, backward)
    return out.reshape(slices, rows_x, inserts, 2, sites)


def body(forward_prop, backward_prop, gamma_table, source_site, momenta):
    slices = forward_prop.shape[0]
    rows_x = forward_prop.shape[4]
    rows_y = backward_prop.shape[5] // LZ
    inserts = gamma_table.shape[0]
    fields = contract(forward_prop, backward_prop, gamma_table)
    fields = fields.reshape(slices, rows_x, inserts, 2, rows_y, LZ)
    count = inserts * slices
    local_re, local_im = project_sites(fields, source_site, momenta, rows_x, rows_y, L, LZ)
    partial = jnp.stack([local_re, local_im], 0)
    groups_y = lax.axis_size("sy")
    groups_x = lax.axis_size("sx")
    tables = dft_matrices(LZ, source_site)
    share_z = LZ // groups_y
    table_z = tables[2].reshape(2, LZ, 2, groups_y, share_z)
    blocks = jnp.einsum("txgryz,rzsjc->jsygtxc", fields, table_z, precision=HIGH)
    blocks = blocks.reshape(groups_y, 2 * rows_y, -1)
    width = blocks.shape[2]
    shares = partial.reshape(groups_y, 1, -1)
    shares = jnp.pad(shares, ((0, 0), (0, 0), (0, width - shares.shape[2])))
    share_y = rows_y * groups_y // groups_x
    ready = turn(jnp.concatenate([blocks, shares], 1), source_site[1:2], groups_x, 2 * share_y)
    blocks, gathered = spread_ready(ready)
    blocks = blocks.reshape(groups_x, width // 128, share_y, 2, 128).transpose(0, 2, 3, 1, 4)
    blocks = blocks.reshape(groups_x, share_y, 2, count, rows_x, share_z)
    gathered = gathered[:, : partial.size // groups_y]
    table_x = tables[0].reshape(2, groups_x, rows_x, 2, -1)
    spectrum = jnp.einsum("ibsnxc,sixtk->ntbck", blocks, table_x, precision=HIGH)
    corr = spectrum.reshape(inserts, slices, 2, share_y, -1)
    listed = gathered.reshape(2, inserts, slices, -1)
    return (corr, listed)


def solution(mesh):
    placed = (
        P(None, None, None, None, "sx", "sy"),
        P(None, None, None, None, "sx", "sy"),
        P(),
        P(),
        P(),
    )
    return jax.shard_map(
        body,
        mesh=mesh,
        in_specs=placed,
        out_specs=(P(None, None, None, "sx", "sy"), P()),
        check_vma=False,
    )
```

```python
import functools
import math

import jax
import jax.numpy as jnp
from jax import lax
from jax.experimental import pallas as pl
from jax.experimental.pallas import tpu as pltpu
from jax.sharding import PartitionSpec as P

L = 64
LZ = 64


HIGHEST = lax.Precision.HIGHEST
HIGH = lax.Precision.HIGH


def gamma_matrices(gamma_table):
    inserts = gamma_table.shape[0]
    columns = gamma_table[:, :, 0]
    powers = gamma_table[:, :, 1]
    spin_ids = jnp.arange(4, dtype=jnp.int32)
    matches = (columns[:, :, None] == spin_ids[None, None, :]).astype(jnp.float32)
    unit_re = (powers == 0).astype(jnp.float32) - (powers == 2).astype(jnp.float32)
    unit_im = (powers == 1).astype(jnp.float32) - (powers == 3).astype(jnp.float32)
    return (
        (matches * unit_re[:, :, None]).reshape(inserts, 16),
        (matches * unit_im[:, :, None]).reshape(inserts, 16),
    )


def dft_table(length, anchor):
    wavenum = jnp.arange(length, dtype=jnp.int32)
    offsets = jnp.mod(wavenum - anchor, length)
    phase_index = jnp.mod(offsets[:, None] * wavenum[None, :], length)
    angles = 2.0 * math.pi / length * phase_index.astype(jnp.float32)
    return (jnp.cos(angles), -jnp.sin(angles))


def dft_matrices(length, anchors):
    wavenum = jnp.arange(length, dtype=jnp.int32)
    offsets = jnp.mod(wavenum[None, :] - anchors[:, None], length)
    phase_index = jnp.mod(offsets[:, :, None] * wavenum[None, None, :], length)
    angles = 2.0 * math.pi / length * phase_index.astype(jnp.float32)
    table_re = jnp.cos(angles)
    table_im = -jnp.sin(angles)
    rows_re = jnp.stack([table_re, table_im], 2)
    rows_im = jnp.stack([-table_im, table_re], 2)
    return jnp.stack([rows_re, rows_im], 1)


def swap_kernel(axis, blocks_ref, out_ref, send_sem, recv_sem):
    parts = blocks_ref.shape[0]
    me = lax.axis_index(axis)
    mesh_ids = pl.DeviceIdType.MESH
    barrier = pltpu.get_barrier_semaphore()
    for step in range(1, parts):
        pl.semaphore_signal(
            barrier, 1, device_id={axis: lax.rem(me + step, parts)}, device_id_type=mesh_ids
        )
    pl.semaphore_wait(barrier, parts - 1)

    def copy_to(step):
        peer = lax.rem(me + step, parts)
        return pltpu.make_async_remote_copy(
            src_ref=blocks_ref.at[peer],
            dst_ref=out_ref.at[me],
            send_sem=send_sem.at[step],
            recv_sem=recv_sem.at[step],
            device_id={axis: peer},
            device_id_type=mesh_ids,
        )

    def copy_from(step):
        source = lax.rem(me + parts - step, parts)
        return pltpu.make_async_remote_copy(
            src_ref=blocks_ref.at[source],
            dst_ref=out_ref.at[source],
            send_sem=send_sem.at[step],
            recv_sem=recv_sem.at[step],
            device_id={axis: source},
            device_id_type=mesh_ids,
        )

    @pl.loop(1, parts)
    def _(step):
        copy_to(step).start()

    out_ref[me] = blocks_ref[me]

    @pl.loop(1, parts)
    def _(step):
        copy_to(step).wait_send()

    @pl.loop(1, parts)
    def _(step):
        copy_from(step).wait_recv()


def swap(blocks, axis, ident):
    parts = blocks.shape[0]
    lanes = 128
    shaped = blocks.reshape(parts, -1, lanes)
    out = pl.pallas_call(
        functools.partial(swap_kernel, axis),
        out_shape=jax.ShapeDtypeStruct(shaped.shape, shaped.dtype),
        in_specs=[pl.BlockSpec(memory_space=pltpu.VMEM)],
        out_specs=pl.BlockSpec(memory_space=pltpu.VMEM),
        scratch_shapes=[pltpu.SemaphoreType.DMA((parts,)), pltpu.SemaphoreType.DMA((parts,))],
        compiler_params=pltpu.CompilerParams(collective_id=ident, has_side_effects=True),
    )(shaped)
    return out.reshape(blocks.shape)


def exchange(blocks, extra, axis, ident):
    width = blocks.shape[1]
    got = swap(jnp.concatenate([blocks, extra], 1), axis, ident)
    return got[:, :width], got[:, width:].sum(0)


def turn_kernel(anchor_ref, sent_ref, ready_ref, landed_ref, table_ref, send_sem, recv_sem):
    parts = sent_ref.shape[0]
    depth = sent_ref.shape[1] - 1
    band = ready_ref.shape[1] - 1
    me = lax.axis_index("sy")
    mesh_ids = pl.DeviceIdType.MESH
    barrier = pltpu.get_barrier_semaphore()
    for step in range(1, parts):
        pl.semaphore_signal(
            barrier, 1, device_id={"sy": lax.rem(me + step, parts)}, device_id_type=mesh_ids
        )
    table_ref[...] = turn_table(
        parts * depth // 2, anchor_ref[0], depth // 2, ready_ref.shape[1] // 2, table_ref.shape
    )
    pl.semaphore_wait(barrier, parts - 1)

    def copy_y(step, outgoing):
        peer = lax.rem(me + (step if outgoing else parts - step), parts)
        return pltpu.make_async_remote_copy(
            src_ref=sent_ref.at[peer],
            dst_ref=landed_ref.at[me if outgoing else peer],
            send_sem=send_sem.at[step],
            recv_sem=recv_sem.at[step],
            device_id={"sy": peer},
            device_id_type=mesh_ids,
        )

    @pl.loop(1, parts)
    def _(step):
        copy_y(step, True).start()

    landed_ref[me] = sent_ref[me]

    @pl.loop(1, parts)
    def _(step):
        copy_y(step, True).wait_send()

    @pl.loop(1, parts)
    def _(step):
        copy_y(step, False).wait_recv()

    lanes = ready_ref.shape[2]
    halves = landed_ref.shape[2] // lanes
    rows = band // halves
    block = landed_ref[:, 0:depth, :].reshape(parts * depth, -1)
    share = landed_ref[0, depth : depth + 1, 0:lanes]
    for source in range(1, parts):
        share = share + landed_ref[source, depth : depth + 1, 0:lanes]
    for half in range(halves):
        turned = jnp.dot(
            table_ref[...], block[:, half * lanes : (half + 1) * lanes], precision=HIGH,
            preferred_element_type=jnp.float32,
        )
        for peer in range(ready_ref.shape[0]):
            ready_ref[peer, half * rows : (half + 1) * rows, :] = turned[peer * rows : (peer + 1) * rows]
    for peer in range(ready_ref.shape[0]):
        ready_ref[peer, band : band + 1, :] = share


def turn(sent, anchor, parts_x, band):
    parts_y, rows, width = sent.shape
    vmem = pl.BlockSpec(memory_space=pltpu.VMEM)
    return pl.pallas_call(
        turn_kernel,
        out_shape=jax.ShapeDtypeStruct((parts_x, band * width // 128 + 1, 128), jnp.float32),
        in_specs=[pl.BlockSpec(memory_space=pltpu.SMEM), vmem],
        out_specs=vmem,
        scratch_shapes=[
            pltpu.VMEM((parts_y, rows, width), jnp.float32),
            pltpu.VMEM((parts_y * (rows - 1), parts_y * (rows - 1)), jnp.float32),
            pltpu.SemaphoreType.DMA((parts_y,)),
            pltpu.SemaphoreType.DMA((parts_y,)),
        ],
        compiler_params=pltpu.CompilerParams(collective_id=0, has_side_effects=True),
    )(anchor, sent)


def turn_table(length, anchor, rows_y, share_y, shape):
    line = lax.broadcasted_iota(jnp.int32, shape, 0)
    column = lax.broadcasted_iota(jnp.int32, shape, 1)
    wave = line // 2
    out_part = line % 2
    in_part = (column // rows_y) % 2
    site = (column // (2 * rows_y)) * rows_y + column % rows_y
    offset = (site - anchor + length) % length
    index = (offset * wave + (length // 4) * (out_part - in_part) + length) % length
    return jnp.cos((2.0 * math.pi / length) * index.astype(jnp.float32))


def spread_kernel(blocks_ref, out_ref, gathered_ref, total_ref, b_send, b_recv, c_send, c_recv):
    parts_x = blocks_ref.shape[0]
    parts_y = gathered_ref.shape[0]
    depth = blocks_ref.shape[1] - 1
    me_x = lax.axis_index("sx")
    me_y = lax.axis_index("sy")
    mesh_ids = pl.DeviceIdType.MESH
    barrier = pltpu.get_barrier_semaphore()
    for step in range(1, parts_x):
        pl.semaphore_signal(
            barrier, 1, device_id={"sx": lax.rem(me_x + step, parts_x)}, device_id_type=mesh_ids
        )
    for step in range(1, parts_y):
        pl.semaphore_signal(
            barrier, 1, device_id={"sy": lax.rem(me_y + step, parts_y)}, device_id_type=mesh_ids
        )
    pl.semaphore_wait(barrier, parts_x + parts_y - 2)

    def copy_x(step, outgoing):
        peer = lax.rem(me_x + (step if outgoing else parts_x - step), parts_x)
        return pltpu.make_async_remote_copy(
            src_ref=blocks_ref.at[peer],
            dst_ref=out_ref.at[me_x if outgoing else peer],
            send_sem=b_send.at[step],
            recv_sem=b_recv.at[step],
            device_id={"sx": peer},
            device_id_type=mesh_ids,
        )

    def copy_y(step, outgoing):
        peer = lax.rem(me_y + (step if outgoing else parts_y - step), parts_y)
        return pltpu.make_async_remote_copy(
            src_ref=total_ref.at[0],
            dst_ref=gathered_ref.at[me_y if outgoing else peer],
            send_sem=c_send.at[step],
            recv_sem=c_recv.at[step],
            device_id={"sy": peer},
            device_id_type=mesh_ids,
        )

    @pl.loop(1, parts_x)
    def _(step):
        copy_x(step, True).start()

    out_ref[me_x] = blocks_ref[me_x]

    @pl.loop(1, parts_x)
    def _(step):
        copy_x(step, True).wait_send()

    @pl.loop(1, parts_x)
    def _(step):
        copy_x(step, False).wait_recv()

    total = out_ref[0, depth : depth + 1, :]
    for source in range(1, parts_x):
        total = total + out_ref[source, depth : depth + 1, :]
    total_ref[...] = total

    @pl.loop(1, parts_y)
    def _(step):
        copy_y(step, True).start()

    gathered_ref[pl.ds(me_y, 1), :] = total

    @pl.loop(1, parts_y)
    def _(step):
        copy_y(step, True).wait_send()

    @pl.loop(1, parts_y)
    def _(step):
        copy_y(step, False).wait_recv()


def spread_ready(shaped):
    parts_x = shaped.shape[0]
    parts_y = lax.axis_size("sy")
    vmem = pl.BlockSpec(memory_space=pltpu.VMEM)
    got, gathered = pl.pallas_call(
        spread_kernel,
        out_shape=(
            jax.ShapeDtypeStruct(shaped.shape, shaped.dtype),
            jax.ShapeDtypeStruct((parts_y, shaped.shape[2]), shaped.dtype),
        ),
        in_specs=[vmem],
        out_specs=(vmem, vmem),
        scratch_shapes=[
            pltpu.VMEM((1, shaped.shape[2]), jnp.float32),
            pltpu.SemaphoreType.DMA((parts_x,)),
            pltpu.SemaphoreType.DMA((parts_x,)),
            pltpu.SemaphoreType.DMA((parts_y,)),
            pltpu.SemaphoreType.DMA((parts_y,)),
        ],
        compiler_params=pltpu.CompilerParams(collective_id=1, has_side_effects=True),
    )(shaped)
    return got[:, :-1], gathered


def spread(blocks, share, parts_y):
    parts_x = blocks.shape[0]
    lanes = 128
    width = share.size
    rows = jnp.pad(share, (0, lanes - width)) if width < lanes else share
    shaped = blocks.reshape(parts_x, -1, rows.size)
    shaped = jnp.concatenate(
        [shaped, jnp.broadcast_to(rows.reshape(1, 1, -1), (parts_x, 1, rows.size))], 1
    )
    vmem = pl.BlockSpec(memory_space=pltpu.VMEM)
    got, gathered = pl.pallas_call(
        spread_kernel,
        out_shape=(
            jax.ShapeDtypeStruct(shaped.shape, shaped.dtype),
            jax.ShapeDtypeStruct((parts_y, 1, rows.size), shaped.dtype),
        ),
        in_specs=[vmem],
        out_specs=(vmem, vmem),
        scratch_shapes=[
            pltpu.VMEM((1, rows.size), jnp.float32),
            pltpu.SemaphoreType.DMA((parts_x,)),
            pltpu.SemaphoreType.DMA((parts_x,)),
            pltpu.SemaphoreType.DMA((parts_y,)),
            pltpu.SemaphoreType.DMA((parts_y,)),
        ],
        compiler_params=pltpu.CompilerParams(collective_id=1, has_side_effects=True),
    )(shaped)
    return got[:, :-1].reshape(blocks.shape), gathered[:, 0, :width]


def apply_gammas(mat_re, mat_im, real_part, imag_part):
    extent = real_part.shape
    flat_re = real_part.reshape(extent[0], -1)
    flat_im = imag_part.reshape(extent[0], -1)
    out_re = jnp.dot(mat_re, flat_re, precision=HIGHEST) - jnp.dot(
        mat_im, flat_im, precision=HIGHEST
    )
    out_im = jnp.dot(mat_re, flat_im, precision=HIGHEST) + jnp.dot(
        mat_im, flat_re, precision=HIGHEST
    )
    return (out_re.reshape(extent), out_im.reshape(extent))


def project_sites(fields, source_site, momenta, rows_x, rows_y, length, depth):
    coord_x = lax.axis_index("sx") * rows_x + jnp.arange(rows_x, dtype=jnp.int32) - source_site[0]
    coord_y = lax.axis_index("sy") * rows_y + jnp.arange(rows_y, dtype=jnp.int32) - source_site[1]
    coord_z = jnp.arange(depth, dtype=jnp.int32) - source_site[2]
    part_x = jnp.mod(momenta[:, 0:1] * coord_x[None, :], length)
    part_y = jnp.mod(momenta[:, 1:2] * coord_y[None, :], length)
    part_z = jnp.mod(momenta[:, 2:3] * coord_z[None, :], depth)
    plane = jnp.mod(part_x[:, :, None] + part_y[:, None, :], length).astype(jnp.float32)
    angles = (
        2.0 * math.pi / length * plane[:, :, :, None]
        + 2.0 * math.pi / depth * part_z.astype(jnp.float32)[:, None, None, :]
    )
    angles = angles.reshape(momenta.shape[0], -1)
    cosine = jnp.cos(angles)
    sine = jnp.sin(angles)
    field_re = fields[:, 0].reshape(fields.shape[0], -1)
    field_im = fields[:, 1].reshape(fields.shape[0], -1)
    local_re = jnp.dot(field_re, cosine.T, precision=HIGH) + jnp.dot(
        field_im, sine.T, precision=HIGH
    )
    local_im = jnp.dot(field_im, cosine.T, precision=HIGH) - jnp.dot(
        field_re, sine.T, precision=HIGH
    )
    return (local_re, local_im)


def gamma_mix(table_ref, inserts):
    shape = (inserts * 2, 32)
    line = lax.broadcasted_iota(jnp.int32, shape, 0)
    column = lax.broadcasted_iota(jnp.int32, shape, 1)
    out_part = line % 2
    in_part = column % 2
    same = out_part == in_part
    sign = 2 * out_part - 1
    mix = jnp.zeros(shape, jnp.int32)
    for g in range(inserts):
        for s in range(4):
            target = table_ref[g * 8 + s * 2]
            power = table_ref[g * 8 + s * 2 + 1]
            unit_re = jnp.where(power == 0, 1, 0) - jnp.where(power == 2, 1, 0)
            unit_im = jnp.where(power == 1, 1, 0) - jnp.where(power == 3, 1, 0)
            hit = (line // 2 == g) & (column // 2 == s * 4 + target)
            mix = jnp.where(hit, jnp.where(same, unit_re, sign * unit_im), mix)
    return mix.astype(jnp.float32)


def contract_kernel(gamma_ref, forward_ref, backward_ref, out_ref, pair_ref):
    slices = forward_ref.shape[0]
    rows = forward_ref.shape[3]
    mix = gamma_mix(gamma_ref, out_ref.shape[2] // 2)
    for t in range(slices):
        for u in range(4):
            f_re = [forward_ref[t, 0, 3 * u + c].astype(jnp.float32) for c in range(3)]
            f_im = [forward_ref[t, 1, 3 * u + c].astype(jnp.float32) for c in range(3)]
            for s in range(4):
                acc_re = None
                acc_im = None
                for c in range(3):
                    b_re = backward_ref[t, 0, 3 * s + c].astype(jnp.float32)
                    b_im = backward_ref[t, 1, 3 * s + c].astype(jnp.float32)
                    term_re = b_re * f_re[c] + b_im * f_im[c]
                    term_im = b_re * f_im[c] - b_im * f_re[c]
                    acc_re = term_re if acc_re is None else acc_re + term_re
                    acc_im = term_im if acc_im is None else acc_im + term_im
                base = (s * 4 + u) * 2 * rows
                pair_ref[base : base + rows, :] = acc_re
                pair_ref[base + rows : base + 2 * rows, :] = acc_im
        width = pair_ref.shape[0]
        kinds = mix.shape[1]
        lines = out_ref.shape[1] * kinds
        row = lax.broadcasted_iota(jnp.int32, (lines, width), 0)
        col = lax.broadcasted_iota(jnp.int32, (lines, width), 1)
        pick = jnp.logical_and(row % kinds == col // rows, row // kinds == col % out_ref.shape[1])
        summed = jnp.dot(
            pick.astype(jnp.float32), pair_ref[...], precision=HIGH,
            preferred_element_type=jnp.float32,
        )
        for x in range(out_ref.shape[1]):
            out_ref[t, x] = jnp.dot(
                mix, summed[x * kinds : (x + 1) * kinds], precision=HIGH,
                preferred_element_type=jnp.float32,
            )


def contract(forward_prop, backward_prop, gamma_table):
    slices = forward_prop.shape[0]
    rows_x = forward_prop.shape[4]
    sites = forward_prop.shape[5]
    inserts = gamma_table.shape[0]
    forward = forward_prop.reshape(slices, 2, 12, 12 * rows_x, sites)
    backward = backward_prop.reshape(slices, 2, 12, 12 * rows_x, sites)
    out = pl.pallas_call(
        contract_kernel,
        out_shape=jax.ShapeDtypeStruct((slices, rows_x, inserts * 2, sites), jnp.float32),
        in_specs=[pl.BlockSpec(memory_space=pltpu.SMEM)]
        + [pl.BlockSpec(memory_space=pltpu.VMEM)] * 2,
        out_specs=pl.BlockSpec(memory_space=pltpu.VMEM),
        scratch_shapes=[pltpu.VMEM((16 * 2 * 12 * rows_x, sites), jnp.float32)],
    )(gamma_table.reshape(-1), forward, backward)
    return out.reshape(slices, rows_x, inserts, 2, sites).transpose(2, 0, 3, 1, 4)


def body(forward_prop, backward_prop, gamma_table, source_site, momenta):
    slices = forward_prop.shape[0]
    rows_x = forward_prop.shape[4]
    rows_y = backward_prop.shape[5] // LZ
    inserts = gamma_table.shape[0]
    fields = contract(forward_prop, backward_prop, gamma_table)
    fields = fields.reshape(inserts * slices, 2, rows_x, rows_y, LZ)
    count = fields.shape[0]
    local_re, local_im = project_sites(fields, source_site, momenta, rows_x, rows_y, L, LZ)
    partial = jnp.stack([local_re, local_im], 0)
    groups_y = lax.axis_size("sy")
    groups_x = lax.axis_size("sx")
    tables = dft_matrices(LZ, source_site)
    share_z = LZ // groups_y
    table_z = tables[2].reshape(2, LZ, 2, groups_y, share_z)
    blocks = jnp.einsum("nrxyz,rzsjc->jsynxc", fields, table_z, precision=HIGH)
    blocks = blocks.reshape(groups_y, 2 * rows_y, -1)
    width = blocks.shape[2]
    shares = partial.reshape(groups_y, 1, -1)
    shares = jnp.pad(shares, ((0, 0), (0, 0), (0, width - shares.shape[2])))
    share_y = rows_y * groups_y // groups_x
    ready = turn(jnp.concatenate([blocks, shares], 1), source_site[1:2], groups_x, 2 * share_y)
    blocks, gathered = spread_ready(ready)
    blocks = blocks.reshape(groups_x, width // 128, share_y, 2, 128).transpose(0, 2, 3, 1, 4)
    blocks = blocks.reshape(groups_x, share_y, 2, count, rows_x, share_z)
    gathered = gathered[:, : partial.size // groups_y]
    table_x = tables[0].reshape(2, groups_x, rows_x, 2, -1)
    spectrum = jnp.einsum("ibsnxc,sixtk->ntbck", blocks, table_x, precision=HIGH)
    corr = spectrum.reshape(inserts, slices, 2, share_y, -1)
    listed = gathered.reshape(2, inserts, slices, -1)
    return (corr, listed)


def solution(mesh):
    placed = (
        P(None, None, None, None, "sx", "sy"),
        P(None, None, None, None, "sx", "sy"),
        P(),
        P(),
        P(),
    )
    return jax.shard_map(
        body,
        mesh=mesh,
        in_specs=placed,
        out_specs=(P(None, None, None, "sx", "sy"), P()),
        check_vma=False,
    )
```
